32 devices in a mesh: groups: 2 (over x), pop: 8 (over z, y), tensor: 2 (over core).
Axes of the slice: x: 2, y: 2, z: 4, core: 2. Of those that a mesh axis runs over, the one named last changes fastest.
Arguments:
- prompts: bfloat16 [48, 8192], P('groups'), parts along dimension 0, may hold values from -6 to 6
- gate_weight: bfloat16 [8192, 14848], P('pop', 'tensor'), may hold values from -0.0625 to 0.0625
- up_weight: bfloat16 [8192, 14848], P('pop', 'tensor'), may hold values from -0.0625 to 0.0625
- down_weight_matrix: bfloat16 [14848, 8192], P('tensor', 'pop'), may hold values from -0.046875 to 0.046875
- gate_in: bfloat16 [16, 8192, 4], P(('groups', 'pop')), parts along dimension 0, may hold values from -6 to 6
- gate_output_factors: bfloat16 [16, 14848, 4], P(('groups', 'pop'), 'tensor'), parts along dimension 0, may hold values from -6 to 6
- up_in: bfloat16 [16, 8192, 4], P(('groups', 'pop')), parts along dimension 0, may hold values from -6 to 6
- up_output_factors: bfloat16 [16, 14848, 4], P(('groups', 'pop'), 'tensor'), parts along dimension 0, may hold values from -6 to 6
- down_input_factors: bfloat16 [16, 14848, 4], P('groups', 'tensor'), parts along dimension 0, may hold values from -6 to 6
- down_out: bfloat16 [16, 8192, 4], P('groups', 'pop'), parts along dimension 0, may hold values from -6 to 6
- label_head: bfloat16 [8192, 128], P('tensor'), may hold values from -0.1875 to 0.1875
- targets: int32 [48], P('groups'), parts along dimension 0, may hold values from 0 to 127
Outputs:
- update: bfloat16 [29696, 8192], P(('groups', 'tensor'), 'pop'), parts along dimension 0
- scores: float32 [16], P(('groups', 'pop')), parts along dimension 0
The draws below stay inside these ranges and needn't reach their ends.
There are 2 independent parts, one for each index of `groups`. The reference program is written for one: setup_inputs(seed, part) draws one part's arguments, and reference() takes and returns one part's arrays. A program takes and returns all parts, laid end to end along the dimension named above; an argument that names none is the same for every part. Nothing has to cross between parts.
All inputs are finite; a program needn't handle non-finite values.
Results may differ from the reference program's by a relative error of at most 0.023.
Values may be sent and summed in bfloat16 or wider, within the bound.
A program may use at most 256 MiB of HBM per device.

```python
import math
import jax
import jax.numpy as jnp
from jax import lax

D = 8192
HIDDEN_UNITS_PART = 14848
RANK = 4
LABELS = 128
ROWS = 24
MEMBERS = 8


def with_ends(drawn, key, smallest, largest):
    place = [jax.random.randint(jax.random.fold_in(key, axis), (), 0, length) for axis, length in enumerate(drawn.shape)]
    widest = drawn.shape.index(max(drawn.shape))
    beside = place[:widest] + [(place[widest] + 1) % drawn.shape[widest]] + place[widest + 1:]
    return drawn.at[tuple(place)].set(smallest).at[tuple(beside)].set(largest)


def shard_levels(rng, dims, split, least, top_value):
    loudness, own = 1.0, jax.random.fold_in(rng, 6)
    for axis_at, parts in split:
        heights = jnp.exp(jax.random.uniform(jax.random.fold_in(own, axis_at), (parts,), jnp.float32, least / len(split), top_value / len(split)))
        loudness = loudness * jnp.repeat(heights, dims[axis_at] // parts).reshape([-1 if axis == axis_at else 1 for axis in range(len(dims))])
    return loudness


def bell_draw(stream_key, dims, scale, bound, pieces=(), held_as=jnp.bfloat16):
    entries = jax.random.normal(stream_key, dims, jnp.float32) * scale
    if len(pieces) > 0:
        entries = shard_levels(stream_key, dims, pieces, -0.22, 0.18) * entries
    return jnp.clip(entries, min=-bound, max=bound).astype(held_as)


def setup_inputs(seed: int = 0, part: int = 0) -> dict:
    keys = jax.random.split(jax.random.key(seed), 13)
    own_keys = jax.random.split(jax.random.fold_in(keys[12], part), 13)
    prompts = bell_draw(own_keys[0], (ROWS, D), 1.0, 6.0)
    gate_weight = bell_draw(keys[1], (D, HIDDEN_UNITS_PART), D ** -0.5, 0.0625, ((0, 8), (1, 2)))
    up_weight = bell_draw(keys[2], (D, HIDDEN_UNITS_PART), D ** -0.5, 0.0625, ((0, 8), (1, 2)))
    down_weight_matrix = bell_draw(keys[3], (HIDDEN_UNITS_PART, D), HIDDEN_UNITS_PART ** -0.5, 0.046875, ((0, 2), (1, 8)))
    gate_in = bell_draw(own_keys[4], (MEMBERS, D, RANK), 1.0, 6.0, ((0, 8),))
    gate_output_factors = bell_draw(own_keys[5], (MEMBERS, HIDDEN_UNITS_PART, RANK), 1.0, 6.0, ((0, 8), (1, 2)))
    up_in = bell_draw(own_keys[6], (MEMBERS, D, RANK), 1.0, 6.0, ((0, 8),))
    up_output_factors = bell_draw(own_keys[7], (MEMBERS, HIDDEN_UNITS_PART, RANK), 1.0, 6.0, ((0, 8), (1, 2)))
    down_input_factors = bell_draw(own_keys[8], (MEMBERS, HIDDEN_UNITS_PART, RANK), 1.0, 6.0, ((1, 2),))
    down_out = bell_draw(own_keys[9], (MEMBERS, D, RANK), 1.0, 6.0, ((1, 8),))
    label_head = bell_draw(keys[10], (D, LABELS), (D // 9) ** -0.5, 0.1875, ((0, 2),))
    targets = with_ends(jax.random.randint(own_keys[11], (ROWS,), 0, LABELS), jax.random.fold_in(own_keys[11], 1), 0, LABELS - 1).astype(jnp.int32)
    return dict(prompts=prompts, gate_weight=gate_weight, up_weight=up_weight, down_weight_matrix=down_weight_matrix, gate_in=gate_in, gate_output_factors=gate_output_factors, up_in=up_in, up_output_factors=up_output_factors, down_input_factors=down_input_factors, down_out=down_out, label_head=label_head, targets=targets)


def scaled_rows(values):
    return values * lax.rsqrt(lax.optimization_barrier(jnp.mean(values * values, axis=-1, keepdims=True)) + 1e-06)

def reference(prompts, gate_weight, up_weight, down_weight_matrix, gate_in, gate_output_factors, up_in, up_output_factors, down_input_factors, down_out, label_head, targets):
    highest_score = lax.Precision.HIGHEST
    prompt_f = prompts.astype(jnp.float32)
    normed = scaled_rows(prompt_f).astype(jnp.bfloat16)
    gate_baseline = jnp.dot(normed, gate_weight, preferred_element_type=jnp.float32).astype(jnp.bfloat16)
    up_baseline = jnp.dot(normed, up_weight, preferred_element_type=jnp.float32).astype(jnp.bfloat16)
    normed_f = normed.astype(jnp.float32)
    in_scale = 0.2 / math.sqrt(D)
    lowrank_gate = (in_scale * jnp.einsum('rd,mdk->mrk', normed_f, gate_in.astype(jnp.float32), precision=highest_score)).astype(jnp.bfloat16)
    lowrank_up = (in_scale * jnp.einsum('rd,mdk->mrk', normed_f, up_in.astype(jnp.float32), precision=highest_score)).astype(jnp.bfloat16)
    gate_activation = gate_baseline.astype(jnp.float32)[None] + jnp.einsum('hvw,hpw->hvp', lowrank_gate.astype(jnp.float32), gate_output_factors.astype(jnp.float32), precision=highest_score)
    upper_bound = up_baseline.astype(jnp.float32)[None] + jnp.einsum('hvw,hpw->hvp', lowrank_up.astype(jnp.float32), up_output_factors.astype(jnp.float32), precision=highest_score)
    hidden_state = (jax.nn.silu(gate_activation) * upper_bound).astype(jnp.bfloat16)
    lowrank_down = 0.2 / math.sqrt(HIDDEN_UNITS_PART) * jnp.einsum('lpq,lqb->lpb', hidden_state.astype(jnp.float32), down_input_factors.astype(jnp.float32), precision=highest_score)
    members = hidden_state.shape[0]
    entry_point = jnp.dot(hidden_state.reshape(members * ROWS, HIDDEN_UNITS_PART), down_weight_matrix, preferred_element_type=jnp.float32).reshape(members, ROWS, D)
    output = prompt_f[None] + entry_point + jnp.einsum('mrk,mdk->mrd', lowrank_down, down_out.astype(jnp.float32), precision=highest_score)
    final = scaled_rows(output).astype(jnp.bfloat16)
    logits = jnp.dot(final.reshape(members * ROWS, D), label_head, preferred_element_type=jnp.float32).reshape(members, ROWS, LABELS)
    picks = targets[:, None] == jnp.arange(LABELS, dtype=jnp.int32)[None, :]
    picked = lax.optimization_barrier(jnp.sum(jnp.where(picks[None], logits, 0.0), axis=-1))
    reward = lax.optimization_barrier(jnp.mean(picked - jnp.log(lax.optimization_barrier(jnp.sum(jnp.exp(logits), axis=-1))), axis=-1))
    centre = jnp.mean(reward)
    spread = jnp.mean((reward - centre) * (reward - centre))
    scores = (reward - centre) * lax.rsqrt(spread + 1e-06)
    weighted = (scores[:, None, None] * down_out.astype(jnp.float32)).astype(jnp.bfloat16)
    left = jnp.transpose(down_input_factors, (1, 0, 2)).reshape(HIDDEN_UNITS_PART, members * RANK)
    right = jnp.transpose(weighted, (1, 0, 2)).reshape(D, members * RANK)
    update = jnp.dot(left, right.T, preferred_element_type=jnp.float32) * (1.0 / math.sqrt(members * RANK))
    return (update.astype(jnp.bfloat16), scores)
```

```python
import functools
import math

import jax
import jax.numpy as jnp
from jax import lax
from jax.experimental import pallas as pl
from jax.experimental.pallas import tpu as pltpu
from jax.sharding import PartitionSpec as P

noise_scale = 0.2
norm_eps = 1e-06


def scaled_rows(values):
    return values * lax.rsqrt(jnp.mean(values * values, axis=-1, keepdims=True) + norm_eps)


def build_hidden(
    gate_baseline, up_baseline, lowrank_gate, lowrank_up, gate_output_factors, up_output_factors
):
    gate_activation = gate_baseline.astype(jnp.float32)[None] + jnp.einsum(
        "hvw,hpw->hvp", lowrank_gate, gate_output_factors, preferred_element_type=jnp.float32
    )
    upper_bound = up_baseline.astype(jnp.float32)[None] + jnp.einsum(
        "hvw,hpw->hvp", lowrank_up, up_output_factors, preferred_element_type=jnp.float32
    )
    return (jax.nn.silu(gate_activation) * upper_bound).astype(jnp.bfloat16)


def label_terms(logits, targets):
    labels = logits.shape[1]
    picks = targets[:, None] == jnp.arange(labels, dtype=jnp.int32)[None, :]
    picked = jnp.sum(jnp.where(picks, logits, 0.0), axis=1)
    return picked - jnp.log(jnp.sum(jnp.exp(logits), axis=1))


def body(
    prompts,
    gate_weight,
    up_weight,
    down_weight_matrix,
    gate_in,
    gate_output_factors,
    up_in,
    up_output_factors,
    down_input_factors,
    down_out,
    label_head,
    targets,
):
    member = lax.axis_index("pop")
    width = prompts.shape[1]
    in_block = gate_weight.shape[0]
    ffn_half = gate_output_factors.shape[1]
    total_ff = ffn_half * lax.axis_size("tensor")
    members = down_input_factors.shape[0]
    rank = down_input_factors.shape[2]
    prompt_f = prompts.astype(jnp.float32)
    normed = scaled_rows(prompt_f).astype(jnp.bfloat16)
    own_cols = lax.dynamic_slice_in_dim(normed, member * in_block, in_block, 1)
    part_gate = jnp.dot(own_cols, gate_weight, preferred_element_type=jnp.float32)
    part_up = jnp.dot(own_cols, up_weight, preferred_element_type=jnp.float32)
    total_gate, total_up = lax.psum((part_gate, part_up), "pop")
    gate_baseline = total_gate.astype(jnp.bfloat16)
    up_baseline = total_up.astype(jnp.bfloat16)
    in_scale = noise_scale / math.sqrt(width)
    lowrank_gate = (
        in_scale * jnp.einsum("rd,mdk->mrk", normed, gate_in, preferred_element_type=jnp.float32)
    ).astype(jnp.bfloat16)
    lowrank_up = (
        in_scale * jnp.einsum("rd,mdk->mrk", normed, up_in, preferred_element_type=jnp.float32)
    ).astype(jnp.bfloat16)
    down_scale = noise_scale / math.sqrt(total_ff)
    hidden_state = build_hidden(
        gate_baseline, up_baseline, lowrank_gate, lowrank_up, gate_output_factors, up_output_factors
    )
    hidden_portion = lax.all_gather(hidden_state, "pop", axis=0, tiled=True)
    out_piece = down_out.astype(jnp.float32)
    entry_point = jnp.einsum(
        "uaz,zh->uah", hidden_portion, down_weight_matrix, preferred_element_type=jnp.float32
    )
    low_part = down_scale * jnp.einsum(
        "lpq,lqb->lpb", hidden_portion, down_input_factors, preferred_element_type=jnp.float32
    )
    partial_rows = entry_point + jnp.einsum(
        "mrk,mdk->mrd", low_part, out_piece, precision=lax.Precision.HIGHEST
    )
    rows_here = lax.all_to_all(partial_rows, "pop", split_axis=0, concat_axis=2, tiled=True)
    summed = lax.psum(rows_here, "tensor")[0]
    output = prompt_f + summed
    final = scaled_rows(output).astype(jnp.bfloat16)
    half = label_head.shape[0]
    own_half = lax.dynamic_slice_in_dim(final, lax.axis_index("tensor") * half, half, 1)
    logits = lax.psum(jnp.dot(own_half, label_head, preferred_element_type=jnp.float32), "tensor")
    reward = jnp.mean(label_terms(logits, targets))
    rewards = lax.all_gather(reward.reshape(1), "pop", axis=0, tiled=True)
    centre = jnp.mean(rewards)
    spread = jnp.mean((rewards - centre) * (rewards - centre))
    scores = (rewards - centre) * lax.rsqrt(spread + norm_eps)
    weighted = (scores[:, None, None] * down_out.astype(jnp.float32)).astype(jnp.bfloat16)
    update = jnp.einsum(
        "mfk,mdk->fd", down_input_factors, weighted, preferred_element_type=jnp.float32
    ) * (1.0 / math.sqrt(members * rank))
    own_score = lax.dynamic_slice_in_dim(scores, member, 1, 0)
    return (update.astype(jnp.bfloat16), own_score)


BF = jnp.bfloat16
F32 = jnp.float32
HI = lax.Precision.HIGHEST
NT = (((1,), (1,)), ((), ()))
TN = (((0,), (0,)), ((), ()))


def pair_kernel(
    pop, total_ff,
    prompts, gate_w, up_w, down_w, gate_in, gof, up_in, uof, dif, dout, head, targets,
    weighted_out, score_out,
    wg, wu, dw, normed, fbuild, fac, low, part, ysum, ysend, yrecv, zsend, zrecv, base,
    lhs, hid, acc, lowd, xsend, xrecv, hloc, hrem, hsel,
    lsend, lrecv, csend, crecv, rbuf,
    wsem, dsem, hsem, ssem, rsem,
):
    rows, width = prompts.shape
    block, ff = gate_w.shape
    outer = pop // 2
    chunk = wg.shape[2]
    members = pop
    rank = gof.shape[0]
    half = block // 2
    labels = head.shape[1]
    over = pop * chunk - ff
    me = lax.axis_index("pop")
    core = lax.axis_index("tensor")
    z = me // 2
    y = me % 2
    sib = {"tensor": 1 - core}

    def spot(zz, yy):
        return zz * 2 + yy

    def start_of(c):
        return pl.multiple_of(c * chunk - (c // (pop - 1)) * over, 128)

    def remote(src, dst, idx, dev):
        return pltpu.make_async_remote_copy(
            src_ref=src, dst_ref=dst, send_sem=ssem.at[idx], recv_sem=rsem.at[idx],
            device_id=dev, device_id_type=pl.DeviceIdType.MESH,
        )

    owners = [spot((z + 1 + i % outer) % outer, (1 - y) if i < outer else y) for i in range(pop)]
    loads = []
    for i in range(pop):
        cols = pl.ds(start_of(owners[i]), chunk)
        a = pltpu.make_async_copy(gate_w.at[:, cols], wg.at[i], wsem.at[2 * i])
        b = pltpu.make_async_copy(up_w.at[:, cols], wu.at[i], wsem.at[2 * i + 1])
        a.start()
        b.start()
        loads.append((a, b))
    hoff = (me % (pop // 2)) * block
    hcopy = pltpu.make_async_copy(head.at[pl.ds(pl.multiple_of(hoff + core * half, half), half)], hloc, hsem.at[0])
    hcopy.start()

    barrier = pltpu.get_barrier_semaphore()
    for k in range(1, pop):
        pl.semaphore_signal(barrier, inc=1, device_id={"pop": (me + k) % pop}, device_id_type=pl.DeviceIdType.MESH)
    pl.semaphore_signal(barrier, inc=1, device_id=sib, device_id_type=pl.DeviceIdType.MESH)

    fbuild[0:rank, :] = gof[...].astype(F32)
    fbuild[rank : 2 * rank, :] = uof[...].astype(F32)
    fac[me] = fbuild[...].astype(BF)
    pl.semaphore_wait(barrier, pop)

    pending = []
    FAC, LOWI, YI, ZI, AGI, XI, HEADI, LI, CI, RI = 0, 8, 16, 20, 24, 32, 33, 34, 42, 43
    fcopies = {}
    for k in range(1, outer):
        d = remote(fac.at[me], fac.at[me], FAC + k, {"pop": spot((z + k) % outer, y)})
        d.start()
        fcopies[k] = d
        pending.append(d)
    hs = remote(
        head.at[pl.ds(pl.multiple_of(hoff + (1 - core) * half, half), half)], hrem, HEADI, sib
    )
    hs.start()
    pending.append(hs)

    x = prompts[...].astype(F32)
    normed[...] = (x * lax.rsqrt(jnp.mean(x * x, axis=-1, keepdims=True) + norm_eps)).astype(BF)

    scale = noise_scale / math.sqrt(width)
    lg = (scale * lax.dot_general(normed[...], gate_in[...], NT, preferred_element_type=F32)).astype(BF)
    lu = (scale * lax.dot_general(normed[...], up_in[...], NT, preferred_element_type=F32)).astype(BF)
    krow = lax.broadcasted_iota(jnp.int32, (rank, 128), 0)
    lane = lax.broadcasted_iota(jnp.int32, (rank, 128), 1)
    sel_g = (lane == me * 2 * rank + krow).astype(F32).astype(BF)
    sel_u = (lane == me * 2 * rank + rank + krow).astype(F32).astype(BF)
    low[me] = (
        jnp.dot(lg, sel_g, preferred_element_type=F32) + jnp.dot(lu, sel_u, preferred_element_type=F32)
    ).astype(BF)
    lcopies = []
    for k in range(1, pop):
        d = remote(low.at[me], low.at[me], LOWI + k, {"pop": (me + k) % pop})
        d.start()
        lcopies.append(d)
        pending.append(d)

    ycopies = []
    zcopies = []
    dloads = []
    xcols = pl.ds(pl.multiple_of(me * block, block), block)
    tile = 256
    for i in range(pop):
        loads[i][0].wait()
        loads[i][1].wait()
        j = i % outer
        if i >= outer:
            ycopies[j].wait_recv()

        for g, w in enumerate((wg, wu)):
            got = jnp.dot(normed[:, xcols], w[i], preferred_element_type=F32)
            if i < outer:
                ysend[j, g] = got.astype(BF)
            elif i < pop - 1:
                zsend[j, g] = (got + yrecv[j, g].astype(F32)).astype(BF)
            else:
                ysum[g] = got + yrecv[j, g].astype(F32)

        if i < outer:
            d = remote(ysend.at[j], yrecv.at[j], YI + j, {"pop": spot(z, 1 - y)})
            d.start()
            ycopies.append(d)
            pending.append(d)
        elif i < pop - 1:
            d = remote(zsend.at[j], zrecv.at[j], ZI + j, {"pop": spot((z + 1 + j) % outer, y)})
            d.start()
            zcopies.append(d)
            pending.append(d)
        if i == outer - 1:
            d = remote(fac.at[me], fac.at[me], FAC + outer, {"pop": spot(z, 1 - y)})
            d.start()
            fcopies[outer] = d
            pending.append(d)
        if i >= outer:
            step = ff // 4
            n = i - outer
            d = pltpu.make_async_copy(
                down_w.at[pl.ds(n * step, step)], dw.at[pl.ds(n * step, step)], dsem.at[n]
            )
            d.start()
            dloads.append(d)

    for k in range(1, outer):
        fcopies[k].wait_recv()
        src = spot((z + outer - k) % outer, y)
        d = remote(fac.at[src], fac.at[src], FAC + outer + k, {"pop": spot(z, 1 - y)})
        d.start()
        fcopies[outer + k] = d
        pending.append(d)

    acc[...] = jnp.zeros_like(acc)
    lowd[...] = jnp.zeros_like(lowd)
    for d in lcopies:
        d.wait_recv()
    coef = jnp.concatenate([low[m].astype(F32) for m in range(members)], axis=0)
    lane = lax.broadcasted_iota(jnp.int32, coef.shape, 1)
    row = lax.broadcasted_iota(jnp.int32, coef.shape, 0) % rows
    kk = 2 * rank * members
    gate_lane = lane % (2 * rank) < rank
    gate_lhs = jnp.where(lane < kk, jnp.where(gate_lane, coef, 0.0), (lane == kk + row).astype(F32))
    up_lhs = jnp.where(lane < kk, jnp.where(gate_lane, 0.0, coef), (lane == kk + rows + row).astype(F32))
    lhs[...] = jnp.concatenate([0.5 * gate_lhs, up_lhs], axis=0).astype(BF)
    for d in dloads:
        d.wait()

    total = [ysum[0], ysum[1]]
    for j in range(outer - 1):
        zcopies[j].wait_recv()
        for g in range(2):
            total[g] = total[g] + zrecv[j, g].astype(F32)
    for g in range(2):
        base[0, g] = total[g].astype(BF)

    acopies = {}
    d = remote(base.at[0], base.at[outer], AGI + outer, {"pop": spot(z, 1 - y)})
    d.start()
    acopies[outer] = d
    pending.append(d)
    for k in (2, 1, 3):
        d = remote(base.at[0], base.at[k], AGI + k, {"pop": spot((z + k) % outer, y)})
        d.start()
        acopies[k] = d
        pending.append(d)

    for k in range(outer, pop):
        fcopies[k].wait_recv()
    big = members * rows

    def expand(slot, c):
        start = start_of(c)
        skip = (c // (pop - 1)) * over

        pad = jnp.zeros((128 - kk - 2 * rows, tile), F32)
        for off in range(0, chunk, tile):
            at = pl.ds(pl.multiple_of(start + off, 128), tile)
            parts = [fac[m, :, at].astype(F32) for m in range(members)]
            parts += [base[slot, g, :, off : off + tile].astype(F32) for g in range(2)]
            keep = (off >= skip).astype(F32)
            rhs = (jnp.concatenate(parts + [pad], axis=0) * keep).astype(BF)
            both = jnp.dot(lhs[...], rhs, preferred_element_type=F32)
            gate, up = both[:big], both[big:]
            hid[:, off : off + tile] = ((gate + gate * jnp.tanh(gate)) * up).astype(BF)
        h = hid[...]
        at = pl.ds(start, chunk)
        right = jnp.concatenate([dif[m, :, at].astype(F32) for m in range(members)], axis=0).astype(BF)
        lowd[...] += lax.dot_general(h, right, NT, preferred_element_type=F32)
        for off in range(0, block, tile):
            acc[:, off : off + tile] += jnp.dot(h, dw[at, off : off + tile], preferred_element_type=F32)

    expand(0, me)
    acopies[outer].wait_recv()
    expand(outer, spot(z, 1 - y))
    for k in (1, 2, 3):
        acopies[k].wait_recv()
        d = remote(base.at[k], base.at[outer + k], AGI + outer + k, {"pop": spot(z, 1 - y)})
        d.start()
        acopies[outer + k] = d
        pending.append(d)
        expand(k, spot((z + outer - k) % outer, y))
    for k in (1, 2, 3):
        acopies[outer + k].wait_recv()
        expand(outer + k, spot((z + outer - k) % outer, 1 - y))

    mine = lax.broadcasted_iota(jnp.int32, lowd.shape, 0) // rows == lax.broadcasted_iota(jnp.int32, lowd.shape, 1) // rank
    lowm = jnp.where(mine, lowd[...] * (noise_scale / math.sqrt(total_ff)), 0.0)
    for m in range(members):
        fbuild[0:rank, 0:block] = dout[m].astype(F32)
        weighted_out[m * rank : (m + 1) * rank, :] = fbuild[0:rank, 0:block]
    acc[...] += jnp.dot(lowm, weighted_out[...], preferred_element_type=F32, precision=HI)

    theirs = pl.ds(pl.multiple_of((1 - core) * half, half), half)
    ours = pl.ds(pl.multiple_of(core * half, half), half)
    xsend[...] = acc[:, theirs]
    xc = remote(xsend, xrecv, XI, sib)
    xc.start()
    pending.append(xc)
    hcopy.wait()
    hs.wait_recv()

    @pl.when(core == me // (pop // 2))
    def _():
        hsel[...] = hloc[...]

    @pl.when(core != me // (pop // 2))
    def _():
        hsel[...] = hrem[...]

    pcols = prompts[:, pl.ds(pl.multiple_of(me * block + core * half, half), half)].astype(F32)
    xc.wait_recv()
    lsend[...] = jnp.zeros_like(lsend)
    ones = jnp.ones((8, half), F32)
    out = acc[:, ours] + xrecv[...] + jnp.concatenate([pcols] * members, axis=0)
    top = out.astype(BF)
    rest = (out - top.astype(F32)).astype(BF)
    logits = jnp.dot(top, hsel[...], preferred_element_type=F32) + jnp.dot(
        rest, hsel[...], preferred_element_type=F32
    )
    squares = out * out
    for m in range(members):
        r = slice(m * rows, (m + 1) * rows)
        lsend[m, 0:rows, :] = logits[r]
        lsend[m, rows : rows + 8, 0:rows] = lax.dot_general(
            ones, squares[r], NT, preferred_element_type=F32, precision=HI
        )
    bcopies = []
    for k in range(1, pop):
        to = (me + k) % pop
        d = remote(lsend.at[to], lrecv.at[k], LI + k, {"pop": to})
        d.start()
        bcopies.append(d)
        pending.append(d)
    tot = lsend[me]
    for k in range(1, pop):
        bcopies[k - 1].wait_recv()
        tot = tot + lrecv[k]
    csend[...] = tot
    cc = remote(csend, crecv, CI, sib)
    cc.start()
    pending.append(cc)
    cc.wait_recv()
    tot = csend[...] + crecv[...]
    eye = (
        lax.broadcasted_iota(jnp.int32, (rows, labels), 0) == lax.broadcasted_iota(jnp.int32, (rows, labels), 1)
    ).astype(F32)
    ssq = jnp.sum(eye * tot[rows : rows + 1, :], axis=1, keepdims=True)
    lgt = tot[0:rows, :] * lax.rsqrt(ssq * (1.0 / width) + norm_eps)
    spread_t = jnp.where(eye[:, :rows] > 0.0, jnp.broadcast_to(targets[...].astype(F32), (rows, rows)), 0.0)
    target = jnp.sum(spread_t, axis=1, keepdims=True).astype(jnp.int32)
    picks = target == lax.broadcasted_iota(jnp.int32, (rows, labels), 1)
    picked = jnp.sum(jnp.where(picks, lgt, 0.0), axis=1, keepdims=True)
    term = picked - jnp.log(jnp.sum(jnp.exp(lgt), axis=1, keepdims=True))
    reward = jnp.sum(jnp.broadcast_to(term, (rows, 128)), axis=0, keepdims=True) * (1.0 / rows)
    rbuf[me] = jnp.broadcast_to(reward, (8, 128))
    rcopies = []
    for k in range(1, pop):
        d = remote(rbuf.at[me], rbuf.at[me], RI + k, {"pop": (me + k) % pop})
        d.start()
        rcopies.append(d)
        pending.append(d)
    for d in rcopies:
        d.wait_recv()
    centre = sum(rbuf[m] for m in range(members)) * (1.0 / members)
    spread = sum((rbuf[m] - centre) * (rbuf[m] - centre) for m in range(members)) * (1.0 / members)
    inv = lax.rsqrt(spread + norm_eps)
    score_out[...] = (rbuf[me] - centre) * inv
    for m in range(members):
        sc = ((rbuf[m] - centre) * inv)[0:1, 0:1]
        r = slice(m * rank, (m + 1) * rank)
        weighted_out[r, :] = (dout[m].astype(F32) * sc).astype(BF).astype(F32)
    for d in pending:
        d.wait_send()


def update_kernel(norm, step, dif, weighted, score, out, score_out, left, right, sem):
    members, rank, ff = dif.shape
    right[...] = weighted[...].astype(BF)
    width = right.shape[1]
    copies = []
    for n, start in enumerate(range(0, ff, step)):
        at = pl.ds(start, min(step, ff - start))
        rows = jnp.concatenate([dif[m, :, at].astype(F32) for m in range(members)], axis=0).T.astype(BF)
        for c in range(0, width, 256):
            got = jnp.dot(rows, right[:, c : c + 256], preferred_element_type=F32)
            left[at, c : c + 256] = (got * norm).astype(BF)
        d = pltpu.make_async_copy(left.at[at], out.at[at], sem.at[n])
        d.start()
        copies.append(d)
    score_out[0] = score[0, 0]
    for d in copies:
        d.wait()


def fast_body(
    pop, prompts, gate_weight, up_weight, down_weight, gate_in, gof, up_in, uof, dif, dout, head, targets
):
    rows, width = prompts.shape
    block, ff = gate_weight.shape
    members, _, rank = dif.shape
    outer = pop // 2
    chunk = -(-(ff // 128) // pop) * 128
    labels = head.shape[1]
    swap = lambda v: jnp.swapaxes(v, 1, 2)
    dif_t, dout_t = swap(dif), swap(dout)
    vm = pl.BlockSpec(memory_space=pltpu.VMEM)
    hb = pl.BlockSpec(memory_space=pl.ANY)
    V = pltpu.VMEM
    big = members * rows
    weighted, score = pl.pallas_call(
        functools.partial(pair_kernel, pop, 2 * ff),
        out_shape=(
            jax.ShapeDtypeStruct((members * rank, block), F32),
            jax.ShapeDtypeStruct((8, 128), F32),
        ),
        in_specs=[vm, hb, hb, hb, vm, vm, vm, vm, vm, vm, hb, vm],
        out_specs=(vm, vm),
        scratch_shapes=[
            V((pop, block, chunk), BF), V((pop, block, chunk), BF), V((ff, block), BF),
            V((rows, width), BF), V((2 * rank, ff), F32), V((members, 2 * rank, ff), BF),
            V((members, rows, 128), BF), V((8, 128), F32), V((2, rows, chunk), F32),
            V((outer, 2, rows, chunk), BF), V((outer, 2, rows, chunk), BF),
            V((outer, 2, rows, chunk), BF), V((outer, 2, rows, chunk), BF),
            V((pop, 2, rows, chunk), BF),
            V((2 * big, 128), BF), V((big, chunk), BF), V((big, block), F32), V((big, members * rank), F32),
            V((big, block // 2), F32), V((big, block // 2), F32),
            V((block // 2, labels), BF), V((block // 2, labels), BF), V((block // 2, labels), BF),
            V((members, rows + 8, labels), F32), V((members, rows + 8, labels), F32),
            V((rows + 8, labels), F32), V((rows + 8, labels), F32), V((members, 8, 128), F32),
            pltpu.SemaphoreType.DMA((2 * pop,)), pltpu.SemaphoreType.DMA((4,)), pltpu.SemaphoreType.DMA((1,)),
            pltpu.SemaphoreType.DMA((52,)), pltpu.SemaphoreType.DMA((52,)),
        ],
        compiler_params=pltpu.CompilerParams(
            collective_id=0, has_side_effects=True, vmem_limit_bytes=66 * 1000 * 1000
        ),
        name="pair",
    )(
        prompts, gate_weight, up_weight, down_weight, swap(gate_in)[0], swap(gof)[0], swap(up_in)[0],
        swap(uof)[0], dif_t, dout_t, head, targets[None],
    )
    step = 512
    update, scores = pl.pallas_call(
        functools.partial(update_kernel, 1.0 / math.sqrt(members * rank), step),
        out_shape=(jax.ShapeDtypeStruct((ff, block), BF), jax.ShapeDtypeStruct((1,), F32)),
        in_specs=[vm, vm, vm],
        out_specs=(hb, pl.BlockSpec(memory_space=pltpu.SMEM)),
        scratch_shapes=[
            V((ff, block), BF), V((members * rank, block), BF), pltpu.SemaphoreType.DMA((-(-ff // step),)),
        ],
        compiler_params=pltpu.CompilerParams(vmem_limit_bytes=40 * 1000 * 1000),
        name="update",
    )(dif_t, weighted, score)
    return update, scores


def solution(mesh):
    placed = (
        P("groups", None),
        P("pop", "tensor"),
        P("pop", "tensor"),
        P("tensor", "pop"),
        P(("groups", "pop"), None, None),
        P(("groups", "pop"), "tensor", None),
        P(("groups", "pop"), None, None),
        P(("groups", "pop"), "tensor", None),
        P("groups", "tensor", None),
        P("groups", "pop", None),
        P("tensor", None),
        P("groups"),
    )
    pop = mesh.shape["pop"]
    run = functools.partial(fast_body, pop) if pop == 8 and mesh.shape["tensor"] == 2 else body
    return jax.shard_map(
        run,
        mesh=mesh,
        in_specs=placed,
        out_specs=(P(("groups", "tensor"), "pop"), P(("groups", "pop"))),
        check_vma=False,
    )
```

```python
import functools
import math

import jax
import jax.numpy as jnp
from jax import lax
from jax.experimental import pallas as pl
from jax.experimental.pallas import tpu as pltpu
from jax.sharding import PartitionSpec as P

noise_scale = 0.2
norm_eps = 1e-06


def scaled_rows(values):
    return values * lax.rsqrt(jnp.mean(values * values, axis=-1, keepdims=True) + norm_eps)


def build_hidden(
    gate_baseline, up_baseline, lowrank_gate, lowrank_up, gate_output_factors, up_output_factors
):
    gate_activation = gate_baseline.astype(jnp.float32)[None] + jnp.einsum(
        "hvw,hpw->hvp", lowrank_gate, gate_output_factors, preferred_element_type=jnp.float32
    )
    upper_bound = up_baseline.astype(jnp.float32)[None] + jnp.einsum(
        "hvw,hpw->hvp", lowrank_up, up_output_factors, preferred_element_type=jnp.float32
    )
    return (jax.nn.silu(gate_activation) * upper_bound).astype(jnp.bfloat16)


def label_terms(logits, targets):
    labels = logits.shape[1]
    picks = targets[:, None] == jnp.arange(labels, dtype=jnp.int32)[None, :]
    picked = jnp.sum(jnp.where(picks, logits, 0.0), axis=1)
    return picked - jnp.log(jnp.sum(jnp.exp(logits), axis=1))


def body(
    prompts,
    gate_weight,
    up_weight,
    down_weight_matrix,
    gate_in,
    gate_output_factors,
    up_in,
    up_output_factors,
    down_input_factors,
    down_out,
    label_head,
    targets,
):
    member = lax.axis_index("pop")
    width = prompts.shape[1]
    in_block = gate_weight.shape[0]
    ffn_half = gate_output_factors.shape[1]
    total_ff = ffn_half * lax.axis_size("tensor")
    members = down_input_factors.shape[0]
    rank = down_input_factors.shape[2]
    prompt_f = prompts.astype(jnp.float32)
    normed = scaled_rows(prompt_f).astype(jnp.bfloat16)
    own_cols = lax.dynamic_slice_in_dim(normed, member * in_block, in_block, 1)
    part_gate = jnp.dot(own_cols, gate_weight, preferred_element_type=jnp.float32)
    part_up = jnp.dot(own_cols, up_weight, preferred_element_type=jnp.float32)
    total_gate, total_up = lax.psum((part_gate, part_up), "pop")
    gate_baseline = total_gate.astype(jnp.bfloat16)
    up_baseline = total_up.astype(jnp.bfloat16)
    in_scale = noise_scale / math.sqrt(width)
    lowrank_gate = (
        in_scale * jnp.einsum("rd,mdk->mrk", normed, gate_in, preferred_element_type=jnp.float32)
    ).astype(jnp.bfloat16)
    lowrank_up = (
        in_scale * jnp.einsum("rd,mdk->mrk", normed, up_in, preferred_element_type=jnp.float32)
    ).astype(jnp.bfloat16)
    down_scale = noise_scale / math.sqrt(total_ff)
    hidden_state = build_hidden(
        gate_baseline, up_baseline, lowrank_gate, lowrank_up, gate_output_factors, up_output_factors
    )
    hidden_portion = lax.all_gather(hidden_state, "pop", axis=0, tiled=True)
    out_piece = down_out.astype(jnp.float32)
    entry_point = jnp.einsum(
        "uaz,zh->uah", hidden_portion, down_weight_matrix, preferred_element_type=jnp.float32
    )
    low_part = down_scale * jnp.einsum(
        "lpq,lqb->lpb", hidden_portion, down_input_factors, preferred_element_type=jnp.float32
    )
    partial_rows = entry_point + jnp.einsum(
        "mrk,mdk->mrd", low_part, out_piece, precision=lax.Precision.HIGHEST
    )
    rows_here = lax.all_to_all(partial_rows, "pop", split_axis=0, concat_axis=2, tiled=True)
    summed = lax.psum(rows_here, "tensor")[0]
    output = prompt_f + summed
    final = scaled_rows(output).astype(jnp.bfloat16)
    half = label_head.shape[0]
    own_half = lax.dynamic_slice_in_dim(final, lax.axis_index("tensor") * half, half, 1)
    logits = lax.psum(jnp.dot(own_half, label_head, preferred_element_type=jnp.float32), "tensor")
    reward = jnp.mean(label_terms(logits, targets))
    rewards = lax.all_gather(reward.reshape(1), "pop", axis=0, tiled=True)
    centre = jnp.mean(rewards)
    spread = jnp.mean((rewards - centre) * (rewards - centre))
    scores = (rewards - centre) * lax.rsqrt(spread + norm_eps)
    weighted = (scores[:, None, None] * down_out.astype(jnp.float32)).astype(jnp.bfloat16)
    update = jnp.einsum(
        "mfk,mdk->fd", down_input_factors, weighted, preferred_element_type=jnp.float32
    ) * (1.0 / math.sqrt(members * rank))
    own_score = lax.dynamic_slice_in_dim(scores, member, 1, 0)
    return (update.astype(jnp.bfloat16), own_score)


BF = jnp.bfloat16
F32 = jnp.float32
HI = lax.Precision.HIGHEST
NT = (((1,), (1,)), ((), ()))
TN = (((0,), (0,)), ((), ()))


def pair_kernel(
    pop, total_ff,
    prompts_in, gate_w, up_w, down_w, gate_in_h, gof_h, up_in_h, uof_h, dif_h, dout_h, head, targets_in,
    weighted_out, score_out,
    prompts, gate_in, gof, up_in, uof, dif, dout, targets,
    wg, wu, dw, normed, fbuild, fac, low, own, ysend, yrecv, zsend, zrecv, base,
    lhs, hid, acc, lowd, dcat, xsend, xrecv, hblock,
    lgsend, lgrecv, lsend, lrecv, rbuf,
    wsem, dsem, msem, ssem, rsem,
):
    rows, width = prompts.shape
    block, ff = gate_w.shape
    outer = pop // 2
    chunk = wg.shape[2]
    members = pop
    rank = gof.shape[0]
    part = members // 2
    big = members * rows
    labels = head.shape[1]
    over = pop * chunk - ff
    tile = 256
    me = lax.axis_index("pop")
    core = lax.axis_index("tensor")
    z = me // 2
    y = me % 2
    sib = {"tensor": 1 - core}
    middle = (z >= 1) & (z <= outer - 2)

    def spot(zz, yy):
        return zz * 2 + yy

    def start_of(c):
        return pl.multiple_of(c * chunk - (c // (pop - 1)) * over, 128)

    def remote(src, dst, sidx, ridx, dev):
        return pltpu.make_async_remote_copy(
            src_ref=src, dst_ref=dst, send_sem=ssem.at[sidx], recv_sem=rsem.at[ridx],
            device_id=dev, device_id_type=pl.DeviceIdType.MESH,
        )

    barrier = pltpu.get_barrier_semaphore()
    for k in range(1, pop):
        for t in range(2):
            pl.semaphore_signal(
                barrier, inc=1, device_id={"pop": (me + k) % pop, "tensor": t}, device_id_type=pl.DeviceIdType.MESH
            )
    pl.semaphore_signal(barrier, inc=1, device_id=sib, device_id_type=pl.DeviceIdType.MESH)

    def load(src, dst, sem):
        d = pltpu.make_async_copy(src, dst, sem)
        d.start()
        return d

    lgof = load(gof_h, gof, msem.at[0])
    luof = load(uof_h, uof, msem.at[1])
    lprompts = load(prompts_in, prompts, msem.at[2])
    lgin = load(gate_in_h, gate_in, msem.at[3])
    luin = load(up_in_h, up_in, msem.at[4])
    owners = [spot((z + 1 + i % outer) % outer, (1 - y) if i < outer else y) for i in range(pop)]

    def weights(i):
        cols = pl.ds(start_of(owners[i]), chunk)
        return (
            load(gate_w.at[:, cols], wg.at[i], wsem.at[2 * i]),
            load(up_w.at[:, cols], wu.at[i], wsem.at[2 * i + 1]),
        )

    loads = [weights(0)]
    for d in (lgof, luof, lprompts, lgin, luin):
        d.wait()
    loads += [weights(i) for i in range(1, pop)]
    ldif = load(dif_h, dif, msem.at[5])
    ldout = load(dout_h, dout, msem.at[6])
    ltar = load(targets_in, targets, msem.at[7])

    fbuild[0:rank, :] = gof[...].astype(F32)
    fbuild[rank : 2 * rank, :] = uof[...].astype(F32)
    fac[me] = fbuild[...].astype(BF)
    pl.semaphore_wait(barrier, 2 * pop - 1)

    pending = []
    (S_FY, S_P, S_M, S_F, S_LOW, S_Y, S_Z, S_A, S_X, S_LG, S_H, S_L, S_R) = (
        0, 1, 4, 7, 10, 18, 22, 25, 33, 34, 35, 36, 40)
    (R_FY, R_FZ, R_FH, R_LOW, R_Y, R_Z, R_A, R_X, R_LG, R_H, R_L, R_R) = (
        0, 1, 5, 9, 17, 21, 24, 32, 33, 34, 35, 43)

    def send(src, dst, sidx, ridx, dev):
        d = remote(src, dst, sidx, ridx, dev)
        d.start()
        pending.append(d)
        return d

    def chain(o, to, sidx):
        src = fac.at[spot(o, y)]
        return remote(src, src, sidx, R_FZ + o, {"pop": spot(to, y)})

    fy = send(fac.at[me], fac.at[me], S_FY, R_FY, {"pop": spot(z, 1 - y)})

    @pl.when(z < outer - 1)
    def _():
        chain(z, z + 1, S_P).start()

    @pl.when(z > 0)
    def _():
        chain(z, z - 1, S_M).start()

    hrows = head.at[pl.ds(pl.multiple_of((me % part) * block, block), block)]
    holds = core == me // part

    x = prompts[...].astype(F32)
    normed[...] = (x * lax.rsqrt(jnp.mean(x * x, axis=-1, keepdims=True) + norm_eps)).astype(BF)

    scale = noise_scale / math.sqrt(width)
    lg = (scale * lax.dot_general(normed[...], gate_in[...], NT, preferred_element_type=F32)).astype(BF)
    lu = (scale * lax.dot_general(normed[...], up_in[...], NT, preferred_element_type=F32)).astype(BF)
    krow = lax.broadcasted_iota(jnp.int32, (rank, 128), 0)
    lane = lax.broadcasted_iota(jnp.int32, (rank, 128), 1)
    sel_g = (lane == me * 2 * rank + krow).astype(F32).astype(BF)
    sel_u = (lane == me * 2 * rank + rank + krow).astype(F32).astype(BF)
    low[me] = (
        jnp.dot(lg, sel_g, preferred_element_type=F32) + jnp.dot(lu, sel_u, preferred_element_type=F32)
    ).astype(BF)
    lcopies = [
        send(low.at[me], low.at[me], S_LOW + k, R_LOW + k, {"pop": (me + k) % pop}) for k in range(1, pop)
    ]

    xcols = pl.ds(pl.multiple_of(me * block, block), block)
    mine_n = normed[:, xcols]

    def relay_first():
        @pl.when(middle)
        def _():
            chain(z - 1, z, S_P).wait_recv()
            chain(z - 1, z + 1, S_P + 1).start()
            chain(z + 1, z, S_M).wait_recv()
            chain(z + 1, z - 1, S_M + 1).start()

    far = 3 * (2 - z)
    end = 3 * (z - 1)

    def relay_second():
        @pl.when(middle)
        def _():
            chain(far, z, S_P).wait_recv()
            chain(far, end, S_P + 2).start()

    order = [
        jnp.where(z == 0, 1, z - 1),
        jnp.where(z == outer - 1, 1, jnp.where(z == 2, 3, 2)),
        jnp.where(z < 2, 3, 0),
    ]

    def forward(n):
        o = order[n]

        @pl.when(jnp.logical_not(middle))
        def _():
            chain(o, z, S_P).wait_recv()

        src = fac.at[spot(o, y)]
        send(src, src, S_F + n, R_FH + o, {"pop": spot(z, 1 - y)})

    ycopies = []
    zcopies = []
    dloads = []
    step = ff // 4
    for i in range(pop):
        loads[i][0].wait()
        loads[i][1].wait()
        j = i % outer
        for g, w in enumerate((wg, wu)):
            got = jnp.dot(mine_n, w[i], preferred_element_type=F32)
            if i < outer:
                ysend[j, g] = got.astype(BF)
            else:
                own[g] = got
        if i < outer:
            ycopies.append(send(ysend.at[j], yrecv.at[j], S_Y + j, R_Y + j, {"pop": spot(z, 1 - y)}))
        else:
            at = pl.ds(j * step, step)
            dloads.append(load(down_w.at[at], dw.at[at], dsem.at[j]))
            ycopies[j].wait_recv()
            for g in range(2):
                if i < pop - 1:
                    zsend[j, g] = (own[g] + yrecv[j, g].astype(F32)).astype(BF)
                else:
                    own[g] = own[g] + yrecv[j, g].astype(F32)
            if i < pop - 1:
                zcopies.append(
                    send(zsend.at[j], zrecv.at[j], S_Z + j, R_Z + j, {"pop": spot((z + 1 + j) % outer, y)})
                )
        if i == 2:
            relay_first()
        if i == outer + 2:
            relay_second()
            forward(0)
        if i == outer + 3:
            forward(1)

    @pl.when(holds)
    def _():
        remote(hrows, hblock, S_H, R_H, sib).start()
        pltpu.make_async_copy(hrows, hblock, msem.at[8]).start()

    ldout.wait()
    ldif.wait()
    ltar.wait()
    dall = jnp.concatenate([dout[m].astype(F32) for m in range(members)], axis=0)
    dcat[...] = jnp.concatenate([dall, dall], axis=0).astype(BF)
    acc[...] = jnp.zeros_like(acc)
    lowd[...] = jnp.zeros_like(lowd)
    for d in lcopies:
        d.wait_recv()
    coef = jnp.concatenate([low[m].astype(F32) for m in range(members)], axis=0)
    lane = lax.broadcasted_iota(jnp.int32, coef.shape, 1)
    row = lax.broadcasted_iota(jnp.int32, coef.shape, 0) % rows
    kk = 2 * rank * members
    gate_lane = lane % (2 * rank) < rank
    gate_lhs = jnp.where(lane < kk, jnp.where(gate_lane, coef, 0.0), (lane == kk + row).astype(F32))
    up_lhs = jnp.where(lane < kk, jnp.where(gate_lane, 0.0, coef), (lane == kk + rows + row).astype(F32))
    lhs[...] = jnp.concatenate([0.5 * gate_lhs, up_lhs], axis=0).astype(BF)

    total = [own[0], own[1]]
    for j in range(outer - 1):
        zcopies[j].wait_recv()
        for g in range(2):
            total[g] = total[g] + zrecv[j, g].astype(F32)
    for g in range(2):
        base[0, g] = total[g].astype(BF)

    acopies = {}
    gaps = [(o - z + outer) % outer for o in order]
    for n in range(outer - 1):
        send(base.at[0], base.at[gaps[n]], S_A + 1 + n, R_A + gaps[n], {"pop": spot(order[n], y)})
    forward(2)
    acopies[outer] = send(base.at[0], base.at[outer], S_A, R_A, {"pop": spot(z, 1 - y)})

    for d in dloads:
        d.wait()
    fy.wait_recv()
    for n in range(1, outer):
        o = (z + n) % outer
        src = fac.at[spot(o, 1 - y)]
        remote(src, src, S_F, R_FH + o, {"pop": spot(z, 1 - y)}).wait_recv()

    def expand(slot, c):
        start = start_of(c)
        skip = (c // (pop - 1)) * over

        pad = jnp.zeros((128 - kk - 2 * rows, tile), F32)
        for off in range(0, chunk, tile):
            at = pl.ds(pl.multiple_of(start + off, 128), tile)
            parts = [fac[m, :, at].astype(F32) for m in range(members)]
            parts += [base[slot, g, :, off : off + tile].astype(F32) for g in range(2)]
            keep = (off >= skip).astype(F32)
            rhs = (jnp.concatenate(parts + [pad], axis=0) * keep).astype(BF)
            both = jnp.dot(lhs[...], rhs, preferred_element_type=F32)
            gate, up = both[:big], both[big:]
            hid[:, off : off + tile] = ((gate + gate * jnp.tanh(gate)) * up).astype(BF)
        h = hid[...]
        at = pl.ds(start, chunk)
        right = jnp.concatenate([dif[m, :, at].astype(F32) for m in range(members)], axis=0).astype(BF)
        lowd[...] += lax.dot_general(h, right, NT, preferred_element_type=F32)
        for off in range(0, block, tile):
            acc[:, off : off + tile] += jnp.dot(h, dw[at, off : off + tile], preferred_element_type=F32)

    expand(0, me)
    for n in range(outer - 1):
        k = (outer - gaps[n]) % outer
        remote(base.at[k], base.at[k], S_A, R_A + k, sib).wait_recv()
        send(base.at[k], base.at[outer + k], S_A + 5 + n, R_A + outer + k, {"pop": spot(z, 1 - y)})
        expand(k, spot(order[n], y))
    acopies[outer].wait_recv()
    expand(outer, spot(z, 1 - y))
    for n in range(outer - 1):
        k = (outer - gaps[n]) % outer
        remote(base.at[outer + k], base.at[outer + k], S_A, R_A + outer + k, sib).wait_recv()
        expand(outer + k, spot(order[n], 1 - y))

    mine = lax.broadcasted_iota(jnp.int32, lowd.shape, 0) // rows == lax.broadcasted_iota(jnp.int32, lowd.shape, 1) // rank
    lowm = jnp.where(mine, lowd[...] * (noise_scale / math.sqrt(total_ff)), 0.0)
    top = lowm.astype(BF).astype(F32)
    pair = jnp.concatenate([top, lowm - top], axis=1).astype(BF)
    acc[...] += jnp.dot(pair, dcat[...], preferred_element_type=F32)

    span = part * rows
    theirs = pl.ds(pl.multiple_of((1 - core) * span, span), span)
    ours = pl.ds(pl.multiple_of(core * span, span), span)
    xsend[...] = acc[theirs, :].astype(BF)
    xc = send(xsend, xrecv, S_X, R_X, sib)

    @pl.when(holds)
    def _():
        pltpu.make_async_copy(hrows, hblock, msem.at[8]).wait()

    @pl.when(jnp.logical_not(holds))
    def _():
        remote(hrows, hblock, S_H, R_H, sib).wait_recv()

    def logits_of(v):
        top = v.astype(BF)
        rest = (v - top.astype(F32)).astype(BF)
        got = jnp.dot(jnp.concatenate([top, rest], axis=0), hblock[...], preferred_element_type=F32)
        return got[:span] + got[span:]

    lgsend[...] = logits_of(acc[theirs, :])
    lc = send(lgsend, lgrecv, S_LG, R_LG, sib)
    pcols = prompts[:, xcols].astype(F32)
    here = acc[ours, :] + jnp.concatenate([pcols] * part, axis=0)
    lgts = logits_of(here)
    xc.wait_recv()
    out = here + xrecv[...].astype(F32)
    squares = out * out
    sq = squares[:, 0:128]
    for off in range(128, block, 128):
        sq = sq + squares[:, off : off + 128]
    top = sq.astype(BF).astype(F32)
    halves = jnp.concatenate([top, sq - top], axis=1).astype(BF)
    sums = lax.dot_general(jnp.ones((8, 256), BF), halves, NT, preferred_element_type=F32)
    for i in range(part):
        lsend[i, rows : rows + 8, :] = jnp.zeros((8, labels), F32)
        lsend[i, rows : rows + 8, 0:rows] = sums[:, i * rows : (i + 1) * rows]
    lc.wait_recv()
    for i in range(part):
        r = slice(i * rows, (i + 1) * rows)
        lsend[i, 0:rows, :] = lgts[r] + lgrecv[r, :]
    for i in range(part):
        m = core * part + i

        @pl.when(m != me)
        def _(i=i, m=m):
            remote(lsend.at[i], lrecv.at[me], S_L + i, R_L + me, {"pop": m}).start()

    @pl.when(holds)
    def _():
        tot = lsend[me % part]
        for k in range(1, pop):
            p = (me + k) % pop
            remote(lsend.at[0], lrecv.at[p], S_L, R_L + p, {"pop": p}).wait_recv()
            tot = tot + lrecv[p]
        eye = (
            lax.broadcasted_iota(jnp.int32, (rows, labels), 0) == lax.broadcasted_iota(jnp.int32, (rows, labels), 1)
        ).astype(F32)
        ssq = jnp.sum(eye * tot[rows : rows + 1, :], axis=1, keepdims=True)
        lgt = tot[0:rows, :] * lax.rsqrt(ssq * (1.0 / width) + norm_eps)
        spread_t = jnp.where(eye[:, :rows] > 0.0, jnp.broadcast_to(targets[...].astype(F32), (rows, rows)), 0.0)
        target = jnp.sum(spread_t, axis=1, keepdims=True).astype(jnp.int32)
        picks = target == lax.broadcasted_iota(jnp.int32, (rows, labels), 1)
        picked = jnp.sum(jnp.where(picks, lgt, 0.0), axis=1, keepdims=True)
        term = picked - jnp.log(jnp.sum(jnp.exp(lgt), axis=1, keepdims=True))
        rbuf[me] = jnp.sum(jnp.broadcast_to(term, (rows, 128)), axis=0, keepdims=True) * (1.0 / rows)
        for k in range(1, pop):
            for t in range(2):
                remote(
                    rbuf.at[me], rbuf.at[me], S_R + 2 * k + t, R_R + me, {"pop": (me + k) % pop, "tensor": t}
                ).start()
        remote(rbuf.at[me], rbuf.at[me], S_R, R_R + me, sib).start()

    for k in range(1, pop):
        p = (me + k) % pop
        remote(rbuf.at[p], rbuf.at[p], S_R, R_R + p, sib).wait_recv()

    @pl.when(jnp.logical_not(holds))
    def _():
        remote(rbuf.at[me], rbuf.at[me], S_R, R_R + me, sib).wait_recv()

    centre = sum(rbuf[m] for m in range(members)) * (1.0 / members)
    spread = sum((rbuf[m] - centre) * (rbuf[m] - centre) for m in range(members)) * (1.0 / members)
    inv = lax.rsqrt(spread + norm_eps)
    score_out[...] = jnp.broadcast_to((rbuf[me] - centre) * inv, score_out.shape)
    of = lax.broadcasted_iota(jnp.int32, (members * rank, 128), 0) // rank
    column = jnp.zeros((members * rank, 128), F32)
    for m in range(members):
        column = jnp.where(of == m, jnp.broadcast_to((rbuf[m] - centre) * inv, column.shape), column)
    for off in range(0, block, 128):
        at = slice(off, off + 128)
        weighted_out[:, at] = (dcat[0 : members * rank, at].astype(F32) * column).astype(BF)

    for d in pending:
        d.wait_send()

    @pl.when(z < outer - 1)
    def _():
        chain(z, z + 1, S_P).wait_send()

    @pl.when(z > 0)
    def _():
        chain(z, z - 1, S_M).wait_send()

    @pl.when(middle)
    def _():
        chain(z - 1, z + 1, S_P + 1).wait_send()
        chain(z + 1, z - 1, S_M + 1).wait_send()
        chain(far, end, S_P + 2).wait_send()

    for i in range(part):
        m = core * part + i

        @pl.when(m != me)
        def _(i=i, m=m):
            remote(lsend.at[i], lrecv.at[me], S_L + i, R_L + me, {"pop": m}).wait_send()

    @pl.when(holds)
    def _():
        remote(hrows, hblock, S_H, R_H, sib).wait_send()
        for k in range(1, pop):
            for t in range(2):
                remote(
                    rbuf.at[me], rbuf.at[me], S_R + 2 * k + t, R_R + me, {"pop": (me + k) % pop, "tensor": t}
                ).wait_send()
        remote(rbuf.at[me], rbuf.at[me], S_R, R_R + me, sib).wait_send()


def update_kernel(norm, step, dif, weighted, score, out, score_out, left, sem):
    members, rank, ff = dif.shape
    width = weighted.shape[1]
    copies = []
    blocks = [(start, min(step, ff - start)) for start in range(0, ff, step)]
    for n, (start, size) in enumerate(blocks):
        at = pl.ds(start, size)
        rows = jnp.concatenate([dif[m, :, at].astype(F32) for m in range(members)], axis=0).T.astype(BF)
        for c in range(0, width, 256):
            got = jnp.dot(rows, weighted[:, c : c + 256], preferred_element_type=F32)
            left[at, c : c + 256] = (got * norm).astype(BF)
        d = pltpu.make_async_copy(left.at[at], out.at[at], sem.at[n])
        d.start()
        copies.append(d)
    score_out[0] = score[0, 0]
    for d in copies:
        d.wait()


def fast_body(
    pop, prompts, gate_weight, up_weight, down_weight, gate_in, gof, up_in, uof, dif, dout, head, targets
):
    rows, width = prompts.shape
    block, ff = gate_weight.shape
    members, _, rank = dif.shape
    outer = pop // 2
    chunk = -(-(ff // 128) // pop) * 128
    labels = head.shape[1]
    swap = lambda v: jnp.swapaxes(v, 1, 2)
    dif_t, dout_t = swap(dif), swap(dout)
    vm = pl.BlockSpec(memory_space=pltpu.VMEM)
    hb = pl.BlockSpec(memory_space=pl.ANY)
    V = pltpu.VMEM
    D = pltpu.SemaphoreType.DMA
    big = members * rows
    weighted, score = pl.pallas_call(
        functools.partial(pair_kernel, pop, 2 * ff),
        out_shape=(
            jax.ShapeDtypeStruct((members * rank, block), BF),
            jax.ShapeDtypeStruct((8, 128), F32),
        ),
        in_specs=[hb] * 12,
        out_specs=(vm, vm),
        scratch_shapes=[
            V((rows, width), BF), V((rank, width), BF), V((rank, ff), BF), V((rank, width), BF), V((rank, ff), BF),
            V((members, rank, ff), BF), V((members, rank, block), BF), V((1, rows), jnp.int32),
            V((pop, block, chunk), BF), V((pop, block, chunk), BF), V((ff, block), BF),
            V((rows, width), BF), V((2 * rank, ff), F32), V((members, 2 * rank, ff), BF),
            V((members, rows, 128), BF), V((2, rows, chunk), F32),
            V((outer, 2, rows, chunk), BF), V((outer, 2, rows, chunk), BF),
            V((outer - 1, 2, rows, chunk), BF), V((outer - 1, 2, rows, chunk), BF),
            V((pop, 2, rows, chunk), BF),
            V((2 * big, 128), BF), V((big, chunk), BF), V((big, block), F32), V((big, members * rank), F32),
            V((2 * members * rank, block), BF), V((big // 2, block), BF), V((big // 2, block), BF),
            V((block, labels), BF),
            V((big // 2, labels), F32), V((big // 2, labels), F32),
            V((members // 2, rows + 8, labels), F32), V((members, rows + 8, labels), F32),
            V((members, 1, 128), F32),
            D((2 * pop,)), D((4,)), D((9,)), D((56,)), D((51,)),
        ],
        compiler_params=pltpu.CompilerParams(
            collective_id=0, has_side_effects=True, vmem_limit_bytes=58 * 1000 * 1000
        ),
        name="pair",
    )(
        prompts, gate_weight, up_weight, down_weight, swap(gate_in)[0], swap(gof)[0], swap(up_in)[0],
        swap(uof)[0], dif_t, dout_t, head, targets[None],
    )
    step = 512
    update, scores = pl.pallas_call(
        functools.partial(update_kernel, 1.0 / math.sqrt(members * rank), step),
        out_shape=(jax.ShapeDtypeStruct((ff, block), BF), jax.ShapeDtypeStruct((1,), F32)),
        in_specs=[vm, vm, vm],
        out_specs=(hb, pl.BlockSpec(memory_space=pltpu.SMEM)),
        scratch_shapes=[
            V((ff, block), BF), D((-(-ff // step),)),
        ],
        compiler_params=pltpu.CompilerParams(vmem_limit_bytes=40 * 1000 * 1000),
        name="update",
    )(dif_t, weighted, score)
    return update, scores


def solution(mesh):
    placed = (
        P("groups", None),
        P("pop", "tensor"),
        P("pop", "tensor"),
        P("tensor", "pop"),
        P(("groups", "pop"), None, None),
        P(("groups", "pop"), "tensor", None),
        P(("groups", "pop"), None, None),
        P(("groups", "pop"), "tensor", None),
        P("groups", "tensor", None),
        P("groups", "pop", None),
        P("tensor", None),
        P("groups"),
    )
    pop = mesh.shape["pop"]
    run = functools.partial(fast_body, pop) if pop == 8 and mesh.shape["tensor"] == 2 else body
    return jax.shard_map(
        run,
        mesh=mesh,
        in_specs=placed,
        out_specs=(P(("groups", "tensor"), "pop"), P(("groups", "pop"))),
        check_vma=False,
    )
```

```python
import functools
import math

import jax
import jax.numpy as jnp
from jax import lax
from jax.experimental import pallas as pl
from jax.experimental.pallas import tpu as pltpu
from jax.sharding import PartitionSpec as P

noise_scale = 0.2
norm_eps = 1e-06


def scaled_rows(values):
    return values * lax.rsqrt(jnp.mean(values * values, axis=-1, keepdims=True) + norm_eps)


def build_hidden(
    gate_baseline, up_baseline, lowrank_gate, lowrank_up, gate_output_factors, up_output_factors
):
    gate_activation = gate_baseline.astype(jnp.float32)[None] + jnp.einsum(
        "hvw,hpw->hvp", lowrank_gate, gate_output_factors, preferred_element_type=jnp.float32
    )
    upper_bound = up_baseline.astype(jnp.float32)[None] + jnp.einsum(
        "hvw,hpw->hvp", lowrank_up, up_output_factors, preferred_element_type=jnp.float32
    )
    return (jax.nn.silu(gate_activation) * upper_bound).astype(jnp.bfloat16)


def label_terms(logits, targets):
    labels = logits.shape[1]
    picks = targets[:, None] == jnp.arange(labels, dtype=jnp.int32)[None, :]
    picked = jnp.sum(jnp.where(picks, logits, 0.0), axis=1)
    return picked - jnp.log(jnp.sum(jnp.exp(logits), axis=1))


def body(
    prompts,
    gate_weight,
    up_weight,
    down_weight_matrix,
    gate_in,
    gate_output_factors,
    up_in,
    up_output_factors,
    down_input_factors,
    down_out,
    label_head,
    targets,
):
    member = lax.axis_index("pop")
    width = prompts.shape[1]
    in_block = gate_weight.shape[0]
    ffn_half = gate_output_factors.shape[1]
    total_ff = ffn_half * lax.axis_size("tensor")
    members = down_input_factors.shape[0]
    rank = down_input_factors.shape[2]
    prompt_f = prompts.astype(jnp.float32)
    normed = scaled_rows(prompt_f).astype(jnp.bfloat16)
    own_cols = lax.dynamic_slice_in_dim(normed, member * in_block, in_block, 1)
    part_gate = jnp.dot(own_cols, gate_weight, preferred_element_type=jnp.float32)
    part_up = jnp.dot(own_cols, up_weight, preferred_element_type=jnp.float32)
    total_gate, total_up = lax.psum((part_gate, part_up), "pop")
    gate_baseline = total_gate.astype(jnp.bfloat16)
    up_baseline = total_up.astype(jnp.bfloat16)
    in_scale = noise_scale / math.sqrt(width)
    lowrank_gate = (
        in_scale * jnp.einsum("rd,mdk->mrk", normed, gate_in, preferred_element_type=jnp.float32)
    ).astype(jnp.bfloat16)
    lowrank_up = (
        in_scale * jnp.einsum("rd,mdk->mrk", normed, up_in, preferred_element_type=jnp.float32)
    ).astype(jnp.bfloat16)
    down_scale = noise_scale / math.sqrt(total_ff)
    hidden_state = build_hidden(
        gate_baseline, up_baseline, lowrank_gate, lowrank_up, gate_output_factors, up_output_factors
    )
    hidden_portion = lax.all_gather(hidden_state, "pop", axis=0, tiled=True)
    out_piece = down_out.astype(jnp.float32)
    entry_point = jnp.einsum(
        "uaz,zh->uah", hidden_portion, down_weight_matrix, preferred_element_type=jnp.float32
    )
    low_part = down_scale * jnp.einsum(
        "lpq,lqb->lpb", hidden_portion, down_input_factors, preferred_element_type=jnp.float32
    )
    partial_rows = entry_point + jnp.einsum(
        "mrk,mdk->mrd", low_part, out_piece, precision=lax.Precision.HIGHEST
    )
    rows_here = lax.all_to_all(partial_rows, "pop", split_axis=0, concat_axis=2, tiled=True)
    summed = lax.psum(rows_here, "tensor")[0]
    output = prompt_f + summed
    final = scaled_rows(output).astype(jnp.bfloat16)
    half = label_head.shape[0]
    own_half = lax.dynamic_slice_in_dim(final, lax.axis_index("tensor") * half, half, 1)
    logits = lax.psum(jnp.dot(own_half, label_head, preferred_element_type=jnp.float32), "tensor")
    reward = jnp.mean(label_terms(logits, targets))
    rewards = lax.all_gather(reward.reshape(1), "pop", axis=0, tiled=True)
    centre = jnp.mean(rewards)
    spread = jnp.mean((rewards - centre) * (rewards - centre))
    scores = (rewards - centre) * lax.rsqrt(spread + norm_eps)
    weighted = (scores[:, None, None] * down_out.astype(jnp.float32)).astype(jnp.bfloat16)
    update = jnp.einsum(
        "mfk,mdk->fd", down_input_factors, weighted, preferred_element_type=jnp.float32
    ) * (1.0 / math.sqrt(members * rank))
    own_score = lax.dynamic_slice_in_dim(scores, member, 1, 0)
    return (update.astype(jnp.bfloat16), own_score)


BF = jnp.bfloat16
F32 = jnp.float32
HI = lax.Precision.HIGHEST
NT = (((1,), (1,)), ((), ()))
TN = (((0,), (0,)), ((), ()))


def pair_kernel(
    pop, total_ff,
    prompts_in, gate_w, up_w, down_w, gate_in_h, gof_h, up_in_h, uof_h, dif_h, dout_h, head, targets_in,
    weighted_out,
    prompts, gate_in, gof, up_in, uof, dif, dout, targets,
    wg, wu, dw, normed, fbuild, fac, low, own, ysend, yrecv, zsend, zrecv, base,
    lhs, hid, acc, lowd, dcat, xsend, xrecv, hblock,
    lgsend, lgrecv, lsend, lrecv, rbuf,
    wsem, dsem, msem, ssem, rsem,
):
    rows, width = prompts.shape
    block, ff = gate_w.shape
    outer = pop // 2
    piece = wg.shape[2]
    chunk = 2 * piece
    members = pop
    rank = gof.shape[0]
    part = members // 2
    big = members * rows
    labels = head.shape[1]
    over = pop * chunk - ff
    tile = 256
    me = lax.axis_index("pop")
    core = lax.axis_index("tensor")
    z = me // 2
    y = me % 2
    sib = {"tensor": 1 - core}
    middle = (z >= 1) & (z <= outer - 2)

    def spot(zz, yy):
        return zz * 2 + yy

    def start_of(c):
        return pl.multiple_of(c * chunk - (c // (pop - 1)) * over, 128)

    def remote(src, dst, sidx, ridx, dev):
        return pltpu.make_async_remote_copy(
            src_ref=src, dst_ref=dst, send_sem=ssem.at[sidx], recv_sem=rsem.at[ridx],
            device_id=dev, device_id_type=pl.DeviceIdType.MESH,
        )

    barrier = pltpu.get_barrier_semaphore()
    for k in range(1, pop):
        for t in range(2):
            pl.semaphore_signal(
                barrier, inc=1, device_id={"pop": (me + k) % pop, "tensor": t}, device_id_type=pl.DeviceIdType.MESH
            )
    pl.semaphore_signal(barrier, inc=1, device_id=sib, device_id_type=pl.DeviceIdType.MESH)

    def load(src, dst, sem):
        d = pltpu.make_async_copy(src, dst, sem)
        d.start()
        return d

    lgof = load(gof_h, gof, msem.at[0])
    luof = load(uof_h, uof, msem.at[1])
    lprompts = load(prompts_in, prompts, msem.at[2])
    lgin = load(gate_in_h, gate_in, msem.at[3])
    luin = load(up_in_h, up_in, msem.at[4])
    owners = [spot((z + 1 + i % outer) % outer, (1 - y) if i < outer else y) for i in range(pop)]

    def weights(h, i):
        cols = pl.ds(pl.multiple_of(start_of(owners[i]) + h * piece, 128), piece)
        n = h * pop + i
        return (
            load(gate_w.at[:, cols], wg.at[n], wsem.at[2 * n]),
            load(up_w.at[:, cols], wu.at[n], wsem.at[2 * n + 1]),
        )

    steps = [(0, i) for i in range(outer + 2)] + [(1, 0), (1, 1), (0, 6), (0, 7)]
    steps += [(1, i) for i in range(2, pop)]
    loads = {at: weights(*at) for at in steps[:1]}
    for d in (lgof, luof, lprompts, lgin, luin):
        d.wait()
    for at in steps[1:]:
        loads[at] = weights(*at)
    ldif = load(dif_h, dif, msem.at[5])
    ldout = load(dout_h, dout, msem.at[6])
    ltar = load(targets_in, targets, msem.at[7])

    fbuild[0:rank, :] = gof[...].astype(F32)
    fbuild[rank : 2 * rank, :] = uof[...].astype(F32)
    fac[me] = fbuild[...].astype(BF)
    pl.semaphore_wait(barrier, 2 * pop - 1)

    pending = []
    S_FY, S_P, S_M, S_F, S_LOW, S_Y, S_Z, S_A, S_X, S_LG, S_H, S_L, S_R = (
        0, 1, 7, 13, 16, 24, 32, 38, 52, 53, 54, 55, 59)
    R_FY, R_FZ, R_FH, R_LOW, R_Y, R_Z, R_A, R_X, R_LG, R_H, R_L, R_R = (
        0, 1, 9, 13, 21, 29, 35, 51, 52, 53, 54, 62)

    def send(src, dst, sidx, ridx, dev):
        d = remote(src, dst, sidx, ridx, dev)
        d.start()
        pending.append(d)
        return d

    cut = ff // 256 * 128

    def chain(o, to, sidx, h):
        src = fac.at[spot(o, y), :, pl.ds(h * cut, cut if h == 0 else ff - cut)]
        return remote(src, src, sidx + 3 * h, R_FZ + 2 * o + h, {"pop": spot(to, y)})

    fy = send(fac.at[me], fac.at[me], S_FY, R_FY, {"pop": spot(z, 1 - y)})

    for h in range(2):

        @pl.when(z < outer - 1)
        def _(h=h):
            chain(z, z + 1, S_P, h).start()

        @pl.when(z > 0)
        def _(h=h):
            chain(z, z - 1, S_M, h).start()

    hrows = head.at[pl.ds(pl.multiple_of((me % part) * block, block), block)]
    holds = core == me // part

    x = prompts[...].astype(F32)
    normed[...] = (x * lax.rsqrt(jnp.mean(x * x, axis=-1, keepdims=True) + norm_eps)).astype(BF)

    scale = noise_scale / math.sqrt(width)
    lg = (scale * lax.dot_general(normed[...], gate_in[...], NT, preferred_element_type=F32)).astype(BF)
    lu = (scale * lax.dot_general(normed[...], up_in[...], NT, preferred_element_type=F32)).astype(BF)
    krow = lax.broadcasted_iota(jnp.int32, (rank, 128), 0)
    lane = lax.broadcasted_iota(jnp.int32, (rank, 128), 1)
    sel_g = (lane == me * 2 * rank + krow).astype(F32).astype(BF)
    sel_u = (lane == me * 2 * rank + rank + krow).astype(F32).astype(BF)
    low[me] = (
        jnp.dot(lg, sel_g, preferred_element_type=F32) + jnp.dot(lu, sel_u, preferred_element_type=F32)
    ).astype(BF)
    lcopies = [
        send(low.at[me], low.at[me], S_LOW + k, R_LOW + k, {"pop": (me + k) % pop}) for k in range(1, pop)
    ]

    xcols = pl.ds(pl.multiple_of(me * block, block), block)
    mine_n = normed[:, xcols]

    def relay_first(h):
        @pl.when(middle)
        def _():
            chain(z - 1, z, S_P, h).wait_recv()
            chain(z - 1, z + 1, S_P + 1, h).start()
            chain(z + 1, z, S_M, h).wait_recv()
            chain(z + 1, z - 1, S_M + 1, h).start()

    far = 3 * (2 - z)
    end = 3 * (z - 1)

    def relay_second(h):
        @pl.when(middle)
        def _():
            chain(far, z, S_P, h).wait_recv()
            chain(far, end, S_P + 2, h).start()

    order = [
        jnp.where(z == 0, 1, z - 1),
        jnp.where(z == outer - 1, 1, jnp.where(z == 2, 3, 2)),
        jnp.where(z < 2, 3, 0),
    ]

    def forward(n):
        o = order[n]

        @pl.when(jnp.logical_not(middle))
        def _():
            for h in range(2):
                chain(o, z, S_P, h).wait_recv()

        src = fac.at[spot(o, y)]
        send(src, src, S_F + n, R_FH + o, {"pop": spot(z, 1 - y)})

    ycopies = {}
    zcopies = {}
    dloads = []
    step = ff // 4
    across = {"pop": spot(z, 1 - y)}

    def product(h, i):
        loads[h, i][0].wait()
        loads[h, i][1].wait()
        return [jnp.dot(mine_n, w[h * pop + i], preferred_element_type=F32) for w in (wg, wu)]

    def part_out(h, i):
        got = product(h, i)
        n = h * outer + i
        for g in range(2):
            ysend[n, g] = got[g].astype(BF)
        ycopies[h, i] = send(ysend.at[n], yrecv.at[n], S_Y + n, R_Y + n, across)

    def part_own(h, i):
        got = product(h, i)
        for g in range(2):
            own[h * outer + i - outer, g] = got[g]

    def part_on(h, i):
        j = i - outer
        n = h * outer + j
        ycopies[h, j].wait_recv()
        if i == pop - 1:
            for g in range(2):
                own[n, g] = own[n, g] + yrecv[n, g].astype(F32)
            return
        n3 = h * (outer - 1) + j
        for g in range(2):
            zsend[n3, g] = (own[n, g] + yrecv[n, g].astype(F32)).astype(BF)
        zcopies[h, j] = send(
            zsend.at[n3], zrecv.at[n3], S_Z + n3, R_Z + n3, {"pop": spot((z + 1 + j) % outer, y)}
        )

    gaps = [(o - z + outer) % outer for o in order]

    def held(slot, h):
        return base.at[2 * slot + h]

    def gather(h):
        last = h * outer + outer - 1
        total = [own[last, 0], own[last, 1]]
        for j in range(outer - 1):
            zcopies[h, j].wait_recv()
            for g in range(2):
                total[g] = total[g] + zrecv[h * (outer - 1) + j, g].astype(F32)
        for g in range(2):
            base[h, g] = total[g].astype(BF)
        for n in range(outer - 1):
            send(
                held(0, h), held(gaps[n], h), S_A + 3 * h + n, R_A + 2 * gaps[n] + h, {"pop": spot(order[n], y)}
            )

    def near(n):
        return (outer - gaps[n]) % outer

    def arrive(n, h):
        k = near(n)
        remote(held(k, h), held(k, h), S_A, R_A + 2 * k + h, sib).wait_recv()
        send(held(k, h), held(outer + k, h), S_A + 8 + 3 * h + n, R_A + 2 * (outer + k) + h, across)

    def hand(h):
        send(held(0, h), held(outer, h), S_A + 6 + h, R_A + 2 * outer + h, across)

    for i in range(outer):
        part_out(0, i)
    part_own(0, 4)
    relay_first(0)
    part_own(0, 5)
    relay_first(1)
    part_out(1, 0)
    part_out(1, 1)
    part_on(0, 4)
    part_own(0, 6)
    part_on(0, 5)
    part_own(0, 7)
    part_on(0, 6)
    relay_second(0)
    part_out(1, 2)
    relay_second(1)
    part_out(1, 3)
    part_on(0, 7)
    for n in range(4):
        at = pl.ds(n * step, step)
        dloads.append(load(down_w.at[at], dw.at[at], dsem.at[n]))
    part_own(1, 4)
    part_own(1, 5)
    part_on(1, 4)
    forward(0)
    part_own(1, 6)
    part_on(1, 5)
    part_own(1, 7)
    forward(1)
    part_on(1, 6)
    gather(0)
    forward(2)
    hand(0)
    part_on(1, 7)

    @pl.when(holds)
    def _():
        remote(hrows, hblock, S_H, R_H, sib).start()
        pltpu.make_async_copy(hrows, hblock, msem.at[8]).start()

    ldout.wait()
    ldif.wait()
    ltar.wait()
    dall = jnp.concatenate([dout[m].astype(F32) for m in range(members)], axis=0)
    dcat[...] = jnp.concatenate([dall, dall], axis=0).astype(BF)
    acc[...] = jnp.zeros_like(acc)
    lowd[...] = jnp.zeros_like(lowd)
    for d in lcopies:
        d.wait_recv()
    coef = jnp.concatenate([low[m].astype(F32) for m in range(members)], axis=0)
    lane = lax.broadcasted_iota(jnp.int32, coef.shape, 1)
    row = lax.broadcasted_iota(jnp.int32, coef.shape, 0) % rows
    kk = 2 * rank * members
    gate_lane = lane % (2 * rank) < rank
    gate_lhs = jnp.where(lane < kk, jnp.where(gate_lane, coef, 0.0), (lane == kk + row).astype(F32))
    up_lhs = jnp.where(lane < kk, jnp.where(gate_lane, 0.0, coef), (lane == kk + rows + row).astype(F32))
    lhs[...] = jnp.concatenate([0.5 * gate_lhs, up_lhs], axis=0).astype(BF)

    gather(1)
    hand(1)
    for n in range(outer - 1):
        arrive(n, 0)

    for d in dloads:
        d.wait()
    fy.wait_recv()
    for n in range(1, outer):
        o = (z + n) % outer
        src = fac.at[spot(o, 1 - y)]
        remote(src, src, S_F, R_FH + o, across).wait_recv()

    def expand(slot, c):
        start = start_of(c)
        skip = (c // (pop - 1)) * over

        pad = jnp.zeros((128 - kk - 2 * rows, tile), F32)
        for off in range(0, chunk, tile):
            at = pl.ds(pl.multiple_of(start + off, 128), tile)
            parts = [fac[m, :, at].astype(F32) for m in range(members)]
            low_off = off % piece
            parts += [
                base[2 * slot + off // piece, g, :, low_off : low_off + tile].astype(F32) for g in range(2)
            ]
            keep = (off >= skip).astype(F32)
            rhs = (jnp.concatenate(parts + [pad], axis=0) * keep).astype(BF)
            both = jnp.dot(lhs[...], rhs, preferred_element_type=F32)
            gate, up = both[:big], both[big:]
            hid[:, off : off + tile] = ((gate + gate * jnp.tanh(gate)) * up).astype(BF)
        h = hid[...]
        at = pl.ds(start, chunk)
        right = jnp.concatenate([dif[m, :, at].astype(F32) for m in range(members)], axis=0).astype(BF)
        lowd[...] += lax.dot_general(h, right, NT, preferred_element_type=F32)
        for off in range(0, block, tile):
            acc[:, off : off + tile] += jnp.dot(h, dw[at, off : off + tile], preferred_element_type=F32)

    expand(0, me)
    for n in range(outer - 1):
        arrive(n, 1)
        expand(near(n), spot(order[n], y))
    for h in range(2):
        remote(held(outer, h), held(outer, h), S_A, R_A + 2 * outer + h, sib).wait_recv()
    expand(outer, spot(z, 1 - y))
    for n in range(outer - 1):
        k = outer + near(n)
        for h in range(2):
            remote(held(k, h), held(k, h), S_A, R_A + 2 * k + h, sib).wait_recv()
        expand(k, spot(order[n], 1 - y))

    mine = lax.broadcasted_iota(jnp.int32, lowd.shape, 0) // rows == lax.broadcasted_iota(jnp.int32, lowd.shape, 1) // rank
    lowm = jnp.where(mine, lowd[...] * (noise_scale / math.sqrt(total_ff)), 0.0)
    top = lowm.astype(BF).astype(F32)
    pair = jnp.concatenate([top, lowm - top], axis=1).astype(BF)
    acc[...] += jnp.dot(pair, dcat[...], preferred_element_type=F32)

    span = part * rows
    theirs = pl.ds(pl.multiple_of((1 - core) * span, span), span)
    ours = pl.ds(pl.multiple_of(core * span, span), span)
    xsend[...] = acc[theirs, :].astype(BF)
    xc = send(xsend, xrecv, S_X, R_X, sib)

    @pl.when(holds)
    def _():
        pltpu.make_async_copy(hrows, hblock, msem.at[8]).wait()

    @pl.when(jnp.logical_not(holds))
    def _():
        remote(hrows, hblock, S_H, R_H, sib).wait_recv()

    def logits_of(v):
        top = v.astype(BF)
        rest = (v - top.astype(F32)).astype(BF)
        got = jnp.dot(jnp.concatenate([top, rest], axis=0), hblock[...], preferred_element_type=F32)
        return got[:span] + got[span:]

    lgsend[...] = logits_of(acc[theirs, :])
    lc = send(lgsend, lgrecv, S_LG, R_LG, sib)
    pcols = prompts[:, xcols].astype(F32)
    here = acc[ours, :] + jnp.concatenate([pcols] * part, axis=0)
    lgts = logits_of(here)
    xc.wait_recv()
    out = here + xrecv[...].astype(F32)
    squares = out * out
    sq = squares[:, 0:128]
    for off in range(128, block, 128):
        sq = sq + squares[:, off : off + 128]
    top = sq.astype(BF).astype(F32)
    halves = jnp.concatenate([top, sq - top], axis=1).astype(BF)
    sums = lax.dot_general(jnp.ones((8, 256), BF), halves, NT, preferred_element_type=F32)
    for i in range(part):
        lsend[i, rows : rows + 8, :] = jnp.zeros((8, labels), F32)
        lsend[i, rows : rows + 8, 0:rows] = sums[:, i * rows : (i + 1) * rows]
    lc.wait_recv()
    for i in range(part):
        r = slice(i * rows, (i + 1) * rows)
        lsend[i, 0:rows, :] = lgts[r] + lgrecv[r, :]
    for i in range(part):
        m = core * part + i

        @pl.when(m != me)
        def _(i=i, m=m):
            remote(lsend.at[i], lrecv.at[me], S_L + i, R_L + me, {"pop": m}).start()

    @pl.when(holds)
    def _():
        tot = lsend[me % part]
        for k in range(1, pop):
            p = (me + k) % pop
            remote(lsend.at[0], lrecv.at[p], S_L, R_L + p, {"pop": p}).wait_recv()
            tot = tot + lrecv[p]
        eye = (
            lax.broadcasted_iota(jnp.int32, (rows, labels), 0) == lax.broadcasted_iota(jnp.int32, (rows, labels), 1)
        ).astype(F32)
        ssq = jnp.sum(eye * tot[rows : rows + 1, :], axis=1, keepdims=True)
        lgt = tot[0:rows, :] * lax.rsqrt(ssq * (1.0 / width) + norm_eps)
        spread_t = jnp.where(eye[:, :rows] > 0.0, jnp.broadcast_to(targets[...].astype(F32), (rows, rows)), 0.0)
        target = jnp.sum(spread_t, axis=1, keepdims=True).astype(jnp.int32)
        picks = target == lax.broadcasted_iota(jnp.int32, (rows, labels), 1)
        picked = jnp.sum(jnp.where(picks, lgt, 0.0), axis=1, keepdims=True)
        term = picked - jnp.log(jnp.sum(jnp.exp(lgt), axis=1, keepdims=True))
        rbuf[me] = jnp.sum(jnp.broadcast_to(term, (rows, 128)), axis=0, keepdims=True) * (1.0 / rows)
        for k in range(1, pop):
            for t in range(2):
                remote(
                    rbuf.at[me], rbuf.at[me], S_R + 2 * k + t, R_R + me, {"pop": (me + k) % pop, "tensor": t}
                ).start()
        remote(rbuf.at[me], rbuf.at[me], S_R, R_R + me, sib).start()

    for k in range(1, pop):
        p = (me + k) % pop
        remote(rbuf.at[p], rbuf.at[p], S_R, R_R + p, sib).wait_recv()

    @pl.when(jnp.logical_not(holds))
    def _():
        remote(rbuf.at[me], rbuf.at[me], S_R, R_R + me, sib).wait_recv()

    centre = sum(rbuf[m] for m in range(members)) * (1.0 / members)
    spread = sum((rbuf[m] - centre) * (rbuf[m] - centre) for m in range(members)) * (1.0 / members)
    inv = lax.rsqrt(spread + norm_eps)
    weighted_out[members * rank :, 0:128] = jnp.broadcast_to((rbuf[me] - centre) * inv, (8, 128))
    of = lax.broadcasted_iota(jnp.int32, (members * rank, 128), 0) // rank
    column = jnp.zeros((members * rank, 128), F32)
    for m in range(members):
        column = jnp.where(of == m, jnp.broadcast_to((rbuf[m] - centre) * inv, column.shape), column)
    for off in range(0, block, 128):
        at = slice(off, off + 128)
        weighted_out[0 : members * rank, at] = (dcat[0 : members * rank, at].astype(F32) * column).astype(BF).astype(F32)

    for d in pending:
        d.wait_send()

    for h in range(2):

        @pl.when(z < outer - 1)
        def _(h=h):
            chain(z, z + 1, S_P, h).wait_send()

        @pl.when(z > 0)
        def _(h=h):
            chain(z, z - 1, S_M, h).wait_send()

        @pl.when(middle)
        def _(h=h):
            chain(z - 1, z + 1, S_P + 1, h).wait_send()
            chain(z + 1, z - 1, S_M + 1, h).wait_send()
            chain(far, end, S_P + 2, h).wait_send()

    for i in range(part):
        m = core * part + i

        @pl.when(m != me)
        def _(i=i, m=m):
            remote(lsend.at[i], lrecv.at[me], S_L + i, R_L + me, {"pop": m}).wait_send()

    @pl.when(holds)
    def _():
        remote(hrows, hblock, S_H, R_H, sib).wait_send()
        for k in range(1, pop):
            for t in range(2):
                remote(
                    rbuf.at[me], rbuf.at[me], S_R + 2 * k + t, R_R + me, {"pop": (me + k) % pop, "tensor": t}
                ).wait_send()
        remote(rbuf.at[me], rbuf.at[me], S_R, R_R + me, sib).wait_send()


def update_kernel(norm, step, dif, weighted, out, score_out, left, right, sem):
    members, rank, ff = dif.shape
    width = weighted.shape[1]
    right[...] = weighted[0 : members * rank, :].astype(BF)
    copies = []
    blocks = [(start, min(step, ff - start)) for start in range(0, ff, step)]
    for n, (start, size) in enumerate(blocks):
        at = pl.ds(start, size)
        rows = jnp.concatenate([dif[m, :, at].astype(F32) for m in range(members)], axis=0).T.astype(BF)
        for c in range(0, width, 256):
            got = jnp.dot(rows, right[:, c : c + 256], preferred_element_type=F32)
            left[at, c : c + 256] = (got * norm).astype(BF)
        d = pltpu.make_async_copy(left.at[at], out.at[at], sem.at[n])
        d.start()
        copies.append(d)
    score_out[0] = weighted[members * rank, 0]
    for d in copies:
        d.wait()


def fast_body(
    pop, prompts, gate_weight, up_weight, down_weight, gate_in, gof, up_in, uof, dif, dout, head, targets
):
    rows, width = prompts.shape
    block, ff = gate_weight.shape
    members, _, rank = dif.shape
    outer = pop // 2
    chunk = -(-(ff // 128) // pop) * 128
    piece = chunk // 2
    labels = head.shape[1]
    swap = lambda v: jnp.swapaxes(v, 1, 2)
    dif_t, dout_t = swap(dif), swap(dout)
    vm = pl.BlockSpec(memory_space=pltpu.VMEM)
    hb = pl.BlockSpec(memory_space=pl.ANY)
    V = pltpu.VMEM
    D = pltpu.SemaphoreType.DMA
    big = members * rows
    weighted = pl.pallas_call(
        functools.partial(pair_kernel, pop, 2 * ff),
        out_shape=jax.ShapeDtypeStruct((members * rank + 8, block), F32),
        in_specs=[hb] * 12,
        out_specs=vm,
        scratch_shapes=[
            V((rows, width), BF), V((rank, width), BF), V((rank, ff), BF), V((rank, width), BF), V((rank, ff), BF),
            V((members, rank, ff), BF), V((members, rank, block), BF), V((1, rows), jnp.int32),
            V((2 * pop, block, piece), BF), V((2 * pop, block, piece), BF), V((ff, block), BF),
            V((rows, width), BF), V((2 * rank, ff), F32), V((members, 2 * rank, ff), BF),
            V((members, rows, 128), BF), V((pop, 2, rows, piece), F32),
            V((pop, 2, rows, piece), BF), V((pop, 2, rows, piece), BF),
            V((pop - 2, 2, rows, piece), BF), V((pop - 2, 2, rows, piece), BF),
            V((2 * pop, 2, rows, piece), BF),
            V((2 * big, 128), BF), V((big, chunk), BF), V((big, block), F32), V((big, members * rank), F32),
            V((2 * members * rank, block), BF), V((big // 2, block), BF), V((big // 2, block), BF),
            V((block, labels), BF),
            V((big // 2, labels), F32), V((big // 2, labels), F32),
            V((members // 2, rows + 8, labels), F32), V((members, rows + 8, labels), F32),
            V((members, 1, 128), F32),
            D((4 * pop,)), D((4,)), D((9,)), D((75,)), D((70,)),
        ],
        compiler_params=pltpu.CompilerParams(
            collective_id=0, has_side_effects=True, vmem_limit_bytes=60 * 1000 * 1000
        ),
        name="pair",
    )(
        prompts, gate_weight, up_weight, down_weight, swap(gate_in)[0], swap(gof)[0], swap(up_in)[0],
        swap(uof)[0], dif_t, dout_t, head, targets[None],
    )
    step = 512
    update, scores = pl.pallas_call(
        functools.partial(update_kernel, 1.0 / math.sqrt(members * rank), step),
        out_shape=(jax.ShapeDtypeStruct((ff, block), BF), jax.ShapeDtypeStruct((1,), F32)),
        in_specs=[vm, vm],
        out_specs=(hb, pl.BlockSpec(memory_space=pltpu.SMEM)),
        scratch_shapes=[
            V((ff, block), BF), V((members * rank, block), BF), D((-(-ff // step),)),
        ],
        compiler_params=pltpu.CompilerParams(vmem_limit_bytes=40 * 1000 * 1000),
        name="update",
    )(dif_t, weighted)
    return update, scores


def solution(mesh):
    placed = (
        P("groups", None),
        P("pop", "tensor"),
        P("pop", "tensor"),
        P("tensor", "pop"),
        P(("groups", "pop"), None, None),
        P(("groups", "pop"), "tensor", None),
        P(("groups", "pop"), None, None),
        P(("groups", "pop"), "tensor", None),
        P("groups", "tensor", None),
        P("groups", "pop", None),
        P("tensor", None),
        P("groups"),
    )
    pop = mesh.shape["pop"]
    run = functools.partial(fast_body, pop) if pop == 8 and mesh.shape["tensor"] == 2 else body
    return jax.shard_map(
        run,
        mesh=mesh,
        in_specs=placed,
        out_specs=(P(("groups", "tensor"), "pop"), P(("groups", "pop"))),
        check_vma=False,
    )
```

```python
import functools
import math

import jax
import jax.numpy as jnp
from jax import lax
from jax.experimental import pallas as pl
from jax.experimental.pallas import tpu as pltpu
from jax.sharding import PartitionSpec as P

noise_scale = 0.2
norm_eps = 1e-06


def scaled_rows(values):
    return values * lax.rsqrt(jnp.mean(values * values, axis=-1, keepdims=True) + norm_eps)


def build_hidden(
    gate_baseline, up_baseline, lowrank_gate, lowrank_up, gate_output_factors, up_output_factors
):
    gate_activation = gate_baseline.astype(jnp.float32)[None] + jnp.einsum(
        "hvw,hpw->hvp", lowrank_gate, gate_output_factors, preferred_element_type=jnp.float32
    )
    upper_bound = up_baseline.astype(jnp.float32)[None] + jnp.einsum(
        "hvw,hpw->hvp", lowrank_up, up_output_factors, preferred_element_type=jnp.float32
    )
    return (jax.nn.silu(gate_activation) * upper_bound).astype(jnp.bfloat16)


def label_terms(logits, targets):
    labels = logits.shape[1]
    picks = targets[:, None] == jnp.arange(labels, dtype=jnp.int32)[None, :]
    picked = jnp.sum(jnp.where(picks, logits, 0.0), axis=1)
    return picked - jnp.log(jnp.sum(jnp.exp(logits), axis=1))


def body(
    prompts,
    gate_weight,
    up_weight,
    down_weight_matrix,
    gate_in,
    gate_output_factors,
    up_in,
    up_output_factors,
    down_input_factors,
    down_out,
    label_head,
    targets,
):
    member = lax.axis_index("pop")
    width = prompts.shape[1]
    in_block = gate_weight.shape[0]
    ffn_half = gate_output_factors.shape[1]
    total_ff = ffn_half * lax.axis_size("tensor")
    members = down_input_factors.shape[0]
    rank = down_input_factors.shape[2]
    prompt_f = prompts.astype(jnp.float32)
    normed = scaled_rows(prompt_f).astype(jnp.bfloat16)
    own_cols = lax.dynamic_slice_in_dim(normed, member * in_block, in_block, 1)
    part_gate = jnp.dot(own_cols, gate_weight, preferred_element_type=jnp.float32)
    part_up = jnp.dot(own_cols, up_weight, preferred_element_type=jnp.float32)
    total_gate, total_up = lax.psum((part_gate, part_up), "pop")
    gate_baseline = total_gate.astype(jnp.bfloat16)
    up_baseline = total_up.astype(jnp.bfloat16)
    in_scale = noise_scale / math.sqrt(width)
    lowrank_gate = (
        in_scale * jnp.einsum("rd,mdk->mrk", normed, gate_in, preferred_element_type=jnp.float32)
    ).astype(jnp.bfloat16)
    lowrank_up = (
        in_scale * jnp.einsum("rd,mdk->mrk", normed, up_in, preferred_element_type=jnp.float32)
    ).astype(jnp.bfloat16)
    down_scale = noise_scale / math.sqrt(total_ff)
    hidden_state = build_hidden(
        gate_baseline, up_baseline, lowrank_gate, lowrank_up, gate_output_factors, up_output_factors
    )
    hidden_portion = lax.all_gather(hidden_state, "pop", axis=0, tiled=True)
    out_piece = down_out.astype(jnp.float32)
    entry_point = jnp.einsum(
        "uaz,zh->uah", hidden_portion, down_weight_matrix, preferred_element_type=jnp.float32
    )
    low_part = down_scale * jnp.einsum(
        "lpq,lqb->lpb", hidden_portion, down_input_factors, preferred_element_type=jnp.float32
    )
    partial_rows = entry_point + jnp.einsum(
        "mrk,mdk->mrd", low_part, out_piece, precision=lax.Precision.HIGHEST
    )
    rows_here = lax.all_to_all(partial_rows, "pop", split_axis=0, concat_axis=2, tiled=True)
    summed = lax.psum(rows_here, "tensor")[0]
    output = prompt_f + summed
    final = scaled_rows(output).astype(jnp.bfloat16)
    half = label_head.shape[0]
    own_half = lax.dynamic_slice_in_dim(final, lax.axis_index("tensor") * half, half, 1)
    logits = lax.psum(jnp.dot(own_half, label_head, preferred_element_type=jnp.float32), "tensor")
    reward = jnp.mean(label_terms(logits, targets))
    rewards = lax.all_gather(reward.reshape(1), "pop", axis=0, tiled=True)
    centre = jnp.mean(rewards)
    spread = jnp.mean((rewards - centre) * (rewards - centre))
    scores = (rewards - centre) * lax.rsqrt(spread + norm_eps)
    weighted = (scores[:, None, None] * down_out.astype(jnp.float32)).astype(jnp.bfloat16)
    update = jnp.einsum(
        "mfk,mdk->fd", down_input_factors, weighted, preferred_element_type=jnp.float32
    ) * (1.0 / math.sqrt(members * rank))
    own_score = lax.dynamic_slice_in_dim(scores, member, 1, 0)
    return (update.astype(jnp.bfloat16), own_score)


BF = jnp.bfloat16
F32 = jnp.float32
HI = lax.Precision.HIGHEST
NT = (((1,), (1,)), ((), ()))
TN = (((0,), (0,)), ((), ()))


def pair_kernel(
    pop, total_ff,
    prompts_in, gate_w, up_w, down_w, gate_in_h, gof_h, up_in_h, uof_h, dif_h, dout_h, head, targets_in,
    weighted_out,
    prompts, gate_in, gof, up_in, uof, dif, dout, targets,
    wg, wu, dw, normed, fbuild, fac, low, own, ysend, yrecv, zsend, zrecv, base,
    lhs, hid, acc, lowd, dcat, xsend, xrecv, hblock,
    lgsend, lgrecv, lsend, lrecv, rbuf,
    wsem, dsem, msem, ssem, rsem,
):
    rows, width = prompts.shape
    block, ff = gate_w.shape
    outer = pop // 2
    piece = wg.shape[2]
    chunk = 2 * piece
    members = pop
    rank = gof.shape[0]
    part = members // 2
    big = members * rows
    labels = head.shape[1]
    over = pop * chunk - ff
    tile = 256
    me = lax.axis_index("pop")
    core = lax.axis_index("tensor")
    z = me // 2
    y = me % 2
    sib = {"tensor": 1 - core}
    middle = (z >= 1) & (z <= outer - 2)

    def spot(zz, yy):
        return zz * 2 + yy

    def start_of(c):
        return pl.multiple_of(c * chunk - (c // (pop - 1)) * over, 128)

    def remote(src, dst, sidx, ridx, dev):
        return pltpu.make_async_remote_copy(
            src_ref=src, dst_ref=dst, send_sem=ssem.at[sidx], recv_sem=rsem.at[ridx],
            device_id=dev, device_id_type=pl.DeviceIdType.MESH,
        )

    barrier = pltpu.get_barrier_semaphore()
    for k in range(1, pop):
        for t in range(2):
            pl.semaphore_signal(
                barrier, inc=1, device_id={"pop": (me + k) % pop, "tensor": t}, device_id_type=pl.DeviceIdType.MESH
            )
    pl.semaphore_signal(barrier, inc=1, device_id=sib, device_id_type=pl.DeviceIdType.MESH)

    def load(src, dst, sem):
        d = pltpu.make_async_copy(src, dst, sem)
        d.start()
        return d

    lgof = load(gof_h, gof, msem.at[0])
    luof = load(uof_h, uof, msem.at[1])
    lprompts = load(prompts_in, prompts, msem.at[2])
    lgin = load(gate_in_h, gate_in, msem.at[3])
    luin = load(up_in_h, up_in, msem.at[4])
    owners = [spot((z + 1 + i % outer) % outer, (1 - y) if i < outer else y) for i in range(pop)]

    def weights(h, i):
        cols = pl.ds(pl.multiple_of(start_of(owners[i]) + h * piece, 128), piece)
        n = h * pop + i
        return (
            load(gate_w.at[:, cols], wg.at[n], wsem.at[2 * n]),
            load(up_w.at[:, cols], wu.at[n], wsem.at[2 * n + 1]),
        )

    steps = [(0, i) for i in range(outer + 2)] + [(1, 0), (1, 1), (0, 6), (0, 7)]
    steps += [(1, i) for i in range(2, pop)]
    loads = {at: weights(*at) for at in steps[:1]}
    for d in (lgof, luof, lprompts, lgin, luin):
        d.wait()
    for at in steps[1:]:
        loads[at] = weights(*at)
    ldif = load(dif_h, dif, msem.at[5])
    ldout = load(dout_h, dout, msem.at[6])
    ltar = load(targets_in, targets, msem.at[7])

    fbuild[0:rank, :] = gof[...].astype(F32)
    fbuild[rank : 2 * rank, :] = uof[...].astype(F32)
    fac[me] = fbuild[...].astype(BF)
    pl.semaphore_wait(barrier, 2 * pop - 1)

    pending = []
    S_FY, S_P, S_M, S_F, S_LOW, S_Y, S_Z, S_A, S_X, S_LG, S_H, S_L, S_R = (
        0, 1, 7, 13, 16, 24, 32, 38, 52, 53, 54, 55, 59)
    R_FY, R_FZ, R_FH, R_LOW, R_Y, R_Z, R_A, R_X, R_LG, R_H, R_L, R_R = (
        0, 1, 9, 13, 21, 29, 35, 51, 52, 53, 54, 62)

    def send(src, dst, sidx, ridx, dev):
        d = remote(src, dst, sidx, ridx, dev)
        d.start()
        pending.append(d)
        return d

    cut = ff // 256 * 128

    def chain(o, to, sidx, h):
        src = fac.at[spot(o, y), :, pl.ds(h * cut, cut if h == 0 else ff - cut)]
        return remote(src, src, sidx + 3 * h, R_FZ + 2 * o + h, {"pop": spot(to, y)})

    fy = send(fac.at[me], fac.at[me], S_FY, R_FY, {"pop": spot(z, 1 - y)})

    for h in range(2):

        @pl.when(z < outer - 1)
        def _(h=h):
            chain(z, z + 1, S_P, h).start()

        @pl.when(z > 0)
        def _(h=h):
            chain(z, z - 1, S_M, h).start()

    hrows = head.at[pl.ds(pl.multiple_of((me % part) * block, block), block)]
    holds = core == me // part

    x = prompts[...].astype(F32)
    normed[...] = (x * lax.rsqrt(jnp.mean(x * x, axis=-1, keepdims=True) + norm_eps)).astype(BF)

    scale = noise_scale / math.sqrt(width)
    lg = (scale * lax.dot_general(normed[...], gate_in[...], NT, preferred_element_type=F32)).astype(BF)
    lu = (scale * lax.dot_general(normed[...], up_in[...], NT, preferred_element_type=F32)).astype(BF)
    krow = lax.broadcasted_iota(jnp.int32, (rank, 128), 0)
    lane = lax.broadcasted_iota(jnp.int32, (rank, 128), 1)
    sel_g = (lane == me * 2 * rank + krow).astype(F32).astype(BF)
    sel_u = (lane == me * 2 * rank + rank + krow).astype(F32).astype(BF)
    low[me] = (
        jnp.dot(lg, sel_g, preferred_element_type=F32) + jnp.dot(lu, sel_u, preferred_element_type=F32)
    ).astype(BF)
    lcopies = [
        send(low.at[me], low.at[me], S_LOW + k, R_LOW + k, {"pop": (me + k) % pop}) for k in range(1, pop)
    ]

    xcols = pl.ds(pl.multiple_of(me * block, block), block)
    mine_n = normed[:, xcols]

    def relay_first(h):
        @pl.when(middle)
        def _():
            chain(z - 1, z, S_P, h).wait_recv()
            chain(z - 1, z + 1, S_P + 1, h).start()
            chain(z + 1, z, S_M, h).wait_recv()
            chain(z + 1, z - 1, S_M + 1, h).start()

    far = 3 * (2 - z)
    end = 3 * (z - 1)

    def relay_second(h):
        @pl.when(middle)
        def _():
            chain(far, z, S_P, h).wait_recv()
            chain(far, end, S_P + 2, h).start()

    order = [
        jnp.where(z == 0, 1, z - 1),
        jnp.where(z == outer - 1, 1, jnp.where(z == 2, 3, 2)),
        jnp.where(z < 2, 3, 0),
    ]

    def forward(n):
        o = order[n]

        @pl.when(jnp.logical_not(middle))
        def _():
            for h in range(2):
                chain(o, z, S_P, h).wait_recv()

        src = fac.at[spot(o, y)]
        send(src, src, S_F + n, R_FH + o, {"pop": spot(z, 1 - y)})

    ycopies = {}
    zcopies = {}
    dloads = []
    step = ff // 4
    across = {"pop": spot(z, 1 - y)}

    def product(h, i):
        loads[h, i][0].wait()
        loads[h, i][1].wait()
        return [jnp.dot(mine_n, w[h * pop + i], preferred_element_type=F32) for w in (wg, wu)]

    def part_out(h, i):
        got = product(h, i)
        n = h * outer + i
        for g in range(2):
            ysend[n, g] = got[g].astype(BF)
        ycopies[h, i] = send(ysend.at[n], yrecv.at[n], S_Y + n, R_Y + n, across)

    def part_own(h, i):
        got = product(h, i)
        for g in range(2):
            own[h * outer + i - outer, g] = got[g]

    def part_on(h, i):
        j = i - outer
        n = h * outer + j
        ycopies[h, j].wait_recv()
        if i == pop - 1:
            for g in range(2):
                own[n, g] = own[n, g] + yrecv[n, g].astype(F32)
            return
        n3 = h * (outer - 1) + j
        for g in range(2):
            zsend[n3, g] = (own[n, g] + yrecv[n, g].astype(F32)).astype(BF)
        zcopies[h, j] = send(
            zsend.at[n3], zrecv.at[n3], S_Z + n3, R_Z + n3, {"pop": spot((z + 1 + j) % outer, y)}
        )

    gaps = [(o - z + outer) % outer for o in order]

    def held(slot, h):
        return base.at[2 * slot + h]

    def gather(h):
        last = h * outer + outer - 1
        total = [own[last, 0], own[last, 1]]
        for j in range(outer - 1):
            zcopies[h, j].wait_recv()
            for g in range(2):
                total[g] = total[g] + zrecv[h * (outer - 1) + j, g].astype(F32)
        for g in range(2):
            base[h, g] = total[g].astype(BF)
        for n in range(outer - 1):
            send(
                held(0, h), held(gaps[n], h), S_A + 3 * h + n, R_A + 2 * gaps[n] + h, {"pop": spot(order[n], y)}
            )

    def near(n):
        return (outer - gaps[n]) % outer

    def arrive(n, h):
        k = near(n)
        remote(held(k, h), held(k, h), S_A, R_A + 2 * k + h, sib).wait_recv()
        send(held(k, h), held(outer + k, h), S_A + 8 + 3 * h + n, R_A + 2 * (outer + k) + h, across)

    def hand(h):
        send(held(0, h), held(outer, h), S_A + 6 + h, R_A + 2 * outer + h, across)

    for i in range(outer):
        part_out(0, i)
    part_own(0, 4)
    relay_first(0)
    part_own(0, 5)
    relay_first(1)
    part_out(1, 0)
    part_out(1, 1)
    part_on(0, 4)
    part_own(0, 6)
    part_on(0, 5)
    part_own(0, 7)
    part_on(0, 6)
    relay_second(0)
    part_out(1, 2)
    relay_second(1)
    part_out(1, 3)
    part_on(0, 7)
    for n in range(4):
        at = pl.ds(n * step, step)
        dloads.append(load(down_w.at[at], dw.at[at], dsem.at[n]))
    part_own(1, 4)
    part_own(1, 5)
    part_on(1, 4)
    forward(0)
    part_own(1, 6)
    part_on(1, 5)
    part_own(1, 7)
    forward(1)
    part_on(1, 6)
    gather(0)
    forward(2)
    hand(0)
    part_on(1, 7)

    @pl.when(holds)
    def _():
        remote(hrows, hblock, S_H, R_H, sib).start()
        pltpu.make_async_copy(hrows, hblock, msem.at[8]).start()

    ldout.wait()
    ldif.wait()
    ltar.wait()
    dall = jnp.concatenate([dout[m].astype(F32) for m in range(members)], axis=0)
    dcat[...] = jnp.concatenate([dall, dall], axis=0).astype(BF)
    acc[...] = jnp.zeros_like(acc)
    lowd[...] = jnp.zeros_like(lowd)
    for d in lcopies:
        d.wait_recv()
    coef = jnp.concatenate([low[m].astype(F32) for m in range(members)], axis=0)
    lane = lax.broadcasted_iota(jnp.int32, coef.shape, 1)
    row = lax.broadcasted_iota(jnp.int32, coef.shape, 0) % rows
    kk = 2 * rank * members
    gate_lane = lane % (2 * rank) < rank
    gate_lhs = jnp.where(lane < kk, jnp.where(gate_lane, coef, 0.0), (lane == kk + row).astype(F32))
    up_lhs = jnp.where(lane < kk, jnp.where(gate_lane, 0.0, coef), (lane == kk + rows + row).astype(F32))
    lhs[...] = jnp.concatenate([0.5 * gate_lhs, up_lhs], axis=0).astype(BF)

    gather(1)
    hand(1)
    arrive(0, 0)

    for d in dloads:
        d.wait()
    fy.wait_recv()
    for n in range(1, outer):
        o = (z + n) % outer
        src = fac.at[spot(o, 1 - y)]
        remote(src, src, S_F, R_FH + o, across).wait_recv()

    def expand(slot, c):
        start = start_of(c)
        skip = (c // (pop - 1)) * over

        pad = jnp.zeros((128 - kk - 2 * rows, tile), F32)
        for off in range(0, chunk, tile):
            at = pl.ds(pl.multiple_of(start + off, 128), tile)
            parts = [fac[m, :, at].astype(F32) for m in range(members)]
            low_off = off % piece
            parts += [
                base[2 * slot + off // piece, g, :, low_off : low_off + tile].astype(F32) for g in range(2)
            ]
            keep = (off >= skip).astype(F32)
            rhs = (jnp.concatenate(parts + [pad], axis=0) * keep).astype(BF)
            both = jnp.dot(lhs[...], rhs, preferred_element_type=F32)
            gate, up = both[:big], both[big:]
            hid[:, off : off + tile] = ((gate + gate * jnp.tanh(gate)) * up).astype(BF)
        h = hid[...]
        at = pl.ds(start, chunk)
        right = jnp.concatenate([dif[m, :, at].astype(F32) for m in range(members)], axis=0).astype(BF)
        lowd[...] += lax.dot_general(h, right, NT, preferred_element_type=F32)
        for off in range(0, block, tile):
            acc[:, off : off + tile] += jnp.dot(h, dw[at, off : off + tile], preferred_element_type=F32)

    expand(0, me)
    arrive(1, 0)
    arrive(0, 1)
    expand(near(0), spot(order[0], y))
    arrive(2, 0)
    arrive(1, 1)
    expand(near(1), spot(order[1], y))
    arrive(2, 1)
    expand(near(2), spot(order[2], y))
    for h in range(2):
        remote(held(outer, h), held(outer, h), S_A, R_A + 2 * outer + h, sib).wait_recv()
    expand(outer, spot(z, 1 - y))
    for n in range(outer - 1):
        k = outer + near(n)
        for h in range(2):
            remote(held(k, h), held(k, h), S_A, R_A + 2 * k + h, sib).wait_recv()
        expand(k, spot(order[n], 1 - y))

    mine = lax.broadcasted_iota(jnp.int32, lowd.shape, 0) // rows == lax.broadcasted_iota(jnp.int32, lowd.shape, 1) // rank
    lowm = jnp.where(mine, lowd[...] * (noise_scale / math.sqrt(total_ff)), 0.0)
    top = lowm.astype(BF).astype(F32)
    pair = jnp.concatenate([top, lowm - top], axis=1).astype(BF)
    acc[...] += jnp.dot(pair, dcat[...], preferred_element_type=F32)

    span = part * rows
    theirs = pl.ds(pl.multiple_of((1 - core) * span, span), span)
    ours = pl.ds(pl.multiple_of(core * span, span), span)
    xsend[...] = acc[theirs, :].astype(BF)
    xc = send(xsend, xrecv, S_X, R_X, sib)

    @pl.when(holds)
    def _():
        pltpu.make_async_copy(hrows, hblock, msem.at[8]).wait()

    @pl.when(jnp.logical_not(holds))
    def _():
        remote(hrows, hblock, S_H, R_H, sib).wait_recv()

    def logits_of(v):
        top = v.astype(BF)
        rest = (v - top.astype(F32)).astype(BF)
        got = jnp.dot(jnp.concatenate([top, rest], axis=0), hblock[...], preferred_element_type=F32)
        return got[:span] + got[span:]

    lgsend[...] = logits_of(acc[theirs, :])
    lc = send(lgsend, lgrecv, S_LG, R_LG, sib)
    pcols = prompts[:, xcols].astype(F32)
    here = acc[ours, :] + jnp.concatenate([pcols] * part, axis=0)
    lgts = logits_of(here)
    xc.wait_recv()
    out = here + xrecv[...].astype(F32)
    squares = out * out
    sq = squares[:, 0:128]
    for off in range(128, block, 128):
        sq = sq + squares[:, off : off + 128]
    top = sq.astype(BF).astype(F32)
    halves = jnp.concatenate([top, sq - top], axis=1).astype(BF)
    sums = lax.dot_general(jnp.ones((8, 256), BF), halves, NT, preferred_element_type=F32)
    for i in range(part):
        lsend[i, rows : rows + 8, :] = jnp.zeros((8, labels), F32)
        lsend[i, rows : rows + 8, 0:rows] = sums[:, i * rows : (i + 1) * rows]
    lc.wait_recv()
    for i in range(part):
        r = slice(i * rows, (i + 1) * rows)
        lsend[i, 0:rows, :] = lgts[r] + lgrecv[r, :]
    for i in range(part):
        m = core * part + i

        @pl.when(m != me)
        def _(i=i, m=m):
            remote(lsend.at[i], lrecv.at[me], S_L + i, R_L + me, {"pop": m}).start()

    @pl.when(holds)
    def _():
        tot = lsend[me % part]
        for k in range(1, pop):
            p = (me + k) % pop
            remote(lsend.at[0], lrecv.at[p], S_L, R_L + p, {"pop": p}).wait_recv()
            tot = tot + lrecv[p]
        eye = (
            lax.broadcasted_iota(jnp.int32, (rows, labels), 0) == lax.broadcasted_iota(jnp.int32, (rows, labels), 1)
        ).astype(F32)
        ssq = jnp.sum(eye * tot[rows : rows + 1, :], axis=1, keepdims=True)
        lgt = tot[0:rows, :] * lax.rsqrt(ssq * (1.0 / width) + norm_eps)
        spread_t = jnp.where(eye[:, :rows] > 0.0, jnp.broadcast_to(targets[...].astype(F32), (rows, rows)), 0.0)
        target = jnp.sum(spread_t, axis=1, keepdims=True).astype(jnp.int32)
        picks = target == lax.broadcasted_iota(jnp.int32, (rows, labels), 1)
        picked = jnp.sum(jnp.where(picks, lgt, 0.0), axis=1, keepdims=True)
        term = picked - jnp.log(jnp.sum(jnp.exp(lgt), axis=1, keepdims=True))
        rbuf[me] = jnp.sum(jnp.broadcast_to(term, (rows, 128)), axis=0, keepdims=True) * (1.0 / rows)
        for k in range(1, pop):
            for t in range(2):
                remote(
                    rbuf.at[me], rbuf.at[me], S_R + 2 * k + t, R_R + me, {"pop": (me + k) % pop, "tensor": t}
                ).start()
        remote(rbuf.at[me], rbuf.at[me], S_R, R_R + me, sib).start()

    for k in range(1, pop):
        p = (me + k) % pop
        remote(rbuf.at[p], rbuf.at[p], S_R, R_R + p, sib).wait_recv()

    @pl.when(jnp.logical_not(holds))
    def _():
        remote(rbuf.at[me], rbuf.at[me], S_R, R_R + me, sib).wait_recv()

    centre = sum(rbuf[m] for m in range(members)) * (1.0 / members)
    spread = sum((rbuf[m] - centre) * (rbuf[m] - centre) for m in range(members)) * (1.0 / members)
    inv = lax.rsqrt(spread + norm_eps)
    weighted_out[members * rank :, 0:128] = jnp.broadcast_to((rbuf[me] - centre) * inv, (8, 128))
    of = lax.broadcasted_iota(jnp.int32, (members * rank, 128), 0) // rank
    column = jnp.zeros((members * rank, 128), F32)
    for m in range(members):
        column = jnp.where(of == m, jnp.broadcast_to((rbuf[m] - centre) * inv, column.shape), column)
    for off in range(0, block, 128):
        at = slice(off, off + 128)
        weighted_out[0 : members * rank, at] = (dcat[0 : members * rank, at].astype(F32) * column).astype(BF).astype(F32)

    for d in pending:
        d.wait_send()

    for h in range(2):

        @pl.when(z < outer - 1)
        def _(h=h):
            chain(z, z + 1, S_P, h).wait_send()

        @pl.when(z > 0)
        def _(h=h):
            chain(z, z - 1, S_M, h).wait_send()

        @pl.when(middle)
        def _(h=h):
            chain(z - 1, z + 1, S_P + 1, h).wait_send()
            chain(z + 1, z - 1, S_M + 1, h).wait_send()
            chain(far, end, S_P + 2, h).wait_send()

    for i in range(part):
        m = core * part + i

        @pl.when(m != me)
        def _(i=i, m=m):
            remote(lsend.at[i], lrecv.at[me], S_L + i, R_L + me, {"pop": m}).wait_send()

    @pl.when(holds)
    def _():
        remote(hrows, hblock, S_H, R_H, sib).wait_send()
        for k in range(1, pop):
            for t in range(2):
                remote(
                    rbuf.at[me], rbuf.at[me], S_R + 2 * k + t, R_R + me, {"pop": (me + k) % pop, "tensor": t}
                ).wait_send()
        remote(rbuf.at[me], rbuf.at[me], S_R, R_R + me, sib).wait_send()


def update_kernel(norm, step, dif, weighted, out, score_out, left, right, sem):
    members, rank, ff = dif.shape
    width = weighted.shape[1]
    right[...] = weighted[0 : members * rank, :].astype(BF)
    copies = []
    blocks = [(start, min(step, ff - start)) for start in range(0, ff, step)]
    for n, (start, size) in enumerate(blocks):
        at = pl.ds(start, size)
        rows = jnp.concatenate([dif[m, :, at].astype(F32) for m in range(members)], axis=0).T.astype(BF)
        for c in range(0, width, 256):
            got = jnp.dot(rows, right[:, c : c + 256], preferred_element_type=F32)
            left[at, c : c + 256] = (got * norm).astype(BF)
        d = pltpu.make_async_copy(left.at[at], out.at[at], sem.at[n])
        d.start()
        copies.append(d)
    score_out[0] = weighted[members * rank, 0]
    for d in copies:
        d.wait()


def fast_body(
    pop, prompts, gate_weight, up_weight, down_weight, gate_in, gof, up_in, uof, dif, dout, head, targets
):
    rows, width = prompts.shape
    block, ff = gate_weight.shape
    members, _, rank = dif.shape
    outer = pop // 2
    chunk = -(-(ff // 128) // pop) * 128
    piece = chunk // 2
    labels = head.shape[1]
    swap = lambda v: jnp.swapaxes(v, 1, 2)
    dif_t, dout_t = swap(dif), swap(dout)
    vm = pl.BlockSpec(memory_space=pltpu.VMEM)
    hb = pl.BlockSpec(memory_space=pl.ANY)
    V = pltpu.VMEM
    D = pltpu.SemaphoreType.DMA
    big = members * rows
    weighted = pl.pallas_call(
        functools.partial(pair_kernel, pop, 2 * ff),
        out_shape=V((members * rank + 8, block), F32),
        in_specs=[hb] * 12,
        out_specs=vm,
        scratch_shapes=[
            V((rows, width), BF), V((rank, width), BF), V((rank, ff), BF), V((rank, width), BF), V((rank, ff), BF),
            V((members, rank, ff), BF), V((members, rank, block), BF), V((1, rows), jnp.int32),
            V((2 * pop, block, piece), BF), V((2 * pop, block, piece), BF), V((ff, block), BF),
            V((rows, width), BF), V((2 * rank, ff), F32), V((members, 2 * rank, ff), BF),
            V((members, rows, 128), BF), V((pop, 2, rows, piece), F32),
            V((pop, 2, rows, piece), BF), V((pop, 2, rows, piece), BF),
            V((pop - 2, 2, rows, piece), BF), V((pop - 2, 2, rows, piece), BF),
            V((2 * pop, 2, rows, piece), BF),
            V((2 * big, 128), BF), V((big, chunk), BF), V((big, block), F32), V((big, members * rank), F32),
            V((2 * members * rank, block), BF), V((big // 2, block), BF), V((big // 2, block), BF),
            V((block, labels), BF),
            V((big // 2, labels), F32), V((big // 2, labels), F32),
            V((members // 2, rows + 8, labels), F32), V((members, rows + 8, labels), F32),
            V((members, 1, 128), F32),
            D((4 * pop,)), D((4,)), D((9,)), D((75,)), D((70,)),
        ],
        compiler_params=pltpu.CompilerParams(
            collective_id=0, has_side_effects=True, vmem_limit_bytes=60 * 1000 * 1000
        ),
        name="pair",
    )(
        prompts, gate_weight, up_weight, down_weight, swap(gate_in)[0], swap(gof)[0], swap(up_in)[0],
        swap(uof)[0], dif_t, dout_t, head, targets[None],
    )
    step = 512
    update, scores = pl.pallas_call(
        functools.partial(update_kernel, 1.0 / math.sqrt(members * rank), step),
        out_shape=(jax.ShapeDtypeStruct((ff, block), BF), jax.ShapeDtypeStruct((1,), F32)),
        in_specs=[vm, vm],
        out_specs=(hb, pl.BlockSpec(memory_space=pltpu.SMEM)),
        scratch_shapes=[
            V((ff, block), BF), V((members * rank, block), BF), D((-(-ff // step),)),
        ],
        compiler_params=pltpu.CompilerParams(vmem_limit_bytes=40 * 1000 * 1000),
        name="update",
    )(dif_t, weighted)
    return update, scores


def solution(mesh):
    placed = (
        P("groups", None),
        P("pop", "tensor"),
        P("pop", "tensor"),
        P("tensor", "pop"),
        P(("groups", "pop"), None, None),
        P(("groups", "pop"), "tensor", None),
        P(("groups", "pop"), None, None),
        P(("groups", "pop"), "tensor", None),
        P("groups", "tensor", None),
        P("groups", "pop", None),
        P("tensor", None),
        P("groups"),
    )
    pop = mesh.shape["pop"]
    run = functools.partial(fast_body, pop) if pop == 8 and mesh.shape["tensor"] == 2 else body
    return jax.shard_map(
        run,
        mesh=mesh,
        in_specs=placed,
        out_specs=(P(("groups", "tensor"), "pop"), P(("groups", "pop"))),
        check_vma=False,
    )
```

```python
import functools
import math

import jax
import jax.numpy as jnp
from jax import lax
from jax.experimental import pallas as pl
from jax.experimental.pallas import tpu as pltpu
from jax.sharding import PartitionSpec as P

noise_scale = 0.2
norm_eps = 1e-06


def scaled_rows(values):
    return values * lax.rsqrt(jnp.mean(values * values, axis=-1, keepdims=True) + norm_eps)


def build_hidden(
    gate_baseline, up_baseline, lowrank_gate, lowrank_up, gate_output_factors, up_output_factors
):
    gate_activation = gate_baseline.astype(jnp.float32)[None] + jnp.einsum(
        "hvw,hpw->hvp", lowrank_gate, gate_output_factors, preferred_element_type=jnp.float32
    )
    upper_bound = up_baseline.astype(jnp.float32)[None] + jnp.einsum(
        "hvw,hpw->hvp", lowrank_up, up_output_factors, preferred_element_type=jnp.float32
    )
    return (jax.nn.silu(gate_activation) * upper_bound).astype(jnp.bfloat16)


def label_terms(logits, targets):
    labels = logits.shape[1]
    picks = targets[:, None] == jnp.arange(labels, dtype=jnp.int32)[None, :]
    picked = jnp.sum(jnp.where(picks, logits, 0.0), axis=1)
    return picked - jnp.log(jnp.sum(jnp.exp(logits), axis=1))


def body(
    prompts,
    gate_weight,
    up_weight,
    down_weight_matrix,
    gate_in,
    gate_output_factors,
    up_in,
    up_output_factors,
    down_input_factors,
    down_out,
    label_head,
    targets,
):
    member = lax.axis_index("pop")
    width = prompts.shape[1]
    in_block = gate_weight.shape[0]
    ffn_half = gate_output_factors.shape[1]
    total_ff = ffn_half * lax.axis_size("tensor")
    members = down_input_factors.shape[0]
    rank = down_input_factors.shape[2]
    prompt_f = prompts.astype(jnp.float32)
    normed = scaled_rows(prompt_f).astype(jnp.bfloat16)
    own_cols = lax.dynamic_slice_in_dim(normed, member * in_block, in_block, 1)
    part_gate = jnp.dot(own_cols, gate_weight, preferred_element_type=jnp.float32)
    part_up = jnp.dot(own_cols, up_weight, preferred_element_type=jnp.float32)
    total_gate, total_up = lax.psum((part_gate, part_up), "pop")
    gate_baseline = total_gate.astype(jnp.bfloat16)
    up_baseline = total_up.astype(jnp.bfloat16)
    in_scale = noise_scale / math.sqrt(width)
    lowrank_gate = (
        in_scale * jnp.einsum("rd,mdk->mrk", normed, gate_in, preferred_element_type=jnp.float32)
    ).astype(jnp.bfloat16)
    lowrank_up = (
        in_scale * jnp.einsum("rd,mdk->mrk", normed, up_in, preferred_element_type=jnp.float32)
    ).astype(jnp.bfloat16)
    down_scale = noise_scale / math.sqrt(total_ff)
    hidden_state = build_hidden(
        gate_baseline, up_baseline, lowrank_gate, lowrank_up, gate_output_factors, up_output_factors
    )
    hidden_portion = lax.all_gather(hidden_state, "pop", axis=0, tiled=True)
    out_piece = down_out.astype(jnp.float32)
    entry_point = jnp.einsum(
        "uaz,zh->uah", hidden_portion, down_weight_matrix, preferred_element_type=jnp.float32
    )
    low_part = down_scale * jnp.einsum(
        "lpq,lqb->lpb", hidden_portion, down_input_factors, preferred_element_type=jnp.float32
    )
    partial_rows = entry_point + jnp.einsum(
        "mrk,mdk->mrd", low_part, out_piece, precision=lax.Precision.HIGHEST
    )
    rows_here = lax.all_to_all(partial_rows, "pop", split_axis=0, concat_axis=2, tiled=True)
    summed = lax.psum(rows_here, "tensor")[0]
    output = prompt_f + summed
    final = scaled_rows(output).astype(jnp.bfloat16)
    half = label_head.shape[0]
    own_half = lax.dynamic_slice_in_dim(final, lax.axis_index("tensor") * half, half, 1)
    logits = lax.psum(jnp.dot(own_half, label_head, preferred_element_type=jnp.float32), "tensor")
    reward = jnp.mean(label_terms(logits, targets))
    rewards = lax.all_gather(reward.reshape(1), "pop", axis=0, tiled=True)
    centre = jnp.mean(rewards)
    spread = jnp.mean((rewards - centre) * (rewards - centre))
    scores = (rewards - centre) * lax.rsqrt(spread + norm_eps)
    weighted = (scores[:, None, None] * down_out.astype(jnp.float32)).astype(jnp.bfloat16)
    update = jnp.einsum(
        "mfk,mdk->fd", down_input_factors, weighted, preferred_element_type=jnp.float32
    ) * (1.0 / math.sqrt(members * rank))
    own_score = lax.dynamic_slice_in_dim(scores, member, 1, 0)
    return (update.astype(jnp.bfloat16), own_score)


BF = jnp.bfloat16
F32 = jnp.float32
HI = lax.Precision.HIGHEST
NT = (((1,), (1,)), ((), ()))
TN = (((0,), (0,)), ((), ()))


def pair_kernel(
    pop, total_ff,
    prompts_in, gate_w, up_w, down_w, gate_in_h, gof_h, up_in_h, uof_h, dif_h, dout_h, head, targets_in,
    weighted_out,
    prompts, gate_in, gof, up_in, uof, dif, dout, targets,
    wgu, dw, normed, fbuild, fac, low, own, ysend, yrecv, zsend, zrecv, base,
    lhs, hid, acc, lowd, dcat, xsend, xrecv, hblock,
    lgsend, lgrecv, lsend, lrecv, rbuf,
    wsem, dsem, msem, ssem, rsem,
):
    rows, width = prompts.shape
    block, ff = gate_w.shape
    outer = pop // 2
    piece = wgu.shape[3]
    chunk = 2 * piece
    members = pop
    rank = gof.shape[0]
    part = members // 2
    big = members * rows
    labels = head.shape[1]
    over = pop * chunk - ff
    tile = 256
    me = lax.axis_index("pop")
    core = lax.axis_index("tensor")
    z = me // 2
    y = me % 2
    sib = {"tensor": 1 - core}
    middle = (z >= 1) & (z <= outer - 2)

    def spot(zz, yy):
        return zz * 2 + yy

    def start_of(c):
        return pl.multiple_of(c * chunk - (c // (pop - 1)) * over, 128)

    def remote(src, dst, sidx, ridx, dev):
        return pltpu.make_async_remote_copy(
            src_ref=src, dst_ref=dst, send_sem=ssem.at[sidx], recv_sem=rsem.at[ridx],
            device_id=dev, device_id_type=pl.DeviceIdType.MESH,
        )

    barrier = pltpu.get_barrier_semaphore()
    for k in range(1, pop):
        for t in range(2):
            pl.semaphore_signal(
                barrier, inc=1, device_id={"pop": (me + k) % pop, "tensor": t}, device_id_type=pl.DeviceIdType.MESH
            )
    pl.semaphore_signal(barrier, inc=1, device_id=sib, device_id_type=pl.DeviceIdType.MESH)

    def load(src, dst, sem):
        d = pltpu.make_async_copy(src, dst, sem)
        d.start()
        return d

    lgof = load(gof_h, gof, msem.at[0])
    luof = load(uof_h, uof, msem.at[1])
    lprompts = load(prompts_in, prompts, msem.at[2])
    lgin = load(gate_in_h, gate_in, msem.at[3])
    luin = load(up_in_h, up_in, msem.at[4])
    owners = [spot((z + 1 + i % outer) % outer, (1 - y) if i < outer else y) for i in range(pop)]

    def weights(h, i):
        cols = pl.ds(pl.multiple_of(start_of(owners[i]) + h * piece, 128), piece)
        n = h * pop + i
        load(gate_w.at[:, cols], wgu.at[n, 0], wsem.at[n])
        load(up_w.at[:, cols], wgu.at[n, 1], wsem.at[n])

    steps = [(0, i) for i in range(outer + 2)] + [(1, 0), (1, 1), (0, 6), (0, 7)]
    steps += [(1, i) for i in range(2, pop)]
    weights(*steps[0])
    for d in (lgof, luof, lprompts, lgin, luin):
        d.wait()
    for at in steps[1:]:
        weights(*at)
    ldif = load(dif_h, dif, msem.at[5])
    ldout = load(dout_h, dout, msem.at[6])
    ltar = load(targets_in, targets, msem.at[7])

    fbuild[0:rank, :] = gof[...].astype(F32)
    fbuild[rank : 2 * rank, :] = uof[...].astype(F32)
    fac[me] = fbuild[...].astype(BF)
    pl.semaphore_wait(barrier, 2 * pop - 1)

    S_FAC, S_CH, S_LOW, S_Y, S_Z, S_A, S_X, S_LG, S_H, S_L, S_R = range(11)
    R_FAC, R_FZ, R_LOW, R_Y, R_Z, R_A, R_B, R_X, R_LG, R_H, R_L, R_R = 0, 1, 9, 10, 18, 20, 28, 32, 33, 34, 35, 36

    def send(src, dst, sidx, ridx, dev):
        d = remote(src, dst, sidx, ridx, dev)
        d.start()
        return d

    def sent(ref, sidx):
        remote(ref, ref, sidx, R_FAC, sib).wait_send()

    def came(ref, ridx):
        remote(ref, ref, S_FAC, ridx, sib).wait_recv()

    cut = ff // 256 * 128

    def chain(o, to, h):
        src = fac.at[spot(o, y), :, pl.ds(h * cut, cut if h == 0 else ff - cut)]
        return remote(src, src, S_CH, R_FZ + 2 * o + h, {"pop": spot(to, y)})

    send(fac.at[me], fac.at[me], S_FAC, R_FAC, {"pop": spot(z, 1 - y)})

    for h in range(2):

        @pl.when(z < outer - 1)
        def _(h=h):
            chain(z, z + 1, h).start()

        @pl.when(z > 0)
        def _(h=h):
            chain(z, z - 1, h).start()

    hrows = head.at[pl.ds(pl.multiple_of((me % part) * block, block), block)]
    holds = core == me // part

    x = prompts[...].astype(F32)
    normed[...] = (x * lax.rsqrt(jnp.mean(x * x, axis=-1, keepdims=True) + norm_eps)).astype(BF)

    scale = noise_scale / math.sqrt(width)
    lg = (scale * lax.dot_general(normed[...], gate_in[...], NT, preferred_element_type=F32)).astype(BF)
    lu = (scale * lax.dot_general(normed[...], up_in[...], NT, preferred_element_type=F32)).astype(BF)
    krow = lax.broadcasted_iota(jnp.int32, (rank, 128), 0)
    lane = lax.broadcasted_iota(jnp.int32, (rank, 128), 1)
    sel_g = (lane == me * 2 * rank + krow).astype(F32).astype(BF)
    sel_u = (lane == me * 2 * rank + rank + krow).astype(F32).astype(BF)
    low[me] = (
        jnp.dot(lg, sel_g, preferred_element_type=F32) + jnp.dot(lu, sel_u, preferred_element_type=F32)
    ).astype(BF)
    for k in range(1, pop):
        send(low.at[me], low.at[me], S_LOW, R_LOW, {"pop": (me + k) % pop})

    xcols = pl.ds(pl.multiple_of(me * block, block), block)
    mine_n = normed[:, xcols]

    def relay_first(h):
        @pl.when(middle)
        def _():
            chain(z - 1, z, h).wait_recv()
            chain(z - 1, z + 1, h).start()
            chain(z + 1, z, h).wait_recv()
            chain(z + 1, z - 1, h).start()

    far = 3 * (2 - z)
    end = 3 * (z - 1)

    def relay_second(h):
        @pl.when(middle)
        def _():
            chain(far, z, h).wait_recv()
            chain(far, end, h).start()

    order = [
        jnp.where(z == 0, 1, z - 1),
        jnp.where(z == outer - 1, 1, jnp.where(z == 2, 3, 2)),
        jnp.where(z < 2, 3, 0),
    ]

    def forward(n):
        o = order[n]

        @pl.when(jnp.logical_not(middle))
        def _():
            for h in range(2):
                chain(o, z, h).wait_recv()

        src = fac.at[spot(o, y)]
        send(src, src, S_FAC, R_FAC, {"pop": spot(z, 1 - y)})

    ycopies = {}
    step = ff // 4
    across = {"pop": spot(z, 1 - y)}

    def product(h, i):
        n = h * pop + i
        pltpu.make_async_copy(wgu.at[n], wgu.at[n], wsem.at[n]).wait()
        return [jnp.dot(mine_n, wgu[n, g], preferred_element_type=F32) for g in range(2)]

    def part_out(h, i):
        got = product(h, i)
        n = h * outer + i
        for g in range(2):
            ysend[n, g] = got[g].astype(BF)
        ycopies[h, i] = send(ysend.at[n], yrecv.at[n], S_Y, R_Y + n, across)

    def part_own(h, i):
        got = product(h, i)
        for g in range(2):
            own[h * outer + i - outer, g] = got[g]

    def part_on(h, i):
        j = i - outer
        n = h * outer + j
        ycopies[h, j].wait_recv()
        if i == pop - 1:
            for g in range(2):
                own[n, g] = own[n, g] + yrecv[n, g].astype(F32)
            return
        n3 = h * (outer - 1) + j
        for g in range(2):
            zsend[n3, g] = (own[n, g] + yrecv[n, g].astype(F32)).astype(BF)
        send(
            zsend.at[n3], zrecv.at[n3], S_Z, R_Z + h, {"pop": spot((z + 1 + j) % outer, y)}
        )

    gaps = [(o - z + outer) % outer for o in order]

    def held(slot, h):
        return base.at[2 * slot + h]

    def gather(h):
        last = h * outer + outer - 1
        total = [own[last, 0], own[last, 1]]
        came(zrecv.at[(outer - 1) * h : (outer - 1) * (h + 1)], R_Z + h)
        for j in range(outer - 1):
            for g in range(2):
                total[g] = total[g] + zrecv[h * (outer - 1) + j, g].astype(F32)
        for g in range(2):
            base[h, g] = total[g].astype(BF)
        for n in range(outer - 1):
            send(
                held(0, h), held(gaps[n], h), S_A, R_A + 2 * gaps[n] + h, {"pop": spot(order[n], y)}
            )

    def near(n):
        return (outer - gaps[n]) % outer

    def arrive(n, h):
        k = near(n)
        came(held(k, h), R_A + 2 * k + h)
        send(held(k, h), held(outer + k, h), S_A, R_B + k, across)

    def hand(h):
        send(held(0, h), held(outer, h), S_A, R_B, across)

    for i in range(outer):
        part_out(0, i)
    part_own(0, 4)
    relay_first(0)
    part_own(0, 5)
    relay_first(1)
    part_out(1, 0)
    part_out(1, 1)
    part_on(0, 4)
    part_own(0, 6)
    part_on(0, 5)
    part_own(0, 7)
    part_on(0, 6)
    relay_second(0)
    part_out(1, 2)
    relay_second(1)
    part_out(1, 3)
    part_on(0, 7)
    for n in range(4):
        at = pl.ds(n * step, step)
        load(down_w.at[at], dw.at[at], dsem.at[0])
    part_own(1, 4)
    part_own(1, 5)
    part_on(1, 4)
    forward(0)
    part_own(1, 6)
    part_on(1, 5)
    part_own(1, 7)
    forward(1)
    part_on(1, 6)
    gather(0)
    forward(2)
    hand(0)
    part_on(1, 7)

    @pl.when(holds)
    def _():
        remote(hrows, hblock, S_H, R_H, sib).start()
        pltpu.make_async_copy(hrows, hblock, msem.at[8]).start()

    ldout.wait()
    ldif.wait()
    ltar.wait()
    dall = jnp.concatenate([dout[m].astype(F32) for m in range(members)], axis=0)
    dcat[...] = jnp.concatenate([dall, dall], axis=0).astype(BF)
    acc[...] = jnp.zeros_like(acc)
    lowd[...] = jnp.zeros_like(lowd)
    came(low.at[1:], R_LOW)
    coef = jnp.concatenate([low[m].astype(F32) for m in range(members)], axis=0)
    lane = lax.broadcasted_iota(jnp.int32, coef.shape, 1)
    row = lax.broadcasted_iota(jnp.int32, coef.shape, 0) % rows
    kk = 2 * rank * members
    gate_lane = lane % (2 * rank) < rank
    gate_lhs = jnp.where(lane < kk, jnp.where(gate_lane, coef, 0.0), (lane == kk + row).astype(F32))
    up_lhs = jnp.where(lane < kk, jnp.where(gate_lane, 0.0, coef), (lane == kk + rows + row).astype(F32))
    lhs[...] = jnp.concatenate([0.5 * gate_lhs, up_lhs], axis=0).astype(BF)

    gather(1)
    hand(1)
    arrive(0, 0)

    pltpu.make_async_copy(down_w, dw, dsem.at[0]).wait()
    came(fac.at[0:outer], R_FAC)

    def expand(slot, c):
        start = start_of(c)
        skip = (c // (pop - 1)) * over

        pad = jnp.zeros((128 - kk - 2 * rows, tile), F32)
        for off in range(0, chunk, tile):
            at = pl.ds(pl.multiple_of(start + off, 128), tile)
            parts = [fac[m, :, at].astype(F32) for m in range(members)]
            low_off = off % piece
            parts += [
                base[2 * slot + off // piece, g, :, low_off : low_off + tile].astype(F32) for g in range(2)
            ]
            keep = (off >= skip).astype(F32)
            rhs = (jnp.concatenate(parts + [pad], axis=0) * keep).astype(BF)
            both = jnp.dot(lhs[...], rhs, preferred_element_type=F32)
            gate, up = both[:big], both[big:]
            hid[:, off : off + tile] = ((gate + gate * jnp.tanh(gate)) * up).astype(BF)
        h = hid[...]
        at = pl.ds(start, chunk)
        right = jnp.concatenate([dif[m, :, at].astype(F32) for m in range(members)], axis=0).astype(BF)
        lowd[...] += lax.dot_general(h, right, NT, preferred_element_type=F32)
        for off in range(0, block, tile):
            acc[:, off : off + tile] += jnp.dot(h, dw[at, off : off + tile], preferred_element_type=F32)

    expand(0, me)
    arrive(1, 0)
    arrive(0, 1)
    expand(near(0), spot(order[0], y))
    arrive(2, 0)
    arrive(1, 1)
    expand(near(1), spot(order[1], y))
    arrive(2, 1)
    expand(near(2), spot(order[2], y))
    came(base.at[2 * outer : 2 * outer + 2], R_B)
    expand(outer, spot(z, 1 - y))
    for n in range(outer - 1):
        k = outer + near(n)
        came(base.at[pl.ds(2 * k, 2)], R_B + near(n))
        expand(k, spot(order[n], 1 - y))

    mine = lax.broadcasted_iota(jnp.int32, lowd.shape, 0) // rows == lax.broadcasted_iota(jnp.int32, lowd.shape, 1) // rank
    lowm = jnp.where(mine, lowd[...] * (noise_scale / math.sqrt(total_ff)), 0.0)
    top = lowm.astype(BF).astype(F32)
    pair = jnp.concatenate([top, lowm - top], axis=1).astype(BF)
    acc[...] += jnp.dot(pair, dcat[...], preferred_element_type=F32)

    span = part * rows
    theirs = pl.ds(pl.multiple_of((1 - core) * span, span), span)
    ours = pl.ds(pl.multiple_of(core * span, span), span)
    xsend[...] = acc[theirs, :].astype(BF)
    xc = send(xsend, xrecv, S_X, R_X, sib)

    @pl.when(holds)
    def _():
        pltpu.make_async_copy(hrows, hblock, msem.at[8]).wait()

    @pl.when(jnp.logical_not(holds))
    def _():
        remote(hrows, hblock, S_H, R_H, sib).wait_recv()

    def logits_of(v):
        top = v.astype(BF)
        rest = (v - top.astype(F32)).astype(BF)
        got = jnp.dot(jnp.concatenate([top, rest], axis=0), hblock[...], preferred_element_type=F32)
        return got[:span] + got[span:]

    lgsend[...] = logits_of(acc[theirs, :])
    lc = send(lgsend, lgrecv, S_LG, R_LG, sib)
    pcols = prompts[:, xcols].astype(F32)
    here = acc[ours, :] + jnp.concatenate([pcols] * part, axis=0)
    lgts = logits_of(here)
    xc.wait_recv()
    out = here + xrecv[...].astype(F32)
    squares = out * out
    sq = squares[:, 0:128]
    for off in range(128, block, 128):
        sq = sq + squares[:, off : off + 128]
    top = sq.astype(BF).astype(F32)
    halves = jnp.concatenate([top, sq - top], axis=1).astype(BF)
    sums = lax.dot_general(jnp.ones((8, 256), BF), halves, NT, preferred_element_type=F32)
    for i in range(part):
        lsend[i, rows : rows + 8, :] = jnp.zeros((8, labels), F32)
        lsend[i, rows : rows + 8, 0:rows] = sums[:, i * rows : (i + 1) * rows]
    lc.wait_recv()
    for i in range(part):
        r = slice(i * rows, (i + 1) * rows)
        lsend[i, 0:rows, :] = lgts[r] + lgrecv[r, :]
    for i in range(part):
        m = core * part + i

        @pl.when(m != me)
        def _(i=i, m=m):
            remote(lsend.at[i], lrecv.at[me], S_L, R_L, {"pop": m}).start()

    @pl.when(holds)
    def _():
        came(lrecv.at[1:], R_L)
        tot = lsend[me % part]
        for k in range(1, pop):
            tot = tot + lrecv[(me + k) % pop]
        eye = (
            lax.broadcasted_iota(jnp.int32, (rows, labels), 0) == lax.broadcasted_iota(jnp.int32, (rows, labels), 1)
        ).astype(F32)
        ssq = jnp.sum(eye * tot[rows : rows + 1, :], axis=1, keepdims=True)
        lgt = tot[0:rows, :] * lax.rsqrt(ssq * (1.0 / width) + norm_eps)
        spread_t = jnp.where(eye[:, :rows] > 0.0, jnp.broadcast_to(targets[...].astype(F32), (rows, rows)), 0.0)
        target = jnp.sum(spread_t, axis=1, keepdims=True).astype(jnp.int32)
        picks = target == lax.broadcasted_iota(jnp.int32, (rows, labels), 1)
        picked = jnp.sum(jnp.where(picks, lgt, 0.0), axis=1, keepdims=True)
        term = picked - jnp.log(jnp.sum(jnp.exp(lgt), axis=1, keepdims=True))
        rbuf[me] = jnp.sum(jnp.broadcast_to(term, (rows, 128)), axis=0, keepdims=True) * (1.0 / rows)
        for k in range(1, pop):
            for t in range(2):
                send(rbuf.at[me], rbuf.at[me], S_R, R_R, {"pop": (me + k) % pop, "tensor": t})
        send(rbuf.at[me], rbuf.at[me], S_R, R_R, sib)
        came(rbuf.at[1:members], R_R)

    @pl.when(jnp.logical_not(holds))
    def _():
        came(rbuf.at[0:members], R_R)

    centre = sum(rbuf[m] for m in range(members)) * (1.0 / members)
    spread = sum((rbuf[m] - centre) * (rbuf[m] - centre) for m in range(members)) * (1.0 / members)
    inv = lax.rsqrt(spread + norm_eps)
    weighted_out[members * rank :, 0:128] = jnp.broadcast_to((rbuf[me] - centre) * inv, (8, 128))
    of = lax.broadcasted_iota(jnp.int32, (members * rank, 128), 0) // rank
    column = jnp.zeros((members * rank, 128), F32)
    for m in range(members):
        column = jnp.where(of == m, jnp.broadcast_to((rbuf[m] - centre) * inv, column.shape), column)
    for off in range(0, block, 128):
        at = slice(off, off + 128)
        weighted_out[0 : members * rank, at] = (dcat[0 : members * rank, at].astype(F32) * column).astype(BF).astype(F32)

    sent(fac.at[0:outer], S_FAC)
    sent(low.at[1:], S_LOW)
    sent(ysend, S_Y)
    sent(zsend, S_Z)
    sent(base.at[0 : 4 * outer - 2], S_A)
    sent(xsend, S_X)
    sent(lgsend, S_LG)

    @pl.when(middle)
    def _():
        sent(fac.at[0 : outer + 1], S_CH)

    @pl.when(jnp.logical_not(middle))
    def _():
        sent(fac.at[0], S_CH)

    @pl.when(holds)
    def _():
        sent(hblock, S_H)
        sent(lsend.at[1:], S_L)
        sent(rbuf.at[1:], S_R)

    @pl.when(jnp.logical_not(holds))
    def _():
        sent(lsend, S_L)


def update_kernel(norm, step, dif, weighted, out, score_out, left, right, sem):
    members, rank, ff = dif.shape
    width = weighted.shape[1]
    right[...] = weighted[0 : members * rank, :].astype(BF)
    copies = []
    blocks = [(start, min(step, ff - start)) for start in range(0, ff, step)]
    for n, (start, size) in enumerate(blocks):
        at = pl.ds(start, size)
        rows = jnp.concatenate([dif[m, :, at].astype(F32) for m in range(members)], axis=0).T.astype(BF)
        for c in range(0, width, 256):
            got = jnp.dot(rows, right[:, c : c + 256], preferred_element_type=F32)
            left[at, c : c + 256] = (got * norm).astype(BF)
        d = pltpu.make_async_copy(left.at[at], out.at[at], sem.at[n])
        d.start()
        copies.append(d)
    score_out[0] = weighted[members * rank, 0]
    for d in copies:
        d.wait()


def fast_body(
    pop, prompts, gate_weight, up_weight, down_weight, gate_in, gof, up_in, uof, dif, dout, head, targets
):
    rows, width = prompts.shape
    block, ff = gate_weight.shape
    members, _, rank = dif.shape
    outer = pop // 2
    chunk = -(-(ff // 128) // pop) * 128
    piece = chunk // 2
    labels = head.shape[1]
    swap = lambda v: jnp.swapaxes(v, 1, 2)
    dif_t, dout_t = swap(dif), swap(dout)
    vm = pl.BlockSpec(memory_space=pltpu.VMEM)
    hb = pl.BlockSpec(memory_space=pl.ANY)
    V = pltpu.VMEM
    D = pltpu.SemaphoreType.DMA
    big = members * rows
    weighted = pl.pallas_call(
        functools.partial(pair_kernel, pop, 2 * ff),
        out_shape=V((members * rank + 8, block), F32),
        in_specs=[hb] * 12,
        out_specs=vm,
        scratch_shapes=[
            V((rows, width), BF), V((rank, width), BF), V((rank, ff), BF), V((rank, width), BF), V((rank, ff), BF),
            V((members, rank, ff), BF), V((members, rank, block), BF), V((1, rows), jnp.int32),
            V((2 * pop, 2, block, piece), BF), V((ff, block), BF),
            V((rows, width), BF), V((2 * rank, ff), F32), V((members, 2 * rank, ff), BF),
            V((members, rows, 128), BF), V((pop, 2, rows, piece), F32),
            V((pop, 2, rows, piece), BF), V((pop, 2, rows, piece), BF),
            V((pop - 2, 2, rows, piece), BF), V((pop - 2, 2, rows, piece), BF),
            V((2 * pop, 2, rows, piece), BF),
            V((2 * big, 128), BF), V((big, chunk), BF), V((big, block), F32), V((big, members * rank), F32),
            V((2 * members * rank, block), BF), V((big // 2, block), BF), V((big // 2, block), BF),
            V((block, labels), BF),
            V((big // 2, labels), F32), V((big // 2, labels), F32),
            V((members // 2, rows + 8, labels), F32), V((members, rows + 8, labels), F32),
            V((2 * members, 1, 128), F32),
            D((2 * pop,)), D((1,)), D((9,)), D((11,)), D((37,)),
        ],
        compiler_params=pltpu.CompilerParams(
            collective_id=0, has_side_effects=True, vmem_limit_bytes=60 * 1000 * 1000
        ),
        name="pair",
    )(
        prompts, gate_weight, up_weight, down_weight, swap(gate_in)[0], swap(gof)[0], swap(up_in)[0],
        swap(uof)[0], dif_t, dout_t, head, targets[None],
    )
    step = 512
    update, scores = pl.pallas_call(
        functools.partial(update_kernel, 1.0 / math.sqrt(members * rank), step),
        out_shape=(jax.ShapeDtypeStruct((ff, block), BF), jax.ShapeDtypeStruct((1,), F32)),
        in_specs=[vm, vm],
        out_specs=(hb, pl.BlockSpec(memory_space=pltpu.SMEM)),
        scratch_shapes=[
            V((ff, block), BF), V((members * rank, block), BF), D((-(-ff // step),)),
        ],
        compiler_params=pltpu.CompilerParams(vmem_limit_bytes=40 * 1000 * 1000),
        name="update",
    )(dif_t, weighted)
    return update, scores


def solution(mesh):
    placed = (
        P("groups", None),
        P("pop", "tensor"),
        P("pop", "tensor"),
        P("tensor", "pop"),
        P(("groups", "pop"), None, None),
        P(("groups", "pop"), "tensor", None),
        P(("groups", "pop"), None, None),
        P(("groups", "pop"), "tensor", None),
        P("groups", "tensor", None),
        P("groups", "pop", None),
        P("tensor", None),
        P("groups"),
    )
    pop = mesh.shape["pop"]
    run = functools.partial(fast_body, pop) if pop == 8 and mesh.shape["tensor"] == 2 else body
    return jax.shard_map(
        run,
        mesh=mesh,
        in_specs=placed,
        out_specs=(P(("groups", "tensor"), "pop"), P(("groups", "pop"))),
        check_vma=False,
    )
```

```python
import functools
import math

import jax
import jax.numpy as jnp
from jax import lax
from jax.experimental import pallas as pl
from jax.experimental.pallas import tpu as pltpu
from jax.sharding import PartitionSpec as P

noise_scale = 0.2
norm_eps = 1e-06


def scaled_rows(values):
    return values * lax.rsqrt(jnp.mean(values * values, axis=-1, keepdims=True) + norm_eps)


def build_hidden(
    gate_baseline, up_baseline, lowrank_gate, lowrank_up, gate_output_factors, up_output_factors
):
    gate_activation = gate_baseline.astype(jnp.float32)[None] + jnp.einsum(
        "hvw,hpw->hvp", lowrank_gate, gate_output_factors, preferred_element_type=jnp.float32
    )
    upper_bound = up_baseline.astype(jnp.float32)[None] + jnp.einsum(
        "hvw,hpw->hvp", lowrank_up, up_output_factors, preferred_element_type=jnp.float32
    )
    return (jax.nn.silu(gate_activation) * upper_bound).astype(jnp.bfloat16)


def label_terms(logits, targets):
    labels = logits.shape[1]
    picks = targets[:, None] == jnp.arange(labels, dtype=jnp.int32)[None, :]
    picked = jnp.sum(jnp.where(picks, logits, 0.0), axis=1)
    return picked - jnp.log(jnp.sum(jnp.exp(logits), axis=1))


def body(
    prompts,
    gate_weight,
    up_weight,
    down_weight_matrix,
    gate_in,
    gate_output_factors,
    up_in,
    up_output_factors,
    down_input_factors,
    down_out,
    label_head,
    targets,
):
    member = lax.axis_index("pop")
    width = prompts.shape[1]
    in_block = gate_weight.shape[0]
    ffn_half = gate_output_factors.shape[1]
    total_ff = ffn_half * lax.axis_size("tensor")
    members = down_input_factors.shape[0]
    rank = down_input_factors.shape[2]
    prompt_f = prompts.astype(jnp.float32)
    normed = scaled_rows(prompt_f).astype(jnp.bfloat16)
    own_cols = lax.dynamic_slice_in_dim(normed, member * in_block, in_block, 1)
    part_gate = jnp.dot(own_cols, gate_weight, preferred_element_type=jnp.float32)
    part_up = jnp.dot(own_cols, up_weight, preferred_element_type=jnp.float32)
    total_gate, total_up = lax.psum((part_gate, part_up), "pop")
    gate_baseline = total_gate.astype(jnp.bfloat16)
    up_baseline = total_up.astype(jnp.bfloat16)
    in_scale = noise_scale / math.sqrt(width)
    lowrank_gate = (
        in_scale * jnp.einsum("rd,mdk->mrk", normed, gate_in, preferred_element_type=jnp.float32)
    ).astype(jnp.bfloat16)
    lowrank_up = (
        in_scale * jnp.einsum("rd,mdk->mrk", normed, up_in, preferred_element_type=jnp.float32)
    ).astype(jnp.bfloat16)
    down_scale = noise_scale / math.sqrt(total_ff)
    hidden_state = build_hidden(
        gate_baseline, up_baseline, lowrank_gate, lowrank_up, gate_output_factors, up_output_factors
    )
    hidden_portion = lax.all_gather(hidden_state, "pop", axis=0, tiled=True)
    out_piece = down_out.astype(jnp.float32)
    entry_point = jnp.einsum(
        "uaz,zh->uah", hidden_portion, down_weight_matrix, preferred_element_type=jnp.float32
    )
    low_part = down_scale * jnp.einsum(
        "lpq,lqb->lpb", hidden_portion, down_input_factors, preferred_element_type=jnp.float32
    )
    partial_rows = entry_point + jnp.einsum(
        "mrk,mdk->mrd", low_part, out_piece, precision=lax.Precision.HIGHEST
    )
    rows_here = lax.all_to_all(partial_rows, "pop", split_axis=0, concat_axis=2, tiled=True)
    summed = lax.psum(rows_here, "tensor")[0]
    output = prompt_f + summed
    final = scaled_rows(output).astype(jnp.bfloat16)
    half = label_head.shape[0]
    own_half = lax.dynamic_slice_in_dim(final, lax.axis_index("tensor") * half, half, 1)
    logits = lax.psum(jnp.dot(own_half, label_head, preferred_element_type=jnp.float32), "tensor")
    reward = jnp.mean(label_terms(logits, targets))
    rewards = lax.all_gather(reward.reshape(1), "pop", axis=0, tiled=True)
    centre = jnp.mean(rewards)
    spread = jnp.mean((rewards - centre) * (rewards - centre))
    scores = (rewards - centre) * lax.rsqrt(spread + norm_eps)
    weighted = (scores[:, None, None] * down_out.astype(jnp.float32)).astype(jnp.bfloat16)
    update = jnp.einsum(
        "mfk,mdk->fd", down_input_factors, weighted, preferred_element_type=jnp.float32
    ) * (1.0 / math.sqrt(members * rank))
    own_score = lax.dynamic_slice_in_dim(scores, member, 1, 0)
    return (update.astype(jnp.bfloat16), own_score)


BF = jnp.bfloat16
F32 = jnp.float32
HI = lax.Precision.HIGHEST
NT = (((1,), (1,)), ((), ()))
TN = (((0,), (0,)), ((), ()))


def pair_kernel(
    pop, total_ff,
    prompts_in, gate_w, up_w, down_w, gate_in_h, gof_h, up_in_h, uof_h, dif_h, dout_h, head, targets_in,
    weighted_out,
    prompts, gate_in, gof, up_in, uof, dif, dout, targets,
    wgu, dw, normed, fbuild, fac, low, own, ysend, yrecv, zsend, zrecv, base,
    lhs, hid, acc, lowd, dcat, xsend, xrecv, hblock,
    lgsend, lgrecv, lsend, lrecv, rbuf,
    wsem, dsem, msem, ssem, rsem,
):
    rows, width = prompts.shape
    block, ff = gate_w.shape
    outer = pop // 2
    piece = wgu.shape[3]
    chunk = 2 * piece
    members = pop
    rank = gof.shape[0]
    part = members // 2
    big = members * rows
    labels = head.shape[1]
    over = pop * chunk - ff
    tile = 256
    me = lax.axis_index("pop")
    core = lax.axis_index("tensor")
    z = me // 2
    y = me % 2
    sib = {"tensor": 1 - core}
    middle = (z >= 1) & (z <= outer - 2)

    def spot(zz, yy):
        return zz * 2 + yy

    def start_of(c):
        return pl.multiple_of(c * chunk - (c // (pop - 1)) * over, 128)

    def remote(src, dst, sidx, ridx, dev):
        return pltpu.make_async_remote_copy(
            src_ref=src, dst_ref=dst, send_sem=ssem.at[sidx], recv_sem=rsem.at[ridx],
            device_id=dev, device_id_type=pl.DeviceIdType.MESH,
        )

    barrier = pltpu.get_barrier_semaphore()
    for k in range(1, pop):
        for t in range(2):
            pl.semaphore_signal(
                barrier, inc=1, device_id={"pop": (me + k) % pop, "tensor": t}, device_id_type=pl.DeviceIdType.MESH
            )
    pl.semaphore_signal(barrier, inc=1, device_id=sib, device_id_type=pl.DeviceIdType.MESH)

    def load(src, dst, sem):
        d = pltpu.make_async_copy(src, dst, sem)
        d.start()
        return d

    lgof = load(gof_h, gof, msem.at[0])
    luof = load(uof_h, uof, msem.at[1])
    lprompts = load(prompts_in, prompts, msem.at[2])
    lgin = load(gate_in_h, gate_in, msem.at[3])
    luin = load(up_in_h, up_in, msem.at[4])
    order = [
        jnp.where(z == 0, 1, z - 1),
        jnp.where(z == outer - 1, 1, jnp.where(z == 2, 3, 2)),
        jnp.where(z < 2, 3, 0),
    ]
    line = order[::-1] + [z]
    owners = [spot(line[i % outer], (1 - y) if i < outer else y) for i in range(pop)]

    def weights(h, i):
        cols = pl.ds(pl.multiple_of(start_of(owners[i]) + h * piece, 128), piece)
        n = h * pop + i
        load(gate_w.at[:, cols], wgu.at[n, 0], wsem.at[n])
        load(up_w.at[:, cols], wgu.at[n, 1], wsem.at[n])

    steps = [(0, i) for i in range(outer + 2)] + [(1, 0), (1, 1), (0, 6), (0, 7)]
    steps += [(1, i) for i in range(2, pop)]
    weights(*steps[0])
    for d in (lgof, luof, lprompts, lgin, luin):
        d.wait()
    for at in steps[1:]:
        weights(*at)
    ldif = load(dif_h, dif, msem.at[5])
    ldout = load(dout_h, dout, msem.at[6])
    ltar = load(targets_in, targets, msem.at[7])

    fbuild[0:rank, :] = gof[...].astype(F32)
    fbuild[rank : 2 * rank, :] = uof[...].astype(F32)
    fac[me] = fbuild[...].astype(BF)
    pl.semaphore_wait(barrier, 2 * pop - 1)

    S_FAC, S_CH, S_LOW, S_Y, S_Z, S_A, S_X, S_LG, S_H, S_L, S_R = range(11)
    R_FAC, R_FZ, R_LOW, R_Y, R_Z, R_A, R_B, R_X, R_LG, R_H, R_L, R_R = 0, 1, 9, 10, 18, 20, 28, 32, 33, 34, 35, 36

    def send(src, dst, sidx, ridx, dev):
        d = remote(src, dst, sidx, ridx, dev)
        d.start()
        return d

    def sent(ref, sidx):
        remote(ref, ref, sidx, R_FAC, sib).wait_send()

    def came(ref, ridx):
        remote(ref, ref, S_FAC, ridx, sib).wait_recv()

    cut = ff // 256 * 128

    def chain(o, to, h):
        src = fac.at[spot(o, y), :, pl.ds(h * cut, cut if h == 0 else ff - cut)]
        return remote(src, src, S_CH, R_FZ + 2 * o + h, {"pop": spot(to, y)})

    send(fac.at[me], fac.at[me], S_FAC, R_FAC, {"pop": spot(z, 1 - y)})

    for h in range(2):

        @pl.when(z < outer - 1)
        def _(h=h):
            chain(z, z + 1, h).start()

        @pl.when(z > 0)
        def _(h=h):
            chain(z, z - 1, h).start()

    hrows = head.at[pl.ds(pl.multiple_of((me % part) * block, block), block)]
    holds = core == me // part

    x = prompts[...].astype(F32)
    normed[...] = (x * lax.rsqrt(jnp.mean(x * x, axis=-1, keepdims=True) + norm_eps)).astype(BF)

    scale = noise_scale / math.sqrt(width)
    lg = (scale * lax.dot_general(normed[...], gate_in[...], NT, preferred_element_type=F32)).astype(BF)
    lu = (scale * lax.dot_general(normed[...], up_in[...], NT, preferred_element_type=F32)).astype(BF)
    krow = lax.broadcasted_iota(jnp.int32, (rank, 128), 0)
    lane = lax.broadcasted_iota(jnp.int32, (rank, 128), 1)
    sel_g = (lane == me * 2 * rank + krow).astype(F32).astype(BF)
    sel_u = (lane == me * 2 * rank + rank + krow).astype(F32).astype(BF)
    low[me] = (
        jnp.dot(lg, sel_g, preferred_element_type=F32) + jnp.dot(lu, sel_u, preferred_element_type=F32)
    ).astype(BF)
    for k in range(1, pop):
        send(low.at[me], low.at[me], S_LOW, R_LOW, {"pop": (me + k) % pop})

    xcols = pl.ds(pl.multiple_of(me * block, block), block)
    mine_n = normed[:, xcols]

    def relay_first(h):
        @pl.when(middle)
        def _():
            chain(z - 1, z, h).wait_recv()
            chain(z - 1, z + 1, h).start()
            chain(z + 1, z, h).wait_recv()
            chain(z + 1, z - 1, h).start()

    far = 3 * (2 - z)
    end = 3 * (z - 1)

    def relay_second(h):
        @pl.when(middle)
        def _():
            chain(far, z, h).wait_recv()
            chain(far, end, h).start()

    def forward(n):
        o = order[n]

        @pl.when(jnp.logical_not(middle))
        def _():
            for h in range(2):
                chain(o, z, h).wait_recv()

        src = fac.at[spot(o, y)]
        send(src, src, S_FAC, R_FAC, {"pop": spot(z, 1 - y)})

    ycopies = {}
    step = ff // 4
    across = {"pop": spot(z, 1 - y)}

    def product(h, i):
        n = h * pop + i
        pltpu.make_async_copy(wgu.at[n], wgu.at[n], wsem.at[n]).wait()
        return [jnp.dot(mine_n, wgu[n, g], preferred_element_type=F32) for g in range(2)]

    def part_out(h, i):
        got = product(h, i)
        n = h * outer + i
        for g in range(2):
            ysend[n, g] = got[g].astype(BF)
        ycopies[h, i] = send(ysend.at[n], yrecv.at[n], S_Y, R_Y + n, across)

    def part_own(h, i):
        got = product(h, i)
        for g in range(2):
            own[h * outer + i - outer, g] = got[g]

    def part_on(h, i):
        j = i - outer
        n = h * outer + j
        ycopies[h, j].wait_recv()
        if i == pop - 1:
            for g in range(2):
                own[n, g] = own[n, g] + yrecv[n, g].astype(F32)
            return
        n3 = h * (outer - 1) + j
        for g in range(2):
            zsend[n3, g] = (own[n, g] + yrecv[n, g].astype(F32)).astype(BF)
        send(
            zsend.at[n3], zrecv.at[(outer - 1) * h + (line[j] - z + outer) % outer - 1],
            S_Z, R_Z + h, {"pop": spot(line[j], y)},
        )

    gaps = [(o - z + outer) % outer for o in order]

    def held(slot, h):
        return base.at[2 * slot + h]

    def gather(h):
        last = h * outer + outer - 1
        total = [own[last, 0], own[last, 1]]
        came(zrecv.at[(outer - 1) * h : (outer - 1) * (h + 1)], R_Z + h)
        for j in range(outer - 1):
            for g in range(2):
                total[g] = total[g] + zrecv[h * (outer - 1) + j, g].astype(F32)
        for g in range(2):
            base[h, g] = total[g].astype(BF)
        for n in (2, 1, 0):
            send(
                held(0, h), held(gaps[n], h), S_A, R_A + 2 * gaps[n] + h, {"pop": spot(order[n], y)}
            )

    def near(n):
        return (outer - gaps[n]) % outer

    def arrive(n, h):
        k = near(n)
        came(held(k, h), R_A + 2 * k + h)
        send(held(k, h), held(outer + k, h), S_A, R_B + k, across)

    def hand(h):
        send(held(0, h), held(outer, h), S_A, R_B, across)

    for i in range(outer):
        part_out(0, i)
    part_own(0, 4)
    relay_first(0)
    part_own(0, 5)
    relay_first(1)
    part_out(1, 0)
    part_out(1, 1)
    part_on(0, 4)
    part_own(0, 6)
    part_on(0, 5)
    part_own(0, 7)
    part_on(0, 6)
    relay_second(0)
    part_out(1, 2)
    relay_second(1)
    part_out(1, 3)
    part_on(0, 7)
    for n in range(4):
        at = pl.ds(n * step, step)
        load(down_w.at[at], dw.at[at], dsem.at[0])
    part_own(1, 4)
    part_own(1, 5)
    part_on(1, 4)
    forward(0)
    part_own(1, 6)
    part_on(1, 5)
    part_own(1, 7)
    forward(1)
    part_on(1, 6)
    gather(0)
    forward(2)
    hand(0)
    part_on(1, 7)

    @pl.when(holds)
    def _():
        remote(hrows, hblock, S_H, R_H, sib).start()
        pltpu.make_async_copy(hrows, hblock, msem.at[8]).start()

    ldout.wait()
    ldif.wait()
    ltar.wait()
    dall = jnp.concatenate([dout[m].astype(F32) for m in range(members)], axis=0)
    dcat[...] = jnp.concatenate([dall, dall], axis=0).astype(BF)
    acc[...] = jnp.zeros_like(acc)
    lowd[...] = jnp.zeros_like(lowd)
    came(low.at[1:], R_LOW)
    coef = jnp.concatenate([low[m].astype(F32) for m in range(members)], axis=0)
    lane = lax.broadcasted_iota(jnp.int32, coef.shape, 1)
    row = lax.broadcasted_iota(jnp.int32, coef.shape, 0) % rows
    kk = 2 * rank * members
    gate_lane = lane % (2 * rank) < rank
    gate_lhs = jnp.where(lane < kk, jnp.where(gate_lane, coef, 0.0), (lane == kk + row).astype(F32))
    up_lhs = jnp.where(lane < kk, jnp.where(gate_lane, 0.0, coef), (lane == kk + rows + row).astype(F32))
    lhs[...] = jnp.concatenate([0.5 * gate_lhs, up_lhs], axis=0).astype(BF)

    gather(1)
    hand(1)
    arrive(0, 0)

    pltpu.make_async_copy(down_w, dw, dsem.at[0]).wait()
    came(fac.at[0:outer], R_FAC)

    def expand(slot, c):
        start = start_of(c)
        skip = (c // (pop - 1)) * over

        pad = jnp.zeros((128 - kk - 2 * rows, tile), F32)
        for off in range(0, chunk, tile):
            at = pl.ds(pl.multiple_of(start + off, 128), tile)
            parts = [fac[m, :, at].astype(F32) for m in range(members)]
            low_off = off % piece
            parts += [
                base[2 * slot + off // piece, g, :, low_off : low_off + tile].astype(F32) for g in range(2)
            ]
            keep = (off >= skip).astype(F32)
            rhs = (jnp.concatenate(parts + [pad], axis=0) * keep).astype(BF)
            both = jnp.dot(lhs[...], rhs, preferred_element_type=F32)
            gate, up = both[:big], both[big:]
            hid[:, off : off + tile] = ((gate + gate * jnp.tanh(gate)) * up).astype(BF)
        h = hid[...]
        at = pl.ds(start, chunk)
        right = jnp.concatenate([dif[m, :, at].astype(F32) for m in range(members)], axis=0).astype(BF)
        lowd[...] += lax.dot_general(h, right, NT, preferred_element_type=F32)
        for off in range(0, block, tile):
            acc[:, off : off + tile] += jnp.dot(h, dw[at, off : off + tile], preferred_element_type=F32)

    expand(0, me)
    arrive(1, 0)
    arrive(0, 1)
    expand(near(0), spot(order[0], y))
    arrive(2, 0)
    arrive(1, 1)
    expand(near(1), spot(order[1], y))
    arrive(2, 1)
    expand(near(2), spot(order[2], y))
    came(base.at[2 * outer : 2 * outer + 2], R_B)
    expand(outer, spot(z, 1 - y))
    for n in range(outer - 1):
        k = outer + near(n)
        came(base.at[pl.ds(2 * k, 2)], R_B + near(n))
        expand(k, spot(order[n], 1 - y))

    mine = lax.broadcasted_iota(jnp.int32, lowd.shape, 0) // rows == lax.broadcasted_iota(jnp.int32, lowd.shape, 1) // rank
    lowm = jnp.where(mine, lowd[...] * (noise_scale / math.sqrt(total_ff)), 0.0)
    top = lowm.astype(BF).astype(F32)
    pair = jnp.concatenate([top, lowm - top], axis=1).astype(BF)
    acc[...] += jnp.dot(pair, dcat[...], preferred_element_type=F32)

    span = part * rows
    theirs = pl.ds(pl.multiple_of((1 - core) * span, span), span)
    ours = pl.ds(pl.multiple_of(core * span, span), span)
    xsend[...] = acc[theirs, :].astype(BF)
    xc = send(xsend, xrecv, S_X, R_X, sib)

    @pl.when(holds)
    def _():
        pltpu.make_async_copy(hrows, hblock, msem.at[8]).wait()

    @pl.when(jnp.logical_not(holds))
    def _():
        remote(hrows, hblock, S_H, R_H, sib).wait_recv()

    def logits_of(v):
        top = v.astype(BF)
        rest = (v - top.astype(F32)).astype(BF)
        got = jnp.dot(jnp.concatenate([top, rest], axis=0), hblock[...], preferred_element_type=F32)
        return got[:span] + got[span:]

    lgsend[...] = logits_of(acc[theirs, :])
    lc = send(lgsend, lgrecv, S_LG, R_LG, sib)
    pcols = prompts[:, xcols].astype(F32)
    here = acc[ours, :] + jnp.concatenate([pcols] * part, axis=0)
    lgts = logits_of(here)
    xc.wait_recv()
    out = here + xrecv[...].astype(F32)
    squares = out * out
    sq = squares[:, 0:128]
    for off in range(128, block, 128):
        sq = sq + squares[:, off : off + 128]
    top = sq.astype(BF).astype(F32)
    halves = jnp.concatenate([top, sq - top], axis=1).astype(BF)
    sums = lax.dot_general(jnp.ones((8, 256), BF), halves, NT, preferred_element_type=F32)
    for i in range(part):
        lsend[i, rows : rows + 8, :] = jnp.zeros((8, labels), F32)
        lsend[i, rows : rows + 8, 0:rows] = sums[:, i * rows : (i + 1) * rows]
    lc.wait_recv()
    for i in range(part):
        r = slice(i * rows, (i + 1) * rows)
        lsend[i, 0:rows, :] = lgts[r] + lgrecv[r, :]
    for i in range(part):
        m = core * part + i

        @pl.when(m != me)
        def _(i=i, m=m):
            remote(lsend.at[i], lrecv.at[me], S_L, R_L, {"pop": m}).start()

    @pl.when(holds)
    def _():
        came(lrecv.at[1:], R_L)
        tot = lsend[me % part]
        for k in range(1, pop):
            tot = tot + lrecv[(me + k) % pop]
        eye = (
            lax.broadcasted_iota(jnp.int32, (rows, labels), 0) == lax.broadcasted_iota(jnp.int32, (rows, labels), 1)
        ).astype(F32)
        ssq = jnp.sum(eye * tot[rows : rows + 1, :], axis=1, keepdims=True)
        lgt = tot[0:rows, :] * lax.rsqrt(ssq * (1.0 / width) + norm_eps)
        spread_t = jnp.where(eye[:, :rows] > 0.0, jnp.broadcast_to(targets[...].astype(F32), (rows, rows)), 0.0)
        target = jnp.sum(spread_t, axis=1, keepdims=True).astype(jnp.int32)
        picks = target == lax.broadcasted_iota(jnp.int32, (rows, labels), 1)
        picked = jnp.sum(jnp.where(picks, lgt, 0.0), axis=1, keepdims=True)
        term = picked - jnp.log(jnp.sum(jnp.exp(lgt), axis=1, keepdims=True))
        rbuf[me] = jnp.sum(jnp.broadcast_to(term, (rows, 128)), axis=0, keepdims=True) * (1.0 / rows)
        for k in range(1, pop):
            for t in range(2):
                send(rbuf.at[me], rbuf.at[me], S_R, R_R, {"pop": (me + k) % pop, "tensor": t})
        send(rbuf.at[me], rbuf.at[me], S_R, R_R, sib)
        came(rbuf.at[1:members], R_R)

    @pl.when(jnp.logical_not(holds))
    def _():
        came(rbuf.at[0:members], R_R)

    centre = sum(rbuf[m] for m in range(members)) * (1.0 / members)
    spread = sum((rbuf[m] - centre) * (rbuf[m] - centre) for m in range(members)) * (1.0 / members)
    inv = lax.rsqrt(spread + norm_eps)
    weighted_out[members * rank :, 0:128] = jnp.broadcast_to((rbuf[me] - centre) * inv, (8, 128))
    of = lax.broadcasted_iota(jnp.int32, (members * rank, 128), 0) // rank
    column = jnp.zeros((members * rank, 128), F32)
    for m in range(members):
        column = jnp.where(of == m, jnp.broadcast_to((rbuf[m] - centre) * inv, column.shape), column)
    for off in range(0, block, 128):
        at = slice(off, off + 128)
        weighted_out[0 : members * rank, at] = (dcat[0 : members * rank, at].astype(F32) * column).astype(BF).astype(F32)

    sent(fac.at[0:outer], S_FAC)
    sent(low.at[1:], S_LOW)
    sent(ysend, S_Y)
    sent(zsend, S_Z)
    sent(base.at[0 : 4 * outer - 2], S_A)
    sent(xsend, S_X)
    sent(lgsend, S_LG)

    @pl.when(middle)
    def _():
        sent(fac.at[0 : outer + 1], S_CH)

    @pl.when(jnp.logical_not(middle))
    def _():
        sent(fac.at[0], S_CH)

    @pl.when(holds)
    def _():
        sent(hblock, S_H)
        sent(lsend.at[1:], S_L)
        sent(rbuf.at[1:], S_R)

    @pl.when(jnp.logical_not(holds))
    def _():
        sent(lsend, S_L)


def update_kernel(norm, step, dif, weighted, out, score_out, left, right, sem):
    members, rank, ff = dif.shape
    width = weighted.shape[1]
    right[...] = weighted[0 : members * rank, :].astype(BF)
    cuts = [0, 128] + list(range(step, ff, step)) + [ff]
    blocks = [(at, end - at) for at, end in zip(cuts, cuts[1:])]
    for start, size in blocks:
        at = pl.ds(start, size)
        rows = jnp.concatenate([dif[m, :, at].astype(F32) for m in range(members)], axis=0).T.astype(BF)
        for c in range(0, width, 256):
            got = jnp.dot(rows, right[:, c : c + 256], preferred_element_type=F32)
            left[at, c : c + 256] = (got * norm).astype(BF)
        pltpu.make_async_copy(left.at[at], out.at[at], sem).start()
    score_out[0] = weighted[members * rank, 0]
    pltpu.make_async_copy(left, out, sem).wait()


def fast_body(
    pop, prompts, gate_weight, up_weight, down_weight, gate_in, gof, up_in, uof, dif, dout, head, targets
):
    rows, width = prompts.shape
    block, ff = gate_weight.shape
    members, _, rank = dif.shape
    outer = pop // 2
    chunk = -(-(ff // 128) // pop) * 128
    piece = chunk // 2
    labels = head.shape[1]
    swap = lambda v: jnp.swapaxes(v, 1, 2)
    dif_t, dout_t = swap(dif), swap(dout)
    vm = pl.BlockSpec(memory_space=pltpu.VMEM)
    hb = pl.BlockSpec(memory_space=pl.ANY)
    V = pltpu.VMEM
    D = pltpu.SemaphoreType.DMA
    big = members * rows
    weighted = pl.pallas_call(
        functools.partial(pair_kernel, pop, 2 * ff),
        out_shape=V((members * rank + 8, block), F32),
        in_specs=[hb] * 12,
        out_specs=vm,
        scratch_shapes=[
            V((rows, width), BF), V((rank, width), BF), V((rank, ff), BF), V((rank, width), BF), V((rank, ff), BF),
            V((members, rank, ff), BF), V((members, rank, block), BF), V((1, rows), jnp.int32),
            V((2 * pop, 2, block, piece), BF), V((ff, block), BF),
            V((rows, width), BF), V((2 * rank, ff), F32), V((members, 2 * rank, ff), BF),
            V((members, rows, 128), BF), V((pop, 2, rows, piece), F32),
            V((pop, 2, rows, piece), BF), V((pop, 2, rows, piece), BF),
            V((pop - 2, 2, rows, piece), BF), V((pop - 2, 2, rows, piece), BF),
            V((2 * pop, 2, rows, piece), BF),
            V((2 * big, 128), BF), V((big, chunk), BF), V((big, block), F32), V((big, members * rank), F32),
            V((2 * members * rank, block), BF), V((big // 2, block), BF), V((big // 2, block), BF),
            V((block, labels), BF),
            V((big // 2, labels), F32), V((big // 2, labels), F32),
            V((members // 2, rows + 8, labels), F32), V((members, rows + 8, labels), F32),
            V((2 * members, 1, 128), F32),
            D((2 * pop,)), D((1,)), D((9,)), D((11,)), D((37,)),
        ],
        compiler_params=pltpu.CompilerParams(
            collective_id=0, has_side_effects=True, vmem_limit_bytes=60 * 1000 * 1000
        ),
        name="pair",
    )(
        prompts, gate_weight, up_weight, down_weight, swap(gate_in)[0], swap(gof)[0], swap(up_in)[0],
        swap(uof)[0], dif_t, dout_t, head, targets[None],
    )
    step = 384
    update, scores = pl.pallas_call(
        functools.partial(update_kernel, 1.0 / math.sqrt(members * rank), step),
        out_shape=(jax.ShapeDtypeStruct((ff, block), BF), jax.ShapeDtypeStruct((1,), F32)),
        in_specs=[vm, vm],
        out_specs=(hb, pl.BlockSpec(memory_space=pltpu.SMEM)),
        scratch_shapes=[
            V((ff, block), BF), V((members * rank, block), BF), D(()),
        ],
        compiler_params=pltpu.CompilerParams(vmem_limit_bytes=40 * 1000 * 1000),
        name="update",
    )(dif_t, weighted)
    return update, scores


def solution(mesh):
    placed = (
        P("groups", None),
        P("pop", "tensor"),
        P("pop", "tensor"),
        P("tensor", "pop"),
        P(("groups", "pop"), None, None),
        P(("groups", "pop"), "tensor", None),
        P(("groups", "pop"), None, None),
        P(("groups", "pop"), "tensor", None),
        P("groups", "tensor", None),
        P("groups", "pop", None),
        P("tensor", None),
        P("groups"),
    )
    pop = mesh.shape["pop"]
    run = functools.partial(fast_body, pop) if pop == 8 and mesh.shape["tensor"] == 2 else body
    return jax.shard_map(
        run,
        mesh=mesh,
        in_specs=placed,
        out_specs=(P(("groups", "tensor"), "pop"), P(("groups", "pop"))),
        check_vma=False,
    )
```

```python
import functools
import math

import jax
import jax.numpy as jnp
from jax import lax
from jax.experimental import pallas as pl
from jax.experimental.pallas import tpu as pltpu
from jax.sharding import PartitionSpec as P

noise_scale = 0.2
norm_eps = 1e-06


def scaled_rows(values):
    return values * lax.rsqrt(jnp.mean(values * values, axis=-1, keepdims=True) + norm_eps)


def build_hidden(
    gate_baseline, up_baseline, lowrank_gate, lowrank_up, gate_output_factors, up_output_factors
):
    gate_activation = gate_baseline.astype(jnp.float32)[None] + jnp.einsum(
        "hvw,hpw->hvp", lowrank_gate, gate_output_factors, preferred_element_type=jnp.float32
    )
    upper_bound = up_baseline.astype(jnp.float32)[None] + jnp.einsum(
        "hvw,hpw->hvp", lowrank_up, up_output_factors, preferred_element_type=jnp.float32
    )
    return (jax.nn.silu(gate_activation) * upper_bound).astype(jnp.bfloat16)


def label_terms(logits, targets):
    labels = logits.shape[1]
    picks = targets[:, None] == jnp.arange(labels, dtype=jnp.int32)[None, :]
    picked = jnp.sum(jnp.where(picks, logits, 0.0), axis=1)
    return picked - jnp.log(jnp.sum(jnp.exp(logits), axis=1))


def body(
    prompts,
    gate_weight,
    up_weight,
    down_weight_matrix,
    gate_in,
    gate_output_factors,
    up_in,
    up_output_factors,
    down_input_factors,
    down_out,
    label_head,
    targets,
):
    member = lax.axis_index("pop")
    width = prompts.shape[1]
    in_block = gate_weight.shape[0]
    ffn_half = gate_output_factors.shape[1]
    total_ff = ffn_half * lax.axis_size("tensor")
    members = down_input_factors.shape[0]
    rank = down_input_factors.shape[2]
    prompt_f = prompts.astype(jnp.float32)
    normed = scaled_rows(prompt_f).astype(jnp.bfloat16)
    own_cols = lax.dynamic_slice_in_dim(normed, member * in_block, in_block, 1)
    part_gate = jnp.dot(own_cols, gate_weight, preferred_element_type=jnp.float32)
    part_up = jnp.dot(own_cols, up_weight, preferred_element_type=jnp.float32)
    total_gate, total_up = lax.psum((part_gate, part_up), "pop")
    gate_baseline = total_gate.astype(jnp.bfloat16)
    up_baseline = total_up.astype(jnp.bfloat16)
    in_scale = noise_scale / math.sqrt(width)
    lowrank_gate = (
        in_scale * jnp.einsum("rd,mdk->mrk", normed, gate_in, preferred_element_type=jnp.float32)
    ).astype(jnp.bfloat16)
    lowrank_up = (
        in_scale * jnp.einsum("rd,mdk->mrk", normed, up_in, preferred_element_type=jnp.float32)
    ).astype(jnp.bfloat16)
    down_scale = noise_scale / math.sqrt(total_ff)
    hidden_state = build_hidden(
        gate_baseline, up_baseline, lowrank_gate, lowrank_up, gate_output_factors, up_output_factors
    )
    hidden_portion = lax.all_gather(hidden_state, "pop", axis=0, tiled=True)
    out_piece = down_out.astype(jnp.float32)
    entry_point = jnp.einsum(
        "uaz,zh->uah", hidden_portion, down_weight_matrix, preferred_element_type=jnp.float32
    )
    low_part = down_scale * jnp.einsum(
        "lpq,lqb->lpb", hidden_portion, down_input_factors, preferred_element_type=jnp.float32
    )
    partial_rows = entry_point + jnp.einsum(
        "mrk,mdk->mrd", low_part, out_piece, precision=lax.Precision.HIGHEST
    )
    rows_here = lax.all_to_all(partial_rows, "pop", split_axis=0, concat_axis=2, tiled=True)
    summed = lax.psum(rows_here, "tensor")[0]
    output = prompt_f + summed
    final = scaled_rows(output).astype(jnp.bfloat16)
    half = label_head.shape[0]
    own_half = lax.dynamic_slice_in_dim(final, lax.axis_index("tensor") * half, half, 1)
    logits = lax.psum(jnp.dot(own_half, label_head, preferred_element_type=jnp.float32), "tensor")
    reward = jnp.mean(label_terms(logits, targets))
    rewards = lax.all_gather(reward.reshape(1), "pop", axis=0, tiled=True)
    centre = jnp.mean(rewards)
    spread = jnp.mean((rewards - centre) * (rewards - centre))
    scores = (rewards - centre) * lax.rsqrt(spread + norm_eps)
    weighted = (scores[:, None, None] * down_out.astype(jnp.float32)).astype(jnp.bfloat16)
    update = jnp.einsum(
        "mfk,mdk->fd", down_input_factors, weighted, preferred_element_type=jnp.float32
    ) * (1.0 / math.sqrt(members * rank))
    own_score = lax.dynamic_slice_in_dim(scores, member, 1, 0)
    return (update.astype(jnp.bfloat16), own_score)


BF = jnp.bfloat16
F32 = jnp.float32
HI = lax.Precision.HIGHEST
NT = (((1,), (1,)), ((), ()))
TN = (((0,), (0,)), ((), ()))


def pair_kernel(
    pop, total_ff,
    prompts_in, gate_w, up_w, down_w, gate_in_h, gof_h, up_in_h, uof_h, dif_h, dout_h, head, targets_in,
    weighted_out,
    prompts, gate_in, gof, up_in, uof, dif, dout, targets,
    wgu, dw, normed, fbuild, fac, low, own, ysend, yrecv, zsend, zrecv, base,
    lhs, hid, acc, lowd, dcat, xsend, xrecv, hblock,
    lgsend, lgrecv, lsend, lrecv, rbuf,
    wsem, dsem, msem, ssem, rsem,
):
    rows, width = prompts.shape
    block, ff = gate_w.shape
    outer = pop // 2
    piece = wgu.shape[3]
    chunk = 2 * piece
    members = pop
    rank = gof.shape[0]
    part = members // 2
    big = members * rows
    labels = head.shape[1]
    over = pop * chunk - ff
    tile = 256
    me = lax.axis_index("pop")
    core = lax.axis_index("tensor")
    z = me // 2
    y = me % 2
    sib = {"tensor": 1 - core}
    middle = (z >= 1) & (z <= outer - 2)

    def spot(zz, yy):
        return zz * 2 + yy

    def start_of(c):
        return pl.multiple_of(c * chunk - (c // (pop - 1)) * over, 128)

    def remote(src, dst, sidx, ridx, dev):
        return pltpu.make_async_remote_copy(
            src_ref=src, dst_ref=dst, send_sem=ssem.at[sidx], recv_sem=rsem.at[ridx],
            device_id=dev, device_id_type=pl.DeviceIdType.MESH,
        )

    barrier = pltpu.get_barrier_semaphore()
    for k in range(1, pop):
        for t in range(2):
            pl.semaphore_signal(
                barrier, inc=1, device_id={"pop": (me + k) % pop, "tensor": t}, device_id_type=pl.DeviceIdType.MESH
            )
    pl.semaphore_signal(barrier, inc=1, device_id=sib, device_id_type=pl.DeviceIdType.MESH)

    def load(src, dst, sem):
        d = pltpu.make_async_copy(src, dst, sem)
        d.start()
        return d

    lgof = load(gof_h, gof, msem.at[0])
    luof = load(uof_h, uof, msem.at[1])
    lprompts = load(prompts_in, prompts, msem.at[2])
    lgin = load(gate_in_h, gate_in, msem.at[3])
    luin = load(up_in_h, up_in, msem.at[4])
    order = [z + 1 - 2 * (z % 2), jnp.where(z < 2, 2, 1), jnp.where(z < 2, 3, 0)]
    line = order[::-1] + [z]
    owners = [spot(line[i % outer], (1 - y) if i < outer else y) for i in range(pop)]

    def weights(h, i):
        cols = pl.ds(pl.multiple_of(start_of(owners[i]) + h * piece, 128), piece)
        n = h * pop + i
        load(gate_w.at[:, cols], wgu.at[n, 0], wsem.at[n])
        load(up_w.at[:, cols], wgu.at[n, 1], wsem.at[n])

    steps = [(0, i) for i in range(outer + 2)] + [(1, 0), (1, 1), (0, 6), (0, 7)]
    steps += [(1, i) for i in range(2, pop)]
    weights(*steps[0])
    for d in (lgof, luof, lprompts, lgin, luin):
        d.wait()
    for at in steps[1:]:
        weights(*at)
    ldif = load(dif_h, dif, msem.at[5])
    ldout = load(dout_h, dout, msem.at[6])
    ltar = load(targets_in, targets, msem.at[7])

    fbuild[0:rank, :] = gof[...].astype(F32)
    fbuild[rank : 2 * rank, :] = uof[...].astype(F32)
    fac[me] = fbuild[...].astype(BF)
    pl.semaphore_wait(barrier, 2 * pop - 1)

    S_FAC, S_CH, S_LOW, S_Y, S_Z, S_A, S_X, S_LG, S_H, S_L, S_R = range(11)
    R_FAC, R_FZ, R_LOW, R_Y, R_Z, R_A, R_B, R_X, R_LG, R_H, R_L, R_R, R_F = 0, 1, 9, 10, 18, 20, 28, 32, 33, 34, 35, 36, 37

    def send(src, dst, sidx, ridx, dev):
        d = remote(src, dst, sidx, ridx, dev)
        d.start()
        return d

    def sent(ref, sidx):
        remote(ref, ref, sidx, R_FAC, sib).wait_send()

    def came(ref, ridx):
        remote(ref, ref, S_FAC, ridx, sib).wait_recv()

    cut = outer * chunk

    def half_of(m, h):
        return fac.at[m, :, pl.ds(h * cut, cut if h == 0 else ff - cut)]

    def chain(o, to, h):
        src = half_of(spot(o, y), h)
        return remote(src, src, S_CH, R_FZ + 2 * o + h, {"pop": spot(to, y)})

    send(fac.at[me], fac.at[me], S_FAC, R_FAC, {"pop": spot(z, 1 - y)})

    for h in range(2):

        @pl.when(z < outer - 1)
        def _(h=h):
            chain(z, z + 1, h).start()

        @pl.when(z > 0)
        def _(h=h):
            chain(z, z - 1, h).start()

    hrows = head.at[pl.ds(pl.multiple_of((me % part) * block, block), block)]
    holds = core == me // part

    x = prompts[...].astype(F32)
    normed[...] = (x * lax.rsqrt(jnp.mean(x * x, axis=-1, keepdims=True) + norm_eps)).astype(BF)

    scale = noise_scale / math.sqrt(width)
    lg = (scale * lax.dot_general(normed[...], gate_in[...], NT, preferred_element_type=F32)).astype(BF)
    lu = (scale * lax.dot_general(normed[...], up_in[...], NT, preferred_element_type=F32)).astype(BF)
    krow = lax.broadcasted_iota(jnp.int32, (rank, 128), 0)
    lane = lax.broadcasted_iota(jnp.int32, (rank, 128), 1)
    sel_g = (lane == me * 2 * rank + krow).astype(F32).astype(BF)
    sel_u = (lane == me * 2 * rank + rank + krow).astype(F32).astype(BF)
    low[me] = (
        jnp.dot(lg, sel_g, preferred_element_type=F32) + jnp.dot(lu, sel_u, preferred_element_type=F32)
    ).astype(BF)
    for k in range(1, pop):
        send(low.at[me], low.at[me], S_LOW, R_LOW, {"pop": (me + k) % pop})

    xcols = pl.ds(pl.multiple_of(me * block, block), block)
    mine_n = normed[:, xcols]

    def relay_first(h):
        @pl.when(middle)
        def _():
            chain(z - 1, z, h).wait_recv()
            chain(z - 1, z + 1, h).start()
            chain(z + 1, z, h).wait_recv()
            chain(z + 1, z - 1, h).start()

    far = 3 * (2 - z)
    end = 3 * (z - 1)

    def relay_second(h):
        @pl.when(middle)
        def _():
            chain(far, z, h).wait_recv()
            chain(far, end, h).start()

    def forward(n):
        o = order[n]

        @pl.when(jnp.logical_not(middle))
        def _():
            for h in range(2):
                chain(o, z, h).wait_recv()

        if n < outer - 2:
            src = fac.at[spot(o, y)]
            send(src, src, S_FAC, R_FAC, {"pop": spot(z, 1 - y)})
            return
        for t, close in enumerate((z < 2, z >= 2)):
            for h in range(2):

                @pl.when(close if h == 0 else jnp.logical_not(close))
                def _(h=h, t=t):
                    src = half_of(spot(o, y), h)
                    send(src, src, S_FAC, R_F + t, {"pop": spot(z, 1 - y)})


    ycopies = {}
    step = ff // 4
    across = {"pop": spot(z, 1 - y)}

    def product(h, i):
        n = h * pop + i
        pltpu.make_async_copy(wgu.at[n], wgu.at[n], wsem.at[n]).wait()
        return [jnp.dot(mine_n, wgu[n, g], preferred_element_type=F32) for g in range(2)]

    def part_out(h, i):
        got = product(h, i)
        n = h * outer + i
        for g in range(2):
            ysend[n, g] = got[g].astype(BF)
        ycopies[h, i] = send(ysend.at[n], yrecv.at[n], S_Y, R_Y + n, across)

    def part_own(h, i):
        got = product(h, i)
        for g in range(2):
            own[h * outer + i - outer, g] = got[g]

    def part_on(h, i):
        j = i - outer
        n = h * outer + j
        ycopies[h, j].wait_recv()
        if i == pop - 1:
            for g in range(2):
                own[n, g] = own[n, g] + yrecv[n, g].astype(F32)
            return
        n3 = h * (outer - 1) + j
        for g in range(2):
            zsend[n3, g] = (own[n, g] + yrecv[n, g].astype(F32)).astype(BF)
        send(
            zsend.at[n3], zrecv.at[(outer - 1) * h + (line[j] - z + outer) % outer - 1],
            S_Z, R_Z + h, {"pop": spot(line[j], y)},
        )

    gaps = [(o - z + outer) % outer for o in order]

    def held(slot, h):
        return base.at[2 * slot + h]

    def gather(h):
        last = h * outer + outer - 1
        total = [own[last, 0], own[last, 1]]
        came(zrecv.at[(outer - 1) * h : (outer - 1) * (h + 1)], R_Z + h)
        for j in range(outer - 1):
            for g in range(2):
                total[g] = total[g] + zrecv[h * (outer - 1) + j, g].astype(F32)
        for g in range(2):
            base[h, g] = total[g].astype(BF)
        for n in (2, 1, 0):
            send(
                held(0, h), held(gaps[n], h), S_A, R_A + 2 * gaps[n] + h, {"pop": spot(order[n], y)}
            )

    def near(n):
        return (outer - gaps[n]) % outer

    def arrive(n, h):
        k = near(n)
        came(held(k, h), R_A + 2 * k + h)
        send(held(k, h), held(outer + k, h), S_A, R_B + k, across)

    def hand(h):
        send(held(0, h), held(outer, h), S_A, R_B, across)

    for i in range(outer):
        part_out(0, i)
    part_own(0, 4)
    relay_first(0)
    part_own(0, 5)
    relay_first(1)
    part_out(1, 0)
    part_out(1, 1)
    part_on(0, 4)
    part_own(0, 6)
    part_on(0, 5)
    part_own(0, 7)
    part_on(0, 6)
    relay_second(0)
    part_out(1, 2)
    relay_second(1)
    part_out(1, 3)
    part_on(0, 7)
    for n in range(4):
        at = pl.ds(n * step, step)
        load(down_w.at[at], dw.at[at], dsem.at[0])
    part_own(1, 4)
    part_own(1, 5)
    part_on(1, 4)
    forward(0)
    part_own(1, 6)
    part_on(1, 5)
    part_own(1, 7)
    forward(1)
    part_on(1, 6)
    gather(0)
    forward(2)
    hand(0)
    part_on(1, 7)

    @pl.when(holds)
    def _():
        remote(hrows, hblock, S_H, R_H, sib).start()
        pltpu.make_async_copy(hrows, hblock, msem.at[8]).start()

    ldout.wait()
    ldif.wait()
    ltar.wait()
    dall = jnp.concatenate([dout[m].astype(F32) for m in range(members)], axis=0)
    dcat[...] = jnp.concatenate([dall, dall], axis=0).astype(BF)
    acc[...] = jnp.zeros_like(acc)
    lowd[...] = jnp.zeros_like(lowd)
    came(low.at[1:], R_LOW)
    coef = jnp.concatenate([low[m].astype(F32) for m in range(members)], axis=0)
    lane = lax.broadcasted_iota(jnp.int32, coef.shape, 1)
    row = lax.broadcasted_iota(jnp.int32, coef.shape, 0) % rows
    kk = 2 * rank * members
    gate_lane = lane % (2 * rank) < rank
    gate_lhs = jnp.where(lane < kk, jnp.where(gate_lane, coef, 0.0), (lane == kk + row).astype(F32))
    up_lhs = jnp.where(lane < kk, jnp.where(gate_lane, 0.0, coef), (lane == kk + rows + row).astype(F32))
    lhs[...] = jnp.concatenate([0.5 * gate_lhs, up_lhs], axis=0).astype(BF)

    gather(1)
    hand(1)
    arrive(0, 0)

    pltpu.make_async_copy(down_w, dw, dsem.at[0]).wait()
    came(fac.at[0 : outer - 1], R_FAC)

    def last_half(t, close):
        for h in range(2):

            @pl.when(close if h == 0 else jnp.logical_not(close))
            def _(h=h):
                came(half_of(0, h), R_F + t)

    last_half(0, z < 2)

    def expand(slot, c):
        start = start_of(c)
        skip = (c // (pop - 1)) * over

        pad = jnp.zeros((128 - kk - 2 * rows, tile), F32)
        for off in range(0, chunk, tile):
            at = pl.ds(pl.multiple_of(start + off, 128), tile)
            parts = [fac[m, :, at].astype(F32) for m in range(members)]
            low_off = off % piece
            parts += [
                base[2 * slot + off // piece, g, :, low_off : low_off + tile].astype(F32) for g in range(2)
            ]
            keep = (off >= skip).astype(F32)
            rhs = (jnp.concatenate(parts + [pad], axis=0) * keep).astype(BF)
            both = jnp.dot(lhs[...], rhs, preferred_element_type=F32)
            gate, up = both[:big], both[big:]
            hid[:, off : off + tile] = ((gate + gate * jnp.tanh(gate)) * up).astype(BF)
        h = hid[...]
        at = pl.ds(start, chunk)
        right = jnp.concatenate([dif[m, :, at].astype(F32) for m in range(members)], axis=0).astype(BF)
        lowd[...] += lax.dot_general(h, right, NT, preferred_element_type=F32)
        for off in range(0, block, tile):
            acc[:, off : off + tile] += jnp.dot(h, dw[at, off : off + tile], preferred_element_type=F32)

    expand(0, me)
    arrive(1, 0)
    arrive(0, 1)
    expand(near(0), spot(order[0], y))
    last_half(1, z >= 2)
    arrive(2, 0)
    arrive(1, 1)
    expand(near(1), spot(order[1], y))
    arrive(2, 1)
    expand(near(2), spot(order[2], y))
    came(base.at[2 * outer : 2 * outer + 2], R_B)
    expand(outer, spot(z, 1 - y))
    for n in range(outer - 1):
        k = outer + near(n)
        came(base.at[pl.ds(2 * k, 2)], R_B + near(n))
        expand(k, spot(order[n], 1 - y))

    mine = lax.broadcasted_iota(jnp.int32, lowd.shape, 0) // rows == lax.broadcasted_iota(jnp.int32, lowd.shape, 1) // rank
    lowm = jnp.where(mine, lowd[...] * (noise_scale / math.sqrt(total_ff)), 0.0)
    top = lowm.astype(BF).astype(F32)
    pair = jnp.concatenate([top, lowm - top], axis=1).astype(BF)
    acc[...] += jnp.dot(pair, dcat[...], preferred_element_type=F32)

    span = part * rows
    theirs = pl.ds(pl.multiple_of((1 - core) * span, span), span)
    ours = pl.ds(pl.multiple_of(core * span, span), span)
    xsend[...] = acc[theirs, :].astype(BF)
    xc = send(xsend, xrecv, S_X, R_X, sib)

    @pl.when(holds)
    def _():
        pltpu.make_async_copy(hrows, hblock, msem.at[8]).wait()

    @pl.when(jnp.logical_not(holds))
    def _():
        remote(hrows, hblock, S_H, R_H, sib).wait_recv()

    def logits_of(v):
        top = v.astype(BF)
        rest = (v - top.astype(F32)).astype(BF)
        got = jnp.dot(jnp.concatenate([top, rest], axis=0), hblock[...], preferred_element_type=F32)
        return got[:span] + got[span:]

    lgsend[...] = logits_of(acc[theirs, :])
    lc = send(lgsend, lgrecv, S_LG, R_LG, sib)
    pcols = prompts[:, xcols].astype(F32)
    here = acc[ours, :] + jnp.concatenate([pcols] * part, axis=0)
    lgts = logits_of(here)
    xc.wait_recv()
    out = here + xrecv[...].astype(F32)
    squares = out * out
    sq = squares[:, 0:128]
    for off in range(128, block, 128):
        sq = sq + squares[:, off : off + 128]
    top = sq.astype(BF).astype(F32)
    halves = jnp.concatenate([top, sq - top], axis=1).astype(BF)
    sums = lax.dot_general(jnp.ones((8, 256), BF), halves, NT, preferred_element_type=F32)
    for i in range(part):
        lsend[i, rows : rows + 8, :] = jnp.zeros((8, labels), F32)
        lsend[i, rows : rows + 8, 0:rows] = sums[:, i * rows : (i + 1) * rows]
    lc.wait_recv()
    for i in range(part):
        r = slice(i * rows, (i + 1) * rows)
        lsend[i, 0:rows, :] = lgts[r] + lgrecv[r, :]
    for i in range(part):
        m = core * part + i

        @pl.when(m != me)
        def _(i=i, m=m):
            remote(lsend.at[i], lrecv.at[me], S_L, R_L, {"pop": m}).start()

    @pl.when(holds)
    def _():
        came(lrecv.at[1:], R_L)
        tot = lsend[me % part]
        for k in range(1, pop):
            tot = tot + lrecv[(me + k) % pop]
        eye = (
            lax.broadcasted_iota(jnp.int32, (rows, labels), 0) == lax.broadcasted_iota(jnp.int32, (rows, labels), 1)
        ).astype(F32)
        ssq = jnp.sum(eye * tot[rows : rows + 1, :], axis=1, keepdims=True)
        lgt = tot[0:rows, :] * lax.rsqrt(ssq * (1.0 / width) + norm_eps)
        spread_t = jnp.where(eye[:, :rows] > 0.0, jnp.broadcast_to(targets[...].astype(F32), (rows, rows)), 0.0)
        target = jnp.sum(spread_t, axis=1, keepdims=True).astype(jnp.int32)
        picks = target == lax.broadcasted_iota(jnp.int32, (rows, labels), 1)
        picked = jnp.sum(jnp.where(picks, lgt, 0.0), axis=1, keepdims=True)
        term = picked - jnp.log(jnp.sum(jnp.exp(lgt), axis=1, keepdims=True))
        rbuf[me] = jnp.sum(jnp.broadcast_to(term, (rows, 128)), axis=0, keepdims=True) * (1.0 / rows)
        for k in range(1, pop):
            for t in range(2):
                send(rbuf.at[me], rbuf.at[me], S_R, R_R, {"pop": (me + k) % pop, "tensor": t})
        send(rbuf.at[me], rbuf.at[me], S_R, R_R, sib)
        came(rbuf.at[1:members], R_R)

    @pl.when(jnp.logical_not(holds))
    def _():
        came(rbuf.at[0:members], R_R)

    centre = sum(rbuf[m] for m in range(members)) * (1.0 / members)
    spread = sum((rbuf[m] - centre) * (rbuf[m] - centre) for m in range(members)) * (1.0 / members)
    inv = lax.rsqrt(spread + norm_eps)
    weighted_out[members * rank :, 0:128] = jnp.broadcast_to((rbuf[me] - centre) * inv, (8, 128))
    of = lax.broadcasted_iota(jnp.int32, (members * rank, 128), 0) // rank
    column = jnp.zeros((members * rank, 128), F32)
    for m in range(members):
        column = jnp.where(of == m, jnp.broadcast_to((rbuf[m] - centre) * inv, column.shape), column)
    for off in range(0, block, 128):
        at = slice(off, off + 128)
        weighted_out[0 : members * rank, at] = (dcat[0 : members * rank, at].astype(F32) * column).astype(BF).astype(F32)

    sent(fac.at[0:outer], S_FAC)
    sent(low.at[1:], S_LOW)
    sent(ysend, S_Y)
    sent(zsend, S_Z)
    sent(base.at[0 : 4 * outer - 2], S_A)
    sent(xsend, S_X)
    sent(lgsend, S_LG)

    @pl.when(middle)
    def _():
        sent(fac.at[0 : outer + 1], S_CH)

    @pl.when(jnp.logical_not(middle))
    def _():
        sent(fac.at[0], S_CH)

    @pl.when(holds)
    def _():
        sent(hblock, S_H)
        sent(lsend.at[1:], S_L)
        sent(rbuf.at[1:], S_R)

    @pl.when(jnp.logical_not(holds))
    def _():
        sent(lsend, S_L)


def update_kernel(norm, step, dif, weighted, out, score_out, left, right, sem):
    members, rank, ff = dif.shape
    width = weighted.shape[1]
    right[...] = weighted[0 : members * rank, :].astype(BF)
    cuts = [0, 128] + list(range(step, ff, step)) + [ff]
    blocks = [(at, end - at) for at, end in zip(cuts, cuts[1:])]
    for start, size in blocks:
        at = pl.ds(start, size)
        rows = jnp.concatenate([dif[m, :, at].astype(F32) for m in range(members)], axis=0).T.astype(BF)
        for c in range(0, width, 256):
            got = jnp.dot(rows, right[:, c : c + 256], preferred_element_type=F32)
            left[at, c : c + 256] = (got * norm).astype(BF)
        pltpu.make_async_copy(left.at[at], out.at[at], sem).start()
    score_out[0] = weighted[members * rank, 0]
    pltpu.make_async_copy(left, out, sem).wait()


def fast_body(
    pop, prompts, gate_weight, up_weight, down_weight, gate_in, gof, up_in, uof, dif, dout, head, targets
):
    rows, width = prompts.shape
    block, ff = gate_weight.shape
    members, _, rank = dif.shape
    outer = pop // 2
    chunk = -(-(ff // 128) // pop) * 128
    piece = chunk // 2
    labels = head.shape[1]
    swap = lambda v: jnp.swapaxes(v, 1, 2)
    dif_t, dout_t = swap(dif), swap(dout)
    vm = pl.BlockSpec(memory_space=pltpu.VMEM)
    hb = pl.BlockSpec(memory_space=pl.ANY)
    V = pltpu.VMEM
    D = pltpu.SemaphoreType.DMA
    big = members * rows
    weighted = pl.pallas_call(
        functools.partial(pair_kernel, pop, 2 * ff),
        out_shape=V((members * rank + 8, block), F32),
        in_specs=[hb] * 12,
        out_specs=vm,
        scratch_shapes=[
            V((rows, width), BF), V((rank, width), BF), V((rank, ff), BF), V((rank, width), BF), V((rank, ff), BF),
            V((members, rank, ff), BF), V((members, rank, block), BF), V((1, rows), jnp.int32),
            V((2 * pop, 2, block, piece), BF), V((ff, block), BF),
            V((rows, width), BF), V((2 * rank, ff), F32), V((members, 2 * rank, ff), BF),
            V((members, rows, 128), BF), V((pop, 2, rows, piece), F32),
            V((pop, 2, rows, piece), BF), V((pop, 2, rows, piece), BF),
            V((pop - 2, 2, rows, piece), BF), V((pop - 2, 2, rows, piece), BF),
            V((2 * pop, 2, rows, piece), BF),
            V((2 * big, 128), BF), V((big, chunk), BF), V((big, block), F32), V((big, members * rank), F32),
            V((2 * members * rank, block), BF), V((big // 2, block), BF), V((big // 2, block), BF),
            V((block, labels), BF),
            V((big // 2, labels), F32), V((big // 2, labels), F32),
            V((members // 2, rows + 8, labels), F32), V((members, rows + 8, labels), F32),
            V((2 * members, 1, 128), F32),
            D((2 * pop,)), D((1,)), D((9,)), D((11,)), D((39,)),
        ],
        compiler_params=pltpu.CompilerParams(
            collective_id=0, has_side_effects=True, vmem_limit_bytes=60 * 1000 * 1000
        ),
        name="pair",
    )(
        prompts, gate_weight, up_weight, down_weight, swap(gate_in)[0], swap(gof)[0], swap(up_in)[0],
        swap(uof)[0], dif_t, dout_t, head, targets[None],
    )
    step = 384
    update, scores = pl.pallas_call(
        functools.partial(update_kernel, 1.0 / math.sqrt(members * rank), step),
        out_shape=(jax.ShapeDtypeStruct((ff, block), BF), jax.ShapeDtypeStruct((1,), F32)),
        in_specs=[vm, vm],
        out_specs=(hb, pl.BlockSpec(memory_space=pltpu.SMEM)),
        scratch_shapes=[
            V((ff, block), BF), V((members * rank, block), BF), D(()),
        ],
        compiler_params=pltpu.CompilerParams(vmem_limit_bytes=40 * 1000 * 1000),
        name="update",
    )(dif_t, weighted)
    return update, scores


def solution(mesh):
    placed = (
        P("groups", None),
        P("pop", "tensor"),
        P("pop", "tensor"),
        P("tensor", "pop"),
        P(("groups", "pop"), None, None),
        P(("groups", "pop"), "tensor", None),
        P(("groups", "pop"), None, None),
        P(("groups", "pop"), "tensor", None),
        P("groups", "tensor", None),
        P("groups", "pop", None),
        P("tensor", None),
        P("groups"),
    )
    pop = mesh.shape["pop"]
    run = functools.partial(fast_body, pop) if pop == 8 and mesh.shape["tensor"] == 2 else body
    return jax.shard_map(
        run,
        mesh=mesh,
        in_specs=placed,
        out_specs=(P(("groups", "tensor"), "pop"), P(("groups", "pop"))),
        check_vma=False,
    )
```

```python
import functools
import math

import jax
import jax.numpy as jnp
from jax import lax
from jax.experimental import pallas as pl
from jax.experimental.pallas import tpu as pltpu
from jax.sharding import PartitionSpec as P

noise_scale = 0.2
norm_eps = 1e-06


def scaled_rows(values):
    return values * lax.rsqrt(jnp.mean(values * values, axis=-1, keepdims=True) + norm_eps)


def build_hidden(
    gate_baseline, up_baseline, lowrank_gate, lowrank_up, gate_output_factors, up_output_factors
):
    gate_activation = gate_baseline.astype(jnp.float32)[None] + jnp.einsum(
        "hvw,hpw->hvp", lowrank_gate, gate_output_factors, preferred_element_type=jnp.float32
    )
    upper_bound = up_baseline.astype(jnp.float32)[None] + jnp.einsum(
        "hvw,hpw->hvp", lowrank_up, up_output_factors, preferred_element_type=jnp.float32
    )
    return (jax.nn.silu(gate_activation) * upper_bound).astype(jnp.bfloat16)


def label_terms(logits, targets):
    labels = logits.shape[1]
    picks = targets[:, None] == jnp.arange(labels, dtype=jnp.int32)[None, :]
    picked = jnp.sum(jnp.where(picks, logits, 0.0), axis=1)
    return picked - jnp.log(jnp.sum(jnp.exp(logits), axis=1))


def body(
    prompts,
    gate_weight,
    up_weight,
    down_weight_matrix,
    gate_in,
    gate_output_factors,
    up_in,
    up_output_factors,
    down_input_factors,
    down_out,
    label_head,
    targets,
):
    member = lax.axis_index("pop")
    width = prompts.shape[1]
    in_block = gate_weight.shape[0]
    ffn_half = gate_output_factors.shape[1]
    total_ff = ffn_half * lax.axis_size("tensor")
    members = down_input_factors.shape[0]
    rank = down_input_factors.shape[2]
    prompt_f = prompts.astype(jnp.float32)
    normed = scaled_rows(prompt_f).astype(jnp.bfloat16)
    own_cols = lax.dynamic_slice_in_dim(normed, member * in_block, in_block, 1)
    part_gate = jnp.dot(own_cols, gate_weight, preferred_element_type=jnp.float32)
    part_up = jnp.dot(own_cols, up_weight, preferred_element_type=jnp.float32)
    total_gate, total_up = lax.psum((part_gate, part_up), "pop")
    gate_baseline = total_gate.astype(jnp.bfloat16)
    up_baseline = total_up.astype(jnp.bfloat16)
    in_scale = noise_scale / math.sqrt(width)
    lowrank_gate = (
        in_scale * jnp.einsum("rd,mdk->mrk", normed, gate_in, preferred_element_type=jnp.float32)
    ).astype(jnp.bfloat16)
    lowrank_up = (
        in_scale * jnp.einsum("rd,mdk->mrk", normed, up_in, preferred_element_type=jnp.float32)
    ).astype(jnp.bfloat16)
    down_scale = noise_scale / math.sqrt(total_ff)
    hidden_state = build_hidden(
        gate_baseline, up_baseline, lowrank_gate, lowrank_up, gate_output_factors, up_output_factors
    )
    hidden_portion = lax.all_gather(hidden_state, "pop", axis=0, tiled=True)
    out_piece = down_out.astype(jnp.float32)
    entry_point = jnp.einsum(
        "uaz,zh->uah", hidden_portion, down_weight_matrix, preferred_element_type=jnp.float32
    )
    low_part = down_scale * jnp.einsum(
        "lpq,lqb->lpb", hidden_portion, down_input_factors, preferred_element_type=jnp.float32
    )
    partial_rows = entry_point + jnp.einsum(
        "mrk,mdk->mrd", low_part, out_piece, precision=lax.Precision.HIGHEST
    )
    rows_here = lax.all_to_all(partial_rows, "pop", split_axis=0, concat_axis=2, tiled=True)
    summed = lax.psum(rows_here, "tensor")[0]
    output = prompt_f + summed
    final = scaled_rows(output).astype(jnp.bfloat16)
    half = label_head.shape[0]
    own_half = lax.dynamic_slice_in_dim(final, lax.axis_index("tensor") * half, half, 1)
    logits = lax.psum(jnp.dot(own_half, label_head, preferred_element_type=jnp.float32), "tensor")
    reward = jnp.mean(label_terms(logits, targets))
    rewards = lax.all_gather(reward.reshape(1), "pop", axis=0, tiled=True)
    centre = jnp.mean(rewards)
    spread = jnp.mean((rewards - centre) * (rewards - centre))
    scores = (rewards - centre) * lax.rsqrt(spread + norm_eps)
    weighted = (scores[:, None, None] * down_out.astype(jnp.float32)).astype(jnp.bfloat16)
    update = jnp.einsum(
        "mfk,mdk->fd", down_input_factors, weighted, preferred_element_type=jnp.float32
    ) * (1.0 / math.sqrt(members * rank))
    own_score = lax.dynamic_slice_in_dim(scores, member, 1, 0)
    return (update.astype(jnp.bfloat16), own_score)


BF = jnp.bfloat16
F32 = jnp.float32
HI = lax.Precision.HIGHEST
NT = (((1,), (1,)), ((), ()))
TN = (((0,), (0,)), ((), ()))


def pair_kernel(
    pop, total_ff,
    prompts_in, gate_w, up_w, down_w, gate_in_h, gof_h, up_in_h, uof_h, dif_h, dout_h, head, targets_in,
    weighted_out,
    prompts, gate_in, gof, up_in, uof, dif, dout, targets,
    wgu, dw, normed, fbuild, fac, low, own, ysend, yrecv, zsend, zrecv, base,
    lhs, hid, acc, lowd, dcat, xsend, xrecv, hblock,
    lgsend, lgrecv, lsend, lrecv, rbuf,
    wsem, dsem, msem, ssem, rsem,
):
    rows, width = prompts.shape
    block, ff = gate_w.shape
    outer = pop // 2
    piece = wgu.shape[3]
    chunk = 2 * piece
    members = pop
    rank = gof.shape[0]
    part = members // 2
    big = members * rows
    labels = head.shape[1]
    over = pop * chunk - ff
    tile = 256
    me = lax.axis_index("pop")
    core = lax.axis_index("tensor")
    z = me // 2
    y = me % 2
    sib = {"tensor": 1 - core}
    middle = (z >= 1) & (z <= outer - 2)

    def spot(zz, yy):
        return zz * 2 + yy

    def start_of(c):
        return pl.multiple_of(c * chunk - (c // (pop - 1)) * over, 128)

    def remote(src, dst, sidx, ridx, dev):
        return pltpu.make_async_remote_copy(
            src_ref=src, dst_ref=dst, send_sem=ssem.at[sidx], recv_sem=rsem.at[ridx],
            device_id=dev, device_id_type=pl.DeviceIdType.MESH,
        )

    barrier = pltpu.get_barrier_semaphore()
    for k in range(1, pop):
        for t in range(2):
            pl.semaphore_signal(
                barrier, inc=1, device_id={"pop": (me + k) % pop, "tensor": t}, device_id_type=pl.DeviceIdType.MESH
            )
    pl.semaphore_signal(barrier, inc=1, device_id=sib, device_id_type=pl.DeviceIdType.MESH)

    def load(src, dst, sem):
        d = pltpu.make_async_copy(src, dst, sem)
        d.start()
        return d

    lgof = load(gof_h, gof, msem.at[0])
    luof = load(uof_h, uof, msem.at[1])
    lprompts = load(prompts_in, prompts, msem.at[2])
    lgin = load(gate_in_h, gate_in, msem.at[3])
    luin = load(up_in_h, up_in, msem.at[4])
    order = [
        jnp.where(z == 0, 1, z - 1),
        jnp.where(z == outer - 1, 1, jnp.where(z == 2, 3, 2)),
        jnp.where(z < 2, 3, 0),
    ]
    line = order[::-1] + [z]
    owners = [spot(line[i % outer], (1 - y) if i < outer else y) for i in range(pop)]

    def weights(h, i):
        cols = pl.ds(pl.multiple_of(start_of(owners[i]) + h * piece, 128), piece)
        n = h * pop + i
        load(gate_w.at[:, cols], wgu.at[n, 0], wsem.at[n])
        load(up_w.at[:, cols], wgu.at[n, 1], wsem.at[n])

    steps = [(0, i) for i in range(outer + 2)] + [(1, 0), (1, 1), (0, 6), (0, 7)]
    steps += [(1, i) for i in range(2, pop)]
    weights(*steps[0])
    for d in (lgof, luof, lprompts, lgin, luin):
        d.wait()
    for at in steps[1:]:
        weights(*at)
    ldif = load(dif_h, dif, msem.at[5])
    ldout = load(dout_h, dout, msem.at[6])
    ltar = load(targets_in, targets, msem.at[7])

    fbuild[0:rank, :] = gof[...].astype(F32)
    fbuild[rank : 2 * rank, :] = uof[...].astype(F32)
    fac[me] = fbuild[...].astype(BF)
    pl.semaphore_wait(barrier, 2 * pop - 1)

    S_FAC, S_CH, S_LOW, S_Y, S_Z, S_A, S_X, S_LG, S_H, S_L, S_R = range(11)
    R_FAC, R_FZ, R_LOW, R_Y, R_Z, R_A, R_B, R_X, R_LG, R_H, R_L, R_R = 0, 1, 9, 10, 18, 20, 28, 32, 33, 34, 35, 36

    def send(src, dst, sidx, ridx, dev):
        d = remote(src, dst, sidx, ridx, dev)
        d.start()
        return d

    def sent(ref, sidx):
        remote(ref, ref, sidx, R_FAC, sib).wait_send()

    def came(ref, ridx):
        remote(ref, ref, S_FAC, ridx, sib).wait_recv()

    cut = ff // 256 * 128

    def chain(o, to, h):
        src = fac.at[spot(o, y), :, pl.ds(h * cut, cut if h == 0 else ff - cut)]
        return remote(src, src, S_CH, R_FZ + 2 * o + h, {"pop": spot(to, y)})

    send(fac.at[me], fac.at[me], S_FAC, R_FAC, {"pop": spot(z, 1 - y)})

    for h in range(2):

        @pl.when(z < outer - 1)
        def _(h=h):
            chain(z, z + 1, h).start()

        @pl.when(z > 0)
        def _(h=h):
            chain(z, z - 1, h).start()

    hrows = head.at[pl.ds(pl.multiple_of((me % part) * block, block), block)]
    holds = core == me // part

    x = prompts[...].astype(F32)
    normed[...] = (x * lax.rsqrt(jnp.mean(x * x, axis=-1, keepdims=True) + norm_eps)).astype(BF)

    scale = noise_scale / math.sqrt(width)
    lg = (scale * lax.dot_general(normed[...], gate_in[...], NT, preferred_element_type=F32)).astype(BF)
    lu = (scale * lax.dot_general(normed[...], up_in[...], NT, preferred_element_type=F32)).astype(BF)
    krow = lax.broadcasted_iota(jnp.int32, (rank, 128), 0)
    lane = lax.broadcasted_iota(jnp.int32, (rank, 128), 1)
    sel_g = (lane == me * 2 * rank + krow).astype(F32).astype(BF)
    sel_u = (lane == me * 2 * rank + rank + krow).astype(F32).astype(BF)
    low[me] = (
        jnp.dot(lg, sel_g, preferred_element_type=F32) + jnp.dot(lu, sel_u, preferred_element_type=F32)
    ).astype(BF)
    for k in range(1, pop):
        send(low.at[me], low.at[me], S_LOW, R_LOW, {"pop": (me + k) % pop})

    xcols = pl.ds(pl.multiple_of(me * block, block), block)
    mine_n = normed[:, xcols]

    def relay_first(h):
        @pl.when(middle)
        def _():
            chain(z - 1, z, h).wait_recv()
            chain(z - 1, z + 1, h).start()
            chain(z + 1, z, h).wait_recv()
            chain(z + 1, z - 1, h).start()

    far = 3 * (2 - z)
    end = 3 * (z - 1)

    def relay_second(h):
        @pl.when(middle)
        def _():
            chain(far, z, h).wait_recv()
            chain(far, end, h).start()

    def forward(n):
        o = order[n]

        @pl.when(jnp.logical_not(middle))
        def _():
            for h in range(2):
                chain(o, z, h).wait_recv()

        src = fac.at[spot(o, y)]
        send(src, src, S_FAC, R_FAC, {"pop": spot(z, 1 - y)})

    ycopies = {}
    step = ff // 4
    across = {"pop": spot(z, 1 - y)}

    def product(h, i):
        n = h * pop + i
        pltpu.make_async_copy(wgu.at[n], wgu.at[n], wsem.at[n]).wait()
        return [jnp.dot(mine_n, wgu[n, g], preferred_element_type=F32) for g in range(2)]

    def part_out(h, i):
        got = product(h, i)
        n = h * outer + i
        for g in range(2):
            ysend[n, g] = got[g].astype(BF)
        ycopies[h, i] = send(ysend.at[n], yrecv.at[n], S_Y, R_Y + n, across)

    def part_own(h, i):
        got = product(h, i)
        for g in range(2):
            own[h * outer + i - outer, g] = got[g]

    def part_on(h, i):
        j = i - outer
        n = h * outer + j
        ycopies[h, j].wait_recv()
        if i == pop - 1:
            for g in range(2):
                own[n, g] = own[n, g] + yrecv[n, g].astype(F32)
            return
        n3 = h * (outer - 1) + j
        for g in range(2):
            zsend[n3, g] = (own[n, g] + yrecv[n, g].astype(F32)).astype(BF)
        send(
            zsend.at[n3], zrecv.at[(outer - 1) * h + (line[j] - z + outer) % outer - 1],
            S_Z, R_Z + h, {"pop": spot(line[j], y)},
        )

    gaps = [(o - z + outer) % outer for o in order]

    def held(slot, h):
        return base.at[2 * slot + h]

    def gather(h):
        last = h * outer + outer - 1
        total = [own[last, 0], own[last, 1]]
        came(zrecv.at[(outer - 1) * h : (outer - 1) * (h + 1)], R_Z + h)
        for j in range(outer - 1):
            for g in range(2):
                total[g] = total[g] + zrecv[h * (outer - 1) + j, g].astype(F32)
        for g in range(2):
            base[h, g] = total[g].astype(BF)
        for n in (2, 1, 0):
            send(
                held(0, h), held(gaps[n], h), S_A, R_A + 2 * gaps[n] + h, {"pop": spot(order[n], y)}
            )

    def near(n):
        return (outer - gaps[n]) % outer

    def arrive(n, h):
        k = near(n)
        came(held(k, h), R_A + 2 * k + h)
        send(held(k, h), held(outer + k, h), S_A, R_B + k, across)

    def hand(h):
        send(held(0, h), held(outer, h), S_A, R_B, across)

    for i in range(outer):
        part_out(0, i)
    part_own(0, 4)
    relay_first(0)
    part_own(0, 5)
    relay_first(1)
    part_out(1, 0)
    part_out(1, 1)
    part_on(0, 4)
    part_own(0, 6)
    part_on(0, 5)
    part_own(0, 7)
    part_on(0, 6)
    relay_second(0)
    part_out(1, 2)
    relay_second(1)
    part_out(1, 3)
    part_on(0, 7)
    for n in range(4):
        at = pl.ds(n * step, step)
        load(down_w.at[at], dw.at[at], dsem.at[0])
    part_own(1, 4)
    part_own(1, 5)
    part_on(1, 4)
    forward(0)
    part_own(1, 6)
    part_on(1, 5)
    part_own(1, 7)
    forward(1)
    part_on(1, 6)
    gather(0)
    forward(2)
    hand(0)
    part_on(1, 7)

    @pl.when(holds)
    def _():
        remote(hrows, hblock, S_H, R_H, sib).start()
        pltpu.make_async_copy(hrows, hblock, msem.at[8]).start()

    ldout.wait()
    ldif.wait()
    ltar.wait()
    dall = jnp.concatenate([dout[m].astype(F32) for m in range(members)], axis=0)
    dcat[...] = jnp.concatenate([dall, dall], axis=0).astype(BF)
    acc[...] = jnp.zeros_like(acc)
    lowd[...] = jnp.zeros_like(lowd)
    came(low.at[1:], R_LOW)
    coef = jnp.concatenate([low[m].astype(F32) for m in range(members)], axis=0)
    lane = lax.broadcasted_iota(jnp.int32, coef.shape, 1)
    row = lax.broadcasted_iota(jnp.int32, coef.shape, 0) % rows
    kk = 2 * rank * members
    gate_lane = lane % (2 * rank) < rank
    gate_lhs = jnp.where(lane < kk, jnp.where(gate_lane, coef, 0.0), (lane == kk + row).astype(F32))
    up_lhs = jnp.where(lane < kk, jnp.where(gate_lane, 0.0, coef), (lane == kk + rows + row).astype(F32))
    lhs[...] = jnp.concatenate([0.5 * gate_lhs, up_lhs], axis=0).astype(BF)

    gather(1)
    hand(1)
    arrive(0, 0)

    pltpu.make_async_copy(down_w, dw, dsem.at[0]).wait()
    came(fac.at[0:outer], R_FAC)

    def expand(slot, c):
        start = start_of(c)
        skip = (c // (pop - 1)) * over

        pad = jnp.zeros((128 - kk - 2 * rows, tile), F32)
        for off in range(0, chunk, tile):
            at = pl.ds(pl.multiple_of(start + off, 128), tile)
            parts = [fac[m, :, at].astype(F32) for m in range(members)]
            low_off = off % piece
            parts += [
                base[2 * slot + off // piece, g, :, low_off : low_off + tile].astype(F32) for g in range(2)
            ]
            keep = (off >= skip).astype(F32)
            rhs = (jnp.concatenate(parts + [pad], axis=0) * keep).astype(BF)
            both = jnp.dot(lhs[...], rhs, preferred_element_type=F32)
            gate, up = both[:big], both[big:]
            hid[:, off : off + tile] = ((gate + gate * jnp.tanh(gate)) * up).astype(BF)
        h = hid[...]
        at = pl.ds(start, chunk)
        right = jnp.concatenate([dif[m, :, at].astype(F32) for m in range(members)], axis=0).astype(BF)
        lowd[...] += lax.dot_general(h, right, NT, preferred_element_type=F32)
        for off in range(0, block, tile):
            acc[:, off : off + tile] += jnp.dot(h, dw[at, off : off + tile], preferred_element_type=F32)

    expand(0, me)
    arrive(1, 0)
    arrive(0, 1)
    expand(near(0), spot(order[0], y))
    arrive(2, 0)
    arrive(1, 1)
    expand(near(1), spot(order[1], y))
    arrive(2, 1)
    expand(near(2), spot(order[2], y))
    came(base.at[2 * outer : 2 * outer + 2], R_B)
    expand(outer, spot(z, 1 - y))
    for n in range(outer - 1):
        k = outer + near(n)
        came(base.at[pl.ds(2 * k, 2)], R_B + near(n))
        expand(k, spot(order[n], 1 - y))

    mine = lax.broadcasted_iota(jnp.int32, lowd.shape, 0) // rows == lax.broadcasted_iota(jnp.int32, lowd.shape, 1) // rank
    lowm = jnp.where(mine, lowd[...] * (noise_scale / math.sqrt(total_ff)), 0.0)
    top = lowm.astype(BF).astype(F32)
    pair = jnp.concatenate([top, lowm - top], axis=1).astype(BF)
    acc[...] += jnp.dot(pair, dcat[...], preferred_element_type=F32)

    span = part * rows
    theirs = pl.ds(pl.multiple_of((1 - core) * span, span), span)
    ours = pl.ds(pl.multiple_of(core * span, span), span)
    xsend[...] = acc[theirs, :].astype(BF)
    xc = send(xsend, xrecv, S_X, R_X, sib)

    @pl.when(holds)
    def _():
        pltpu.make_async_copy(hrows, hblock, msem.at[8]).wait()

    @pl.when(jnp.logical_not(holds))
    def _():
        remote(hrows, hblock, S_H, R_H, sib).wait_recv()

    def logits_of(v):
        top = v.astype(BF)
        rest = (v - top.astype(F32)).astype(BF)
        got = jnp.dot(jnp.concatenate([top, rest], axis=0), hblock[...], preferred_element_type=F32)
        return got[:span] + got[span:]

    lgsend[...] = logits_of(acc[theirs, :])
    lc = send(lgsend, lgrecv, S_LG, R_LG, sib)
    pcols = prompts[:, xcols].astype(F32)
    here = acc[ours, :] + jnp.concatenate([pcols] * part, axis=0)
    lgts = logits_of(here)
    xc.wait_recv()
    out = here + xrecv[...].astype(F32)
    squares = out * out
    sq = squares[:, 0:128]
    for off in range(128, block, 128):
        sq = sq + squares[:, off : off + 128]
    top = sq.astype(BF).astype(F32)
    halves = jnp.concatenate([top, sq - top], axis=1).astype(BF)
    sums = lax.dot_general(jnp.ones((8, 256), BF), halves, NT, preferred_element_type=F32)
    for i in range(part):
        lsend[i, rows : rows + 8, :] = jnp.zeros((8, labels), F32)
        lsend[i, rows : rows + 8, 0:rows] = sums[:, i * rows : (i + 1) * rows]
    lc.wait_recv()
    for i in range(part):
        r = slice(i * rows, (i + 1) * rows)
        lsend[i, 0:rows, :] = lgts[r] + lgrecv[r, :]
    for i in range(part):
        m = core * part + i

        @pl.when(m != me)
        def _(i=i, m=m):
            remote(lsend.at[i], lrecv.at[me], S_L, R_L, {"pop": m}).start()

    @pl.when(holds)
    def _():
        came(lrecv.at[1:], R_L)
        tot = lsend[me % part]
        for k in range(1, pop):
            tot = tot + lrecv[(me + k) % pop]
        eye = (
            lax.broadcasted_iota(jnp.int32, (rows, labels), 0) == lax.broadcasted_iota(jnp.int32, (rows, labels), 1)
        ).astype(F32)
        ssq = jnp.sum(eye * tot[rows : rows + 1, :], axis=1, keepdims=True)
        lgt = tot[0:rows, :] * lax.rsqrt(ssq * (1.0 / width) + norm_eps)
        spread_t = jnp.where(eye[:, :rows] > 0.0, jnp.broadcast_to(targets[...].astype(F32), (rows, rows)), 0.0)
        target = jnp.sum(spread_t, axis=1, keepdims=True).astype(jnp.int32)
        picks = target == lax.broadcasted_iota(jnp.int32, (rows, labels), 1)
        picked = jnp.sum(jnp.where(picks, lgt, 0.0), axis=1, keepdims=True)
        term = picked - jnp.log(jnp.sum(jnp.exp(lgt), axis=1, keepdims=True))
        rbuf[me] = jnp.sum(jnp.broadcast_to(term, (rows, 128)), axis=0, keepdims=True) * (1.0 / rows)
        for to in [spot(o, w) for o in order[::-1] for w in (1 - y, y)] + [spot(z, 1 - y)]:
            for t in range(2):
                send(rbuf.at[me], rbuf.at[me], S_R, R_R, {"pop": to, "tensor": t})
        send(rbuf.at[me], rbuf.at[me], S_R, R_R, sib)
        came(rbuf.at[1:members], R_R)

    @pl.when(jnp.logical_not(holds))
    def _():
        came(rbuf.at[0:members], R_R)

    centre = sum(rbuf[m] for m in range(members)) * (1.0 / members)
    spread = sum((rbuf[m] - centre) * (rbuf[m] - centre) for m in range(members)) * (1.0 / members)
    inv = lax.rsqrt(spread + norm_eps)
    weighted_out[members * rank :, 0:128] = jnp.broadcast_to((rbuf[me] - centre) * inv, (8, 128))
    of = lax.broadcasted_iota(jnp.int32, (members * rank, 128), 0) // rank
    column = jnp.zeros((members * rank, 128), F32)
    for m in range(members):
        column = jnp.where(of == m, jnp.broadcast_to((rbuf[m] - centre) * inv, column.shape), column)
    for off in range(0, block, 128):
        at = slice(off, off + 128)
        weighted_out[0 : members * rank, at] = (dcat[0 : members * rank, at].astype(F32) * column).astype(BF).astype(F32)

    sent(fac.at[0:outer], S_FAC)
    sent(low.at[1:], S_LOW)
    sent(ysend, S_Y)
    sent(zsend, S_Z)
    sent(base.at[0 : 4 * outer - 2], S_A)
    sent(xsend, S_X)
    sent(lgsend, S_LG)

    @pl.when(middle)
    def _():
        sent(fac.at[0 : outer + 1], S_CH)

    @pl.when(jnp.logical_not(middle))
    def _():
        sent(fac.at[0], S_CH)

    @pl.when(holds)
    def _():
        sent(hblock, S_H)
        sent(lsend.at[1:], S_L)
        sent(rbuf.at[1:], S_R)

    @pl.when(jnp.logical_not(holds))
    def _():
        sent(lsend, S_L)


def update_kernel(norm, step, dif, weighted, out, score_out, left, right, sem):
    members, rank, ff = dif.shape
    width = weighted.shape[1]
    right[...] = weighted[0 : members * rank, :].astype(BF)
    cuts = [0, 128] + list(range(step, ff, step)) + [ff]
    blocks = [(at, end - at) for at, end in zip(cuts, cuts[1:])]
    for start, size in blocks:
        at = pl.ds(start, size)
        rows = jnp.concatenate([dif[m, :, at].astype(F32) for m in range(members)], axis=0).T.astype(BF)
        for c in range(0, width, 256):
            got = jnp.dot(rows, right[:, c : c + 256], preferred_element_type=F32)
            left[at, c : c + 256] = (got * norm).astype(BF)
        pltpu.make_async_copy(left.at[at], out.at[at], sem).start()
    score_out[0] = weighted[members * rank, 0]
    pltpu.make_async_copy(left, out, sem).wait()


def fast_body(
    pop, prompts, gate_weight, up_weight, down_weight, gate_in, gof, up_in, uof, dif, dout, head, targets
):
    rows, width = prompts.shape
    block, ff = gate_weight.shape
    members, _, rank = dif.shape
    outer = pop // 2
    chunk = -(-(ff // 128) // pop) * 128
    piece = chunk // 2
    labels = head.shape[1]
    swap = lambda v: jnp.swapaxes(v, 1, 2)
    dif_t, dout_t = swap(dif), swap(dout)
    vm = pl.BlockSpec(memory_space=pltpu.VMEM)
    hb = pl.BlockSpec(memory_space=pl.ANY)
    V = pltpu.VMEM
    D = pltpu.SemaphoreType.DMA
    big = members * rows
    weighted = pl.pallas_call(
        functools.partial(pair_kernel, pop, 2 * ff),
        out_shape=V((members * rank + 8, block), F32),
        in_specs=[hb] * 12,
        out_specs=vm,
        scratch_shapes=[
            V((rows, width), BF), V((rank, width), BF), V((rank, ff), BF), V((rank, width), BF), V((rank, ff), BF),
            V((members, rank, ff), BF), V((members, rank, block), BF), V((1, rows), jnp.int32),
            V((2 * pop, 2, block, piece), BF), V((ff, block), BF),
            V((rows, width), BF), V((2 * rank, ff), F32), V((members, 2 * rank, ff), BF),
            V((members, rows, 128), BF), V((pop, 2, rows, piece), F32),
            V((pop, 2, rows, piece), BF), V((pop, 2, rows, piece), BF),
            V((pop - 2, 2, rows, piece), BF), V((pop - 2, 2, rows, piece), BF),
            V((2 * pop, 2, rows, piece), BF),
            V((2 * big, 128), BF), V((big, chunk), BF), V((big, block), F32), V((big, members * rank), F32),
            V((2 * members * rank, block), BF), V((big // 2, block), BF), V((big // 2, block), BF),
            V((block, labels), BF),
            V((big // 2, labels), F32), V((big // 2, labels), F32),
            V((members // 2, rows + 8, labels), F32), V((members, rows + 8, labels), F32),
            V((2 * members, 1, 128), F32),
            D((2 * pop,)), D((1,)), D((9,)), D((11,)), D((37,)),
        ],
        compiler_params=pltpu.CompilerParams(
            collective_id=0, has_side_effects=True, vmem_limit_bytes=60 * 1000 * 1000
        ),
        name="pair",
    )(
        prompts, gate_weight, up_weight, down_weight, swap(gate_in)[0], swap(gof)[0], swap(up_in)[0],
        swap(uof)[0], dif_t, dout_t, head, targets[None],
    )
    step = 384
    update, scores = pl.pallas_call(
        functools.partial(update_kernel, 1.0 / math.sqrt(members * rank), step),
        out_shape=(jax.ShapeDtypeStruct((ff, block), BF), jax.ShapeDtypeStruct((1,), F32)),
        in_specs=[vm, vm],
        out_specs=(hb, pl.BlockSpec(memory_space=pltpu.SMEM)),
        scratch_shapes=[
            V((ff, block), BF), V((members * rank, block), BF), D(()),
        ],
        compiler_params=pltpu.CompilerParams(vmem_limit_bytes=40 * 1000 * 1000),
        name="update",
    )(dif_t, weighted)
    return update, scores


def solution(mesh):
    placed = (
        P("groups", None),
        P("pop", "tensor"),
        P("pop", "tensor"),
        P("tensor", "pop"),
        P(("groups", "pop"), None, None),
        P(("groups", "pop"), "tensor", None),
        P(("groups", "pop"), None, None),
        P(("groups", "pop"), "tensor", None),
        P("groups", "tensor", None),
        P("groups", "pop", None),
        P("tensor", None),
        P("groups"),
    )
    pop = mesh.shape["pop"]
    run = functools.partial(fast_body, pop) if pop == 8 and mesh.shape["tensor"] == 2 else body
    return jax.shard_map(
        run,
        mesh=mesh,
        in_specs=placed,
        out_specs=(P(("groups", "tensor"), "pop"), P(("groups", "pop"))),
        check_vma=False,
    )
```
